256 devices in a mesh: section: 4 (over x_lo, core), dp: 64 (over z, x_hi, y).
Axes of the slice: x: 4 (x_hi: 2, x_lo: 2; x = x_hi * 2 + x_lo), y: 4, z: 8, core: 2. Of those that a mesh axis runs over, the one named last changes fastest.
Arguments:
- obs_features: bfloat16 [4, 2048, 1024], P(None, 'dp'), may hold values from -1.1953125 to 1.1953125
- w_input: bfloat16 [4, 1024, 4096], P('section'), may hold values from -1 to 1
- w_recurrent: bfloat16 [4, 1024, 4096], P('section', None, 'dp'), may hold values from -0.1875 to 0.1875
- bias: float32 [4, 4096], P('section'), may hold values from -3 to 3
- stored_states: bfloat16 [4, 4, 2048, 2048], P('section', None, 'dp'), may hold values from -3 to 3
- state_owner: int32 [2048], P('dp'), may hold values from 0 to 3
- burn_steps: int32 [2048], P('dp'), may hold values from 1 to 2
- valid_steps: int32 [2048], P('dp'), may hold values from 3 to 4
- cotangent: bfloat16 [4, 2048, 1024], P(None, 'dp'), may hold values from -3 to 3
Outputs:
- hidden_all: bfloat16 [4, 4, 2048, 1024], P('section', None, 'dp')
- grad_recurrent: float32 [4, 1024, 4096], P('section', None, 'dp')
- grad_bias: float32 [4, 4096], P('section', 'dp')
The draws below stay inside these ranges and needn't reach their ends.
All inputs are finite; a program needn't handle non-finite values.
Results may differ from the reference program's by a relative error of at most 0.017.
Values may be sent and summed in bfloat16 or wider, within the bound.
A program may use at most 128 MiB of HBM per device.

```python
import jax
import jax.numpy as jnp
from jax import lax

D = 1024
GATES = 4096
LAYERS = 4
SEQS = 2048
STEPS = 4
BURN = 2
N_SECTION = 4


def set_ends(array, own_key, low, high):
    spot = [jax.random.randint(jax.random.fold_in(own_key, axis), (), 0, length) for axis, length in enumerate(array.shape)]
    main_axis = array.shape.index(max(array.shape))
    next_to = spot[:main_axis] + [(spot[main_axis] + 1) % array.shape[main_axis]] + spot[main_axis + 1:]
    return array.at[tuple(spot)].set(low).at[tuple(next_to)].set(high)


def shard_levels(own_key, dims, pieces, least, high):
    def one(dim, parts):
        heights = jax.random.uniform(jax.random.fold_in(jax.random.fold_in(own_key, 6), dim), (parts,), jnp.float32, least / len(pieces), high / len(pieces))
        return jnp.repeat(jnp.exp(heights), dims[dim] // parts).reshape((-1,) + (1,) * (len(dims) - dim - 1))

    loudness = one(*pieces[0])
    for cut in pieces[1:]:
        loudness = loudness * one(*cut)
    return loudness


def bell_draw(rng, shape, deviation, reach, pieces=(), kind=jnp.bfloat16):
    array = jax.random.normal(rng, shape, jnp.float32) * deviation
    if len(pieces) > 0:
        array = shard_levels(rng, shape, pieces, -0.22, 0.18) * array
    return jnp.clip(array, min=-reach, max=reach).astype(kind)


def setup_inputs(seed: int = 0) -> dict:
    arg_keys = jax.random.split(jax.random.key(seed), 10)
    return {
        "obs_features": bell_draw(arg_keys[0], (STEPS, SEQS, D), 0.2, 1.1953125, ((1, 64),)),
        "w_input": bell_draw(arg_keys[1], (LAYERS, D, GATES), (D // 25) ** -0.5, 1.0, ((0, 4),)),
        "w_recurrent": bell_draw(arg_keys[2], (LAYERS, D, GATES), D ** -0.5, 0.1875, ((0, 4), (2, 64))),
        "bias": bell_draw(arg_keys[3], (LAYERS, GATES), 0.5, 3.0, ((0, 4),), jnp.float32),
        "stored_states": bell_draw(arg_keys[4], (N_SECTION, LAYERS, SEQS, 2 * D), 0.5, 3.0, ((0, 4), (2, 64))),
        "state_owner": set_ends(jax.random.randint(arg_keys[5], (SEQS,), 0, N_SECTION), jax.random.fold_in(arg_keys[5], 1), 0, N_SECTION - 1).astype(jnp.int32),
        "burn_steps": set_ends(jax.random.randint(arg_keys[6], (SEQS,), BURN // 2, BURN + 1), jax.random.fold_in(arg_keys[6], 1), BURN // 2, BURN).astype(jnp.int32),
        "valid_steps": set_ends(jax.random.randint(arg_keys[7], (SEQS,), STEPS - (STEPS - BURN) // 2, STEPS + 1), jax.random.fold_in(arg_keys[7], 1), STEPS - (STEPS - BURN) // 2, STEPS).astype(jnp.int32),
        "cotangent": bell_draw(arg_keys[8], (STEPS, SEQS, D), 0.5, 3.0, ((1, 64),)),
    }


def lstm_cell(preact, cell_prev):
    breadth = cell_prev.shape[-1]
    in_gate = jax.nn.sigmoid(preact[:, :breadth])
    forget = jax.nn.sigmoid(preact[:, breadth:2 * breadth])
    candidate = jnp.tanh(preact[:, 2 * breadth:3 * breadth])
    out_gate = jax.nn.sigmoid(preact[:, 3 * breadth:])
    cell_new = forget * cell_prev + in_gate * candidate
    hidden_new = (out_gate * jnp.tanh(cell_new)).astype(jnp.bfloat16)
    gate_vals = jnp.concatenate([in_gate, forget, candidate, out_gate], axis=-1)
    return hidden_new, cell_new, gate_vals


def forward_span(inputs, w_in, w_rec, bias_row, hidden_start, cell_start):
    step_count, seq_rows, breadth = inputs.shape
    projected = jnp.dot(inputs.reshape(step_count * seq_rows, breadth), w_in, preferred_element_type=jnp.float32)
    projected = projected.reshape(step_count, seq_rows, -1) + bias_row

    def advance(carried, proj_row):
        hidden_prev, cell_prev = carried
        preact = proj_row + jnp.dot(hidden_prev, w_rec, preferred_element_type=jnp.float32)
        hidden_new, cell_new, gate_vals = lstm_cell(preact, cell_prev)
        return (hidden_new, cell_new), (hidden_new, cell_new, gate_vals)

    (hidden_end, cell_end), (hidden_seq, cell_seq, gate_seq) = lax.scan(advance, (hidden_start, cell_start), projected)
    return hidden_seq, cell_seq, gate_seq, hidden_end, cell_end


def times_transposed(operand, matrix):
    return lax.dot_general(operand, matrix, (((1,), (1,)), ((), ())), preferred_element_type=jnp.float32)


def backward_span(above_grads, cell_now, cell_old, gate_seq, live_mask, w_rec, grad_h, grad_c):
    def retreat(carried, inputs):
        grad_hidden, grad_cell = carried
        grad_out, cell_cur, cell_before, gate_vals, alive_row = inputs
        breadth = cell_cur.shape[-1]
        in_gate = gate_vals[:, :breadth]
        forget = gate_vals[:, breadth:2 * breadth]
        candidate = gate_vals[:, 2 * breadth:3 * breadth]
        out_gate = gate_vals[:, 3 * breadth:]
        total_h = grad_out.astype(jnp.float32) + grad_hidden
        squashed = jnp.tanh(cell_cur)
        total_c = grad_cell + total_h * out_gate * (1.0 - squashed * squashed)
        grad_pre = jnp.concatenate([
            total_c * candidate * in_gate * (1.0 - in_gate),
            total_c * cell_before * forget * (1.0 - forget),
            total_c * in_gate * (1.0 - candidate * candidate),
            total_h * squashed * out_gate * (1.0 - out_gate)], axis=-1) * alive_row[:, None]
        gate_grads = grad_pre.astype(jnp.bfloat16)
        return (times_transposed(gate_grads, w_rec), total_c * forget * alive_row[:, None]), gate_grads

    (grad_h_end, grad_c_end), gate_grads = lax.scan(
        retreat, (grad_h, grad_c), (above_grads, cell_now, cell_old, gate_seq, live_mask), reverse=True)
    return gate_grads, grad_h_end, grad_c_end


def reference(obs_features, w_input, w_recurrent, bias, stored_states, state_owner, burn_steps, valid_steps, cotangent):
    breadth = w_input.shape[1]
    seq_rows = obs_features.shape[1]
    owners = jnp.arange(N_SECTION, dtype=jnp.int32)
    picked = (state_owner[None, :] == owners[:, None])[:, :, None]
    positions = jnp.arange(STEPS, dtype=jnp.int32)[:, None]
    live_mask = ((positions >= burn_steps[None, :]) & (positions < valid_steps[None, :])).astype(jnp.float32)
    layer_input = obs_features
    stored_acts = []
    hidden_list = []
    for layer_index in range(LAYERS):
        delivered = jnp.sum(jnp.where(picked, stored_states[:, layer_index].astype(jnp.float32), jnp.float32(0.0)), axis=0)
        hidden_start = delivered[:, :breadth].astype(jnp.bfloat16)
        cell_start = delivered[:, breadth:]
        hidden_seq, cell_seq, gate_seq, hidden_end, cell_end = forward_span(
            layer_input, w_input[layer_index], w_recurrent[layer_index], bias[layer_index], hidden_start, cell_start)
        hidden_full = jnp.concatenate([hidden_start[None], hidden_seq], axis=0)
        cell_full = jnp.concatenate([cell_start[None], cell_seq], axis=0)
        stored_acts.append((hidden_full, cell_full, gate_seq))
        hidden_list.append(hidden_seq)
        layer_input = hidden_seq
    above_grads = cotangent
    weight_list = []
    bias_list = []
    zero_state = jnp.zeros((seq_rows, breadth), jnp.float32)
    for layer_index in range(LAYERS - 1, -1, -1):
        hidden_full, cell_full, gate_seq = stored_acts[layer_index]
        gate_grads, grad_h_end, grad_c_end = backward_span(
            above_grads, cell_full[1:], cell_full[:-1], gate_seq, live_mask, w_recurrent[layer_index], zero_state, zero_state)
        gate_rows = gate_grads.reshape(STEPS * seq_rows, -1)
        prev_rows = hidden_full[:-1].reshape(STEPS * seq_rows, breadth)
        weight_list.append(jnp.dot(prev_rows.T, gate_rows, preferred_element_type=jnp.float32))
        bias_list.append(jnp.sum(gate_rows.astype(jnp.float32), axis=0))
        above_grads = times_transposed(gate_rows, w_input[layer_index]).reshape(STEPS, seq_rows, breadth).astype(jnp.bfloat16)
    weight_list = weight_list[::-1]
    bias_list = bias_list[::-1]
    return jnp.stack(hidden_list), jnp.stack(weight_list), jnp.stack(bias_list)
```

```python
import jax
import jax.numpy as jnp
from jax import lax
from jax.experimental import pallas as pl
from jax.experimental.pallas import tpu as pltpu
from jax.sharding import Mesh
from jax.sharding import PartitionSpec as P

S, Z, X, Y = 4, 8, 2, 4
STEPS = 4
ROWS = 32
D = 1024
LANES = 128
GATES = 4
ALL_ROWS = Y * ROWS
LOCAL = GATES * 2 * LANES
MESH = pl.DeviceIdType.MESH
BF16 = jnp.bfloat16
F32 = jnp.float32


def sigmoid(v):
    return 0.5 * jnp.tanh(0.5 * v) + 0.5


def nt_dot(a, b):
    return lax.dot_general(a, b, (((1,), (1,)), ((), ())), preferred_element_type=F32)


def nn_dot(a, b):
    return jnp.dot(a, b, preferred_element_type=F32)


def remote(src, dst, send_sem, recv_sem, where):
    return pltpu.make_async_remote_copy(
        src_ref=src,
        dst_ref=dst,
        send_sem=send_sem,
        recv_sem=recv_sem,
        device_id=where,
        device_id_type=MESH,
    )


def kernel(
    obs_ref, cot_ref, win_hbm, wrt_hbm, bias_ref, st_hbm, info_ref,
    hid_out, dw_out, db_out,
    info, st, win, wrt, xb, hb, eb, cot_st, c_st, c_in, cells, gates, acc, live,
    grads, grads_t, carry, a_send, a_recv, g_send, g_recv, e_send, hmat, dbs, db_in,
    dw_send, dw_recv, hid_st,
    info_ss, info_rs, st_ss, st_rs, st_ls, wa_ss, wa_rs, wa_ls, ring_ss, ring_rs, win_ls,
    obs_ss, obs_rs, cot_ss, cot_rs, c_ss, c_rs, h_ss, h_rs, x_ss, x_rs,
    a_ss, a_rs, g_ss, g_rs, e_ss, e_rs, dw_ss, dw_rs, db_ss, db_rs, hid_ls,
):
    s = lax.axis_index("s")
    z = lax.axis_index("z")
    x = lax.axis_index("x")
    y = lax.axis_index("y")
    up_y = [lax.rem(y + k, Y) for k in range(1, Y)]
    down_y = [lax.rem(y + Y - k, Y) for k in range(1, Y)]
    up_s = [lax.rem(s + k, S) for k in range(1, S)]
    down_s = [lax.rem(s + S - k, S) for k in range(1, S)]
    z_up, z_down = lax.rem(z + 1, Z), lax.rem(z + Z - 1, Z)
    own_half = lax.rem(y, 2)
    user_y = 2 * x + y // 2
    owner_x = y // 2
    owner_y = [2 * own_half + p for p in range(2)]

    def is_me(zz, xx, yy):
        return (zz == z) & (xx == x) & (yy == y)

    barrier = pltpu.get_barrier_semaphore()

    def greet(where):
        pl.semaphore_signal(barrier, inc=1, device_id=where, device_id_type=MESH)

    for k in range(Y - 1):
        greet({"y": down_y[k]})
    for k in range(S - 1):
        greet({"s": down_s[k]})
    greet({"z": z_up})
    greet({"z": z_down})
    for p in range(2):
        @pl.when(jnp.logical_not(is_me(z, owner_x, owner_y[p])))
        def _():
            greet({"x": owner_x, "y": owner_y[p]})

    @pl.loop(0, Z)
    def _(zz):
        for xx in range(X):
            @pl.when(jnp.logical_not(is_me(zz, xx, user_y)))
            def _():
                greet({"z": zz, "x": xx, "y": user_y})

    mine = is_me(z, owner_x, owner_y[0]) | is_me(z, owner_x, owner_y[1])
    base = (Y - 1) + (S - 1) + 2 + X + Z * 2
    pl.semaphore_wait(barrier, jnp.where(mine, base - 2, base))

    def first_hop(xx):
        return remote(
            wrt_hbm, wrt.at[z, own_half], wa_ss.at[xx], wa_rs.at[own_half],
            {"x": xx, "y": user_y},
        )

    own_copy = pltpu.make_async_copy(wrt_hbm, wrt.at[z, own_half], wa_ls)
    for xx in range(X):
        @pl.when(is_me(z, xx, user_y))
        def _():
            own_copy.start()

        @pl.when(jnp.logical_not(is_me(z, xx, user_y)))
        def _():
            first_hop(xx).start()

    def st_copy(k):
        return remote(st_hbm.at[up_s[k]], st.at[s], st_ss.at[k], st_rs.at[k], {"s": up_s[k]})

    def st_arrival(k):
        return remote(
            st.at[down_s[k]], st.at[down_s[k]], st_ss.at[k], st_rs.at[k], {"s": up_s[k]}
        )

    for k in range(S - 1):
        st_copy(k).start()
    st_own = pltpu.make_async_copy(st_hbm.at[s], st.at[s], st_ls)
    st_own.start()

    def win_copy(gate, half):
        first = pl.multiple_of(gate * D + half * Y * LANES + y * LANES, LANES)
        block = gate * 2 + half
        return pltpu.make_async_copy(
            win_hbm.at[:, pl.ds(first, LANES)],
            win.at[:, pl.ds(block * LANES, LANES)],
            win_ls.at[block],
        )

    for gate in range(GATES):
        for half in range(2):
            win_copy(gate, half).start()

    info[y] = info_ref[...]

    def info_copy(k):
        return remote(info.at[y], info.at[y], info_ss.at[k], info_rs.at[k], {"y": up_y[k]})

    def info_arrival(k):
        return remote(
            info.at[down_y[k]], info.at[down_y[k]], info_ss.at[k], info_rs.at[k], {"y": up_y[k]}
        )

    for k in range(Y - 1):
        info_copy(k).start()

    def obs_copy(k):
        return remote(
            xb.at[:, :, :, y], xb.at[:, :, :, y], obs_ss.at[k], obs_rs.at[k], {"y": up_y[k]}
        )

    def obs_arrival(k):
        part = xb.at[:, :, :, down_y[k]]
        return remote(part, part, obs_ss.at[k], obs_rs.at[k], {"y": up_y[k]})

    @pl.when(s == 0)
    def _():
        for t in range(STEPS):
            for half in range(2):
                for yy in range(Y):
                    first = (half * Y + yy) * LANES
                    xb[t, half, yy, y] = obs_ref[t, :, first : first + LANES]
        for k in range(Y - 1):
            obs_copy(k).start()

    def cot_copy(k):
        return remote(
            cot_st.at[up_y[k]], eb.at[:, :, y], cot_ss.at[k], cot_rs.at[k], {"y": up_y[k]}
        )

    def cot_arrival(k):
        part = eb.at[:, :, down_y[k]]
        return remote(part, part, cot_ss.at[k], cot_rs.at[k], {"y": up_y[k]})

    @pl.when(s == S - 1)
    def _():
        for t in range(STEPS):
            for half in range(2):
                for yy in range(Y):
                    first = (half * Y + yy) * LANES
                    cot_st[yy, t, half] = cot_ref[t, :, first : first + LANES]
        for t in range(STEPS):
            for half in range(2):
                eb[t, half, y] = cot_st[y, t, half]
        for k in range(Y - 1):
            cot_copy(k).start()

    def ring_up(step):
        part = wrt.at[lax.rem(z + Z - step, Z)]
        if step == Z // 2 - 1:
            part = part.at[0]
        return remote(part, part, ring_ss.at[0, step], ring_rs.at[0, step], {"z": z_up})

    def ring_down(step):
        part = wrt.at[lax.rem(z + step, Z)]
        if step == Z // 2 - 1:
            part = part.at[1]
        return remote(part, part, ring_ss.at[1, step], ring_rs.at[1, step], {"z": z_down})

    def ring_wait(step):
        from_down = wrt.at[lax.rem(z + Z - 1 - step, Z)]
        from_up = wrt.at[lax.rem(z + 1 + step, Z)]
        if step == Z // 2 - 1:
            from_down = from_down.at[0]
            from_up = from_up.at[1]
        remote(
            from_down, from_down, ring_ss.at[0, step], ring_rs.at[0, step], {"z": z_up}
        ).wait_recv()
        remote(
            from_up, from_up, ring_ss.at[1, step], ring_rs.at[1, step], {"z": z_down}
        ).wait_recv()

    for p in range(2):
        @pl.when(is_me(z, owner_x, owner_y[p]))
        def _():
            own_copy.wait()

        @pl.when(jnp.logical_not(is_me(z, owner_x, owner_y[p])))
        def _():
            part = wrt.at[z, p]
            remote(
                part, part, wa_ss.at[0], wa_rs.at[p], {"x": owner_x, "y": owner_y[p]}
            ).wait_recv()

    ring_up(0).start()
    ring_down(0).start()

    st_own.wait()
    for k in range(S - 1):
        st_arrival(k).wait_recv()
    marks = info[y]
    chosen = jnp.zeros((ROWS, 2 * D), F32)
    for owner in range(S):
        here = marks[:, STEPS + owner : STEPS + owner + 1] > 0.5
        chosen = chosen + jnp.where(here, st[owner].astype(F32), 0.0)
    for half in range(2):
        for yy in range(Y):
            first = (half * Y + yy) * LANES
            hb[0, half, yy, y] = chosen[:, first : first + LANES].astype(BF16)
            c_st[yy, half] = chosen[:, D + first : D + first + LANES].astype(BF16)
    c_in[y] = c_st[y]

    def h0_copy(k):
        part = hb.at[0, :, :, y]
        return remote(part, part, h_ss.at[0, k], h_rs.at[0, k], {"y": up_y[k]})

    def h0_arrival(k):
        part = hb.at[0, :, :, down_y[k]]
        return remote(part, part, h_ss.at[0, k], h_rs.at[0, k], {"y": up_y[k]})

    def c0_copy(k):
        return remote(c_st.at[up_y[k]], c_in.at[y], c_ss.at[k], c_rs.at[k], {"y": up_y[k]})

    def c0_arrival(k):
        part = c_in.at[down_y[k]]
        return remote(part, part, c_ss.at[k], c_rs.at[k], {"y": up_y[k]})

    for k in range(Y - 1):
        h0_copy(k).start()
        c0_copy(k).start()

    ring_wait(0)
    ring_up(1).start()
    ring_down(1).start()

    for k in range(Y - 1):
        info_arrival(k).wait_recv()
        c0_arrival(k).wait_recv()
    marks_all = info[...].reshape(ALL_ROWS, LANES)
    for t in range(STEPS):
        live[t] = jnp.broadcast_to(marks_all[:, t : t + 1], (ALL_ROWS, LANES))
    for half in range(2):
        cells[0, half] = c_in[:, half].reshape(ALL_ROWS, LANES).astype(F32)
    for gate in range(GATES):
        for half in range(2):
            win_copy(gate, half).wait()

    ring_wait(1)
    ring_up(2).start()
    ring_down(2).start()

    @pl.when(s == 0)
    def _():
        for k in range(Y - 1):
            obs_arrival(k).wait_recv()

    @pl.when(s == S - 1)
    def _():
        for k in range(Y - 1):
            cot_arrival(k).wait_recv()

    for k in range(Y - 1):
        h0_arrival(k).wait_recv()

    ring_wait(2)
    ring_up(3).start()
    ring_down(3).start()
    ring_wait(3)

    def whole(ref, t):
        return jnp.concatenate(
            [
                ref[t, half, yy].reshape(ALL_ROWS, LANES)
                for half in range(2)
                for yy in range(Y)
            ],
            axis=1,
        )

    def h_copy(t, k):
        part = hb.at[t, :, y]
        return remote(part, part, h_ss.at[t, k], h_rs.at[t, k], {"y": up_y[k]})

    def h_arrival(t, k):
        part = hb.at[t, :, down_y[k]]
        return remote(part, part, h_ss.at[t, k], h_rs.at[t, k], {"y": up_y[k]})

    def x_copy(t):
        return remote(hb.at[t + 1], xb.at[t], x_ss.at[t], x_rs.at[t], {"s": up_s[0]})

    def x_arrival(t):
        return remote(xb.at[t], xb.at[t], x_ss.at[t], x_rs.at[t], {"s": up_s[0]})

    def pass_up(t):
        for k in range(Y - 1):
            h_arrival(t + 1, k).wait_recv()

        @pl.when(s < S - 1)
        def _():
            x_copy(t).start()

    def project(t):
        inputs = whole(xb, t)
        for gate in range(GATES):
            columns = slice(gate * 2 * LANES, (gate + 1) * 2 * LANES)
            part = nn_dot(inputs, win[:, columns])
            for half in range(2):
                first = pl.multiple_of(gate * D + half * Y * LANES + y * LANES, LANES)
                acc[gate, half] = (
                    part[:, half * LANES : (half + 1) * LANES] + bias_ref[:, pl.ds(first, LANES)]
                )

    @pl.loop(0, STEPS)
    def _(t):
        @pl.when(s == 0)
        def _():
            project(t)

        @pl.when(t > 0)
        def _():
            pass_up(t - 1)

        @pl.when(s > 0)
        def _():
            x_arrival(t).wait_recv()
            project(t)

        before = whole(hb, t)
        for gate in range(GATES):
            rows = wrt[2 * gate : 2 * gate + 2].reshape(2 * LANES, D)
            part = nt_dot(before, rows)
            for half in range(2):
                pre = acc[gate, half] + part[:, half * LANES : (half + 1) * LANES]
                gates[t, gate, half] = jnp.tanh(pre) if gate == 2 else sigmoid(pre)
        for half in range(2):
            cell = (
                gates[t, 1, half] * cells[t, half] + gates[t, 0, half] * gates[t, 2, half]
            )
            cells[t + 1, half] = cell
            hidden = (gates[t, 3, half] * jnp.tanh(cell)).astype(BF16)
            hb[t + 1, half, y] = hidden.reshape(Y, ROWS, LANES)
        for k in range(Y - 1):
            h_copy(t + 1, k).start()

    pass_up(STEPS - 1)
    for t in range(STEPS):
        for half in range(2):
            for yy in range(Y):
                first = (half * Y + yy) * LANES
                hid_st[t, :, first : first + LANES] = hb[t + 1, half, yy, y]
    hid_copy = pltpu.make_async_copy(hid_st, hid_out, hid_ls)
    hid_copy.start()
    for t in range(STEPS):
        hmat[t * ALL_ROWS : (t + 1) * ALL_ROWS, :] = whole(hb, t)

    carry[...] = jnp.zeros_like(carry)
    dbs[...] = jnp.zeros_like(dbs)

    def a_copy(t, k):
        return remote(
            a_send.at[t, up_y[k]], a_recv.at[t, y], a_ss.at[t, k], a_rs.at[t, k], {"y": up_y[k]}
        )

    def a_arrival(t, k):
        part = a_recv.at[t, down_y[k]]
        return remote(part, part, a_ss.at[t, k], a_rs.at[t, k], {"y": up_y[k]})

    def g_copy(t, k):
        return remote(
            g_send.at[t, up_y[k]], g_recv.at[t, y], g_ss.at[t, k], g_rs.at[t, k], {"y": up_y[k]}
        )

    def g_arrival(t, k):
        part = g_recv.at[t, down_y[k]]
        return remote(part, part, g_ss.at[t, k], g_rs.at[t, k], {"y": up_y[k]})

    def e_copy(t):
        return remote(e_send.at[t], eb.at[t], e_ss.at[t], e_rs.at[t], {"s": down_s[0]})

    def e_arrival(t):
        return remote(eb.at[t], eb.at[t], e_ss.at[t], e_rs.at[t], {"s": down_s[0]})

    def total(sent, received, t, half):
        value = sent[t, y, half].astype(F32)
        for k in range(Y - 1):
            value = value + received[t, down_y[k], half].astype(F32)
        return value

    @pl.loop(0, STEPS)
    def _(back):
        t = STEPS - 1 - back

        @pl.when(s < S - 1)
        def _():
            e_arrival(t).wait_recv()

        for half in range(2):
            acc[0, half] = eb[t, half].reshape(ALL_ROWS, LANES).astype(F32)

        @pl.when(back > 0)
        def _():
            for k in range(Y - 1):
                a_arrival(t + 1, k).wait_recv()
            for half in range(2):
                acc[0, half] = acc[0, half] + total(a_send, a_recv, t + 1, half)

        for half in range(2):
            in_gate = gates[t, 0, half]
            forget = gates[t, 1, half]
            candidate = gates[t, 2, half]
            out_gate = gates[t, 3, half]
            alive = live[t]
            total_h = acc[0, half]
            squashed = jnp.tanh(cells[t + 1, half])
            total_c = carry[half] + total_h * out_gate * (1.0 - squashed * squashed)
            parts = (
                total_c * candidate * in_gate * (1.0 - in_gate) * alive,
                total_c * cells[t, half] * forget * (1.0 - forget) * alive,
                total_c * in_gate * (1.0 - candidate * candidate) * alive,
                total_h * squashed * out_gate * (1.0 - out_gate) * alive,
            )
            carry[half] = total_c * forget * alive
            for gate in range(GATES):
                grads[2 * gate + half] = parts[gate].astype(BF16)

        gate_grads = jnp.concatenate([grads[block] for block in range(2 * GATES)], axis=1)

        @pl.when(t > 0)
        def _():
            for j in range(4):
                columns = slice(j * 2 * LANES, (j + 1) * 2 * LANES)
                part = nn_dot(
                    gate_grads, wrt[:, :, :, columns].reshape(LOCAL, 2 * LANES)
                ).astype(BF16)
                for n in range(2):
                    block = 2 * j + n
                    a_send[t, block % Y, block // Y] = part[:, n * LANES : (n + 1) * LANES]
            for k in range(Y - 1):
                a_copy(t, k).start()

        @pl.when(s > 0)
        def _():
            for j in range(4):
                part = nt_dot(
                    gate_grads, win[j * 2 * LANES : (j + 1) * 2 * LANES, :]
                ).astype(BF16)
                for n in range(2):
                    block = 2 * j + n
                    g_send[t, block % Y, block // Y] = part[:, n * LANES : (n + 1) * LANES]
            for k in range(Y - 1):
                g_copy(t, k).start()

        for block in range(2 * GATES):
            values = grads[block].astype(F32)
            grads_t[t, block] = values.T.astype(BF16)
            dbs[block : block + 1, :] += jnp.sum(values, axis=0, keepdims=True)

        @pl.when(s > 0)
        def _():
            for k in range(Y - 1):
                g_arrival(t, k).wait_recv()
            for half in range(2):
                e_send[t, half] = total(g_send, g_recv, t, half).astype(BF16).reshape(
                    Y, ROWS, LANES
                )
            e_copy(t).start()

    def db_copy(zz, p):
        return remote(
            dbs, db_in.at[z, x], db_ss.at[zz, p], db_rs.at[z, x],
            {"z": zz, "x": owner_x, "y": owner_y[p]},
        )

    def dw_copy(zz, p):
        return remote(
            dw_send.at[zz, p], dw_recv.at[z, x], dw_ss.at[zz, p], dw_rs.at[z, x],
            {"z": zz, "x": owner_x, "y": owner_y[p]},
        )

    @pl.loop(0, Z)
    def _(turn):
        zz = lax.rem(z + Z // 2 + turn, Z)
        rows = jnp.concatenate([grads_t[t, zz] for t in range(STEPS)], axis=1)
        for j in range(4):
            columns = slice(j * 2 * LANES, (j + 1) * 2 * LANES)
            part = nn_dot(rows, hmat[:, columns]).astype(BF16)
            for p in range(2):
                dw_send[zz, p, :, columns] = part[p * LANES // 2 : (p + 1) * LANES // 2, :]
        for p in range(2):
            @pl.when(is_me(zz, owner_x, owner_y[p]))
            def _():
                dw_recv[z, x] = dw_send[zz, p]
                db_in[z, x] = dbs[...]

            @pl.when(jnp.logical_not(is_me(zz, owner_x, owner_y[p])))
            def _():
                dw_copy(zz, p).start()
                db_copy(zz, p).start()

    @pl.loop(0, Z)
    def _(zz):
        for xx in range(X):
            @pl.when(jnp.logical_not(is_me(zz, xx, user_y)))
            def _():
                where = {"z": zz, "x": xx, "y": user_y}
                dw_part = dw_recv.at[zz, xx]
                db_part = db_in.at[zz, xx]
                remote(dw_part, dw_part, dw_ss.at[0, 0], dw_rs.at[zz, xx], where).wait_recv()
                remote(db_part, db_part, db_ss.at[0, 0], db_rs.at[zz, xx], where).wait_recv()

    for j in range(4):
        columns = slice(j * 2 * LANES, (j + 1) * 2 * LANES)
        weight_sum = jnp.zeros((LANES // 2, 2 * LANES), F32)
        for zz in range(Z):
            for xx in range(X):
                weight_sum = weight_sum + dw_recv[zz, xx, :, columns].astype(F32)
        dw_out[:, columns] = weight_sum
    bias_sum = jnp.zeros((1, LANES), F32)
    for zz in range(Z):
        for xx in range(X):
            bias_sum = bias_sum + db_in[zz, xx, pl.ds(z, 1), :]
    db_out[...] = jnp.where(own_half == 0, bias_sum[:, : LANES // 2], bias_sum[:, LANES // 2 :])

    for xx in range(X):
        @pl.when(jnp.logical_not(is_me(z, xx, user_y)))
        def _():
            first_hop(xx).wait_send()

    for k in range(S - 1):
        st_copy(k).wait_send()
    for step in range(Z // 2):
        ring_up(step).wait_send()
        ring_down(step).wait_send()
    for k in range(Y - 1):
        info_copy(k).wait_send()
        h0_copy(k).wait_send()
        c0_copy(k).wait_send()

    @pl.when(s == 0)
    def _():
        for k in range(Y - 1):
            obs_copy(k).wait_send()

    @pl.when(s == S - 1)
    def _():
        for k in range(Y - 1):
            cot_copy(k).wait_send()

    @pl.loop(0, STEPS)
    def _(t):
        for k in range(Y - 1):
            h_copy(t + 1, k).wait_send()

        @pl.when(s < S - 1)
        def _():
            x_copy(t).wait_send()

        @pl.when(t > 0)
        def _():
            for k in range(Y - 1):
                a_copy(t, k).wait_send()

        @pl.when(s > 0)
        def _():
            for k in range(Y - 1):
                g_copy(t, k).wait_send()
            e_copy(t).wait_send()

    @pl.loop(0, Z)
    def _(zz):
        for p in range(2):
            @pl.when(jnp.logical_not(is_me(zz, owner_x, owner_y[p])))
            def _():
                dw_copy(zz, p).wait_send()
                db_copy(zz, p).wait_send()

    hid_copy.wait()


def on_device(
    obs_features, w_input, w_recurrent, bias, stored_states, state_owner, burn_steps, valid_steps, cotangent
):
    lane = lax.broadcasted_iota(jnp.int32, (ROWS, LANES), 1)
    alive = (lane >= burn_steps[:, None]) & (lane < valid_steps[:, None])
    owned = (lane - STEPS) == state_owner[:, None]
    info = jnp.where(lane < STEPS, alive, owned).astype(F32)
    vmem = pl.BlockSpec(memory_space=pltpu.VMEM)
    hbm = pl.BlockSpec(memory_space=pl.ANY)
    dma = pltpu.SemaphoreType.DMA
    piece = (Y, ROWS, LANES)
    hidden, weights, biases = pl.pallas_call(
        kernel,
        out_shape=(
            jax.ShapeDtypeStruct((STEPS, ROWS, D), BF16),
            jax.ShapeDtypeStruct((LANES // 2, D), F32),
            jax.ShapeDtypeStruct((1, LANES // 2), F32),
        ),
        in_specs=[vmem, vmem, hbm, hbm, vmem, hbm, vmem],
        out_specs=(hbm, vmem, vmem),
        scratch_shapes=[
            pltpu.VMEM((Y, ROWS, LANES), F32),
            pltpu.VMEM((S, ROWS, 2 * D), BF16),
            pltpu.VMEM((D, LOCAL), BF16),
            pltpu.VMEM((Z, 2, LANES // 2, D), BF16),
            pltpu.VMEM((STEPS, 2, Y, *piece), BF16),
            pltpu.VMEM((STEPS + 1, 2, Y, *piece), BF16),
            pltpu.VMEM((STEPS, 2, *piece), BF16),
            pltpu.VMEM((Y, STEPS, 2, ROWS, LANES), BF16),
            pltpu.VMEM((Y, 2, ROWS, LANES), BF16),
            pltpu.VMEM((Y, 2, ROWS, LANES), BF16),
            pltpu.VMEM((STEPS + 1, 2, ALL_ROWS, LANES), F32),
            pltpu.VMEM((STEPS, GATES, 2, ALL_ROWS, LANES), F32),
            pltpu.VMEM((GATES, 2, ALL_ROWS, LANES), F32),
            pltpu.VMEM((STEPS, ALL_ROWS, LANES), F32),
            pltpu.VMEM((2 * GATES, ALL_ROWS, LANES), BF16),
            pltpu.VMEM((STEPS, 2 * GATES, LANES, ALL_ROWS), BF16),
            pltpu.VMEM((2, ALL_ROWS, LANES), F32),
            pltpu.VMEM((STEPS, Y, 2, ALL_ROWS, LANES), BF16),
            pltpu.VMEM((STEPS, Y, 2, ALL_ROWS, LANES), BF16),
            pltpu.VMEM((STEPS, Y, 2, ALL_ROWS, LANES), BF16),
            pltpu.VMEM((STEPS, Y, 2, ALL_ROWS, LANES), BF16),
            pltpu.VMEM((STEPS, 2, *piece), BF16),
            pltpu.VMEM((STEPS * ALL_ROWS, D), BF16),
            pltpu.VMEM((2 * GATES, LANES), F32),
            pltpu.VMEM((Z, X, 2 * GATES, LANES), F32),
            pltpu.VMEM((Z, 2, LANES // 2, D), BF16),
            pltpu.VMEM((Z, X, LANES // 2, D), BF16),
            pltpu.VMEM((STEPS, ROWS, D), BF16),
            dma((Y - 1,)), dma((Y - 1,)),
            dma((S - 1,)), dma((S - 1,)), dma,
            dma((X,)), dma((2,)), dma,
            dma((2, Z // 2)), dma((2, Z // 2)),
            dma((2 * GATES,)),
            dma((Y - 1,)), dma((Y - 1,)),
            dma((Y - 1,)), dma((Y - 1,)),
            dma((Y - 1,)), dma((Y - 1,)),
            dma((STEPS + 1, Y - 1)), dma((STEPS + 1, Y - 1)),
            dma((STEPS,)), dma((STEPS,)),
            dma((STEPS, Y - 1)), dma((STEPS, Y - 1)),
            dma((STEPS, Y - 1)), dma((STEPS, Y - 1)),
            dma((STEPS,)), dma((STEPS,)),
            dma((Z, 2)), dma((Z, X)),
            dma((Z, 2)), dma((Z, X)),
            dma,
        ],
        compiler_params=pltpu.CompilerParams(
            collective_id=0, has_side_effects=True, vmem_limit_bytes=56 * 1024 * 1024
        ),
        name="replay_window",
    )(
        obs_features, cotangent, w_input[0], w_recurrent[0].T, bias, stored_states[0], info
    )
    return hidden[None], weights.T[None], biases


def solution(mesh):
    axes = ("s", "z", "x", "y")
    grid = Mesh(mesh.devices.reshape(S, Z, X, Y), axes)
    dp = ("z", "x", "y")
    return jax.shard_map(
        on_device,
        mesh=grid,
        in_specs=(
            P(None, dp, None),
            P("s", None, None),
            P("s", None, dp),
            P("s", None),
            P("s", None, dp, None),
            P(dp),
            P(dp),
            P(dp),
            P(None, dp, None),
        ),
        out_specs=(P("s", None, dp, None), P("s", None, dp), P("s", dp)),
        check_vma=False,
    )
```

```python
import jax
import jax.numpy as jnp
from jax import lax
from jax.experimental import pallas as pl
from jax.experimental.pallas import tpu as pltpu
from jax.sharding import Mesh
from jax.sharding import PartitionSpec as P

S, Z, X, Y = 4, 8, 2, 4
STEPS = 4
ROWS = 32
D = 1024
LANES = 128
GATES = 4
ALL_ROWS = Y * ROWS
LOCAL = GATES * 2 * LANES
MESH = pl.DeviceIdType.MESH
BF16 = jnp.bfloat16
F32 = jnp.float32


def sigmoid(v):
    return 0.5 * jnp.tanh(0.5 * v) + 0.5


def nt_dot(a, b):
    return lax.dot_general(a, b, (((1,), (1,)), ((), ())), preferred_element_type=F32)


def nn_dot(a, b):
    return jnp.dot(a, b, preferred_element_type=F32)


def remote(src, dst, send_sem, recv_sem, where):
    return pltpu.make_async_remote_copy(
        src_ref=src,
        dst_ref=dst,
        send_sem=send_sem,
        recv_sem=recv_sem,
        device_id=where,
        device_id_type=MESH,
    )


def kernel(
    obs_hbm, cot_hbm, win_hbm, wrt_hbm, bias_ref, st_hbm, owner_ref, burn_ref, valid_ref,
    hid_out, dw_out, db_out,
    obs_st, cot_in, info, st, wts, wrt, wint, act, hb_pair, eb, cot_st, c_st, c_in, cells, gates, acc, live,
    grads, grads_t, grads_pair, carry, a_send, a_recv, g_send, g_recv, e_send, hmat, hmat_pair,
    dw_acc, dw_send, dw_recv, db_send, db_recv, dw2_send, dw2_recv, db2_send, db2_recv, hid_st,
    in_ls, info_ss, info_rs, st_ss, st_rs, st_ls, wa_ss, wa_rs, wa_ls, ring_ss, ring_rs, win_ls,
    obs_ss, obs_rs, cot_ss, cot_rs, c_ss, c_rs, h_ss, h_rs, x_ss, x_rs, hz_ss, hz_rs, gz_ss, gz_rs,
    a_ss, a_rs, g_ss, g_rs, e_ss, e_rs, dw_ss, dw_rs, db_ss, db_rs,
    dw2_ss, dw2_rs, db2_ss, db2_rs, hid_ls,
):
    xb, hb = act.at[0], act.at[1]
    s = lax.axis_index("s")
    z = lax.axis_index("z")
    x = lax.axis_index("x")
    y = lax.axis_index("y")
    up_y = [lax.rem(y + k, Y) for k in range(1, Y)]
    down_y = [lax.rem(y + Y - k, Y) for k in range(1, Y)]
    up_s = [lax.rem(s + k, S) for k in range(1, S)]
    down_s = [lax.rem(s + S - k, S) for k in range(1, S)]
    z_up, z_down = lax.rem(z + 1, Z), lax.rem(z + Z - 1, Z)
    z_half = lax.rem(z, 2)
    z_other = 1 - z_half
    z_pair = z + 1 - 2 * z_half
    quad = z // 2
    QUADS = Z // 2
    far = [lax.rem(quad + k, QUADS) for k in (2, 1, 3)]
    near = [lax.rem(quad + QUADS - k, QUADS) for k in (2, 1, 3)]
    own_half = lax.rem(y, 2)
    user_y = 2 * x + y // 2
    owner_x = y // 2
    owner_y = [2 * own_half + p for p in range(2)]

    def is_me(zz, xx, yy):
        return (zz == z) & (xx == x) & (yy == y)

    barrier = pltpu.get_barrier_semaphore()

    def greet(where):
        pl.semaphore_signal(barrier, inc=1, device_id=where, device_id_type=MESH)

    for k in range(Y - 1):
        greet({"y": down_y[k]})
    for k in range(S - 1):
        greet({"s": down_s[k]})
    greet({"z": z_up})
    greet({"z": z_down})
    for k in range(QUADS - 1):
        greet({"z": 2 * near[k] + z_half})
    for p in range(2):
        @pl.when(jnp.logical_not(is_me(z, owner_x, owner_y[p])))
        def _():
            greet({"x": owner_x, "y": owner_y[p]})

    for xx in range(X):
        @pl.when(jnp.logical_not(is_me(z, xx, user_y)))
        def _():
            greet({"x": xx, "y": user_y})

    mine = is_me(z, owner_x, owner_y[0]) | is_me(z, owner_x, owner_y[1])
    base = (Y - 1) + (S - 1) + 2 + (QUADS - 1) + X + 2
    obs_copy_in = pltpu.make_async_copy(obs_hbm, obs_st, in_ls.at[0])
    cot_copy_in = pltpu.make_async_copy(cot_hbm, cot_in, in_ls.at[1])

    @pl.when(s == 0)
    def _():
        obs_copy_in.start()

    @pl.when(s == S - 1)
    def _():
        cot_copy_in.start()

    pl.semaphore_wait(barrier, jnp.where(mine, base - 2, base))

    def first_hop(xx):
        return remote(
            wrt_hbm, wrt.at[z, own_half], wa_ss.at[xx], wa_rs.at[own_half],
            {"x": xx, "y": user_y},
        )

    own_copy = pltpu.make_async_copy(wrt_hbm, wrt.at[z, own_half], wa_ls)
    for xx in range(X):
        @pl.when(is_me(z, xx, user_y))
        def _():
            own_copy.start()

        @pl.when(jnp.logical_not(is_me(z, xx, user_y)))
        def _():
            first_hop(xx).start()

    def st_copy(k):
        return remote(st_hbm.at[up_s[k]], st.at[s], st_ss.at[k], st_rs.at[k], {"s": up_s[k]})

    def st_arrival(k):
        return remote(
            st.at[down_s[k]], st.at[down_s[k]], st_ss.at[k], st_rs.at[k], {"s": up_s[k]}
        )

    for k in range(S - 1):
        st_copy(k).start()
    st_own = pltpu.make_async_copy(st_hbm.at[s], st.at[s], st_ls)
    st_own.start()

    def win_copy(gate, half):
        first = pl.multiple_of(gate * D + half * Y * LANES + y * LANES, LANES)
        block = gate * 2 + half
        return pltpu.make_async_copy(
            win_hbm.at[:, pl.ds(first, LANES)],
            wts.at[0, block],
            win_ls.at[block],
        )

    for gate in range(GATES):
        for half in range(2):
            win_copy(gate, half).start()

    def column(row_ref):
        row = jnp.broadcast_to(row_ref[...].astype(F32), (ROWS, ROWS))
        down = lax.broadcasted_iota(jnp.int32, (ROWS, ROWS), 0)
        across = lax.broadcasted_iota(jnp.int32, (ROWS, ROWS), 1)
        return jnp.sum(jnp.where(down == across, row, 0.0), axis=1, keepdims=True)

    lane = lax.broadcasted_iota(jnp.int32, (ROWS, LANES), 1)
    info[y] = jnp.where(lane == 0, column(burn_ref), column(valid_ref))

    def info_copy(k):
        return remote(info.at[y], info.at[y], info_ss.at[k], info_rs.at[k], {"y": up_y[k]})

    def info_arrival(k):
        return remote(
            info.at[down_y[k]], info.at[down_y[k]], info_ss.at[k], info_rs.at[k], {"y": up_y[k]}
        )

    for k in range(Y - 1):
        info_copy(k).start()

    def obs_copy(k):
        return remote(
            xb.at[:, :, :, y], xb.at[:, :, :, y], obs_ss.at[k], obs_rs.at[k], {"y": up_y[k]}
        )

    def obs_arrival(k):
        part = xb.at[:, :, :, down_y[k]]
        return remote(part, part, obs_ss.at[k], obs_rs.at[k], {"y": up_y[k]})

    @pl.when(s == 0)
    def _():
        obs_copy_in.wait()
        for t in range(STEPS):
            for half in range(2):
                for yy in range(Y):
                    first = (half * Y + yy) * LANES
                    xb[t, half, yy, y] = obs_st[t, :, first : first + LANES]
        for k in range(Y - 1):
            obs_copy(k).start()

    def cot_copy(k):
        return remote(
            cot_st.at[up_y[k]], eb.at[:, :, y], cot_ss.at[k], cot_rs.at[k], {"y": up_y[k]}
        )

    def cot_arrival(k):
        part = eb.at[:, :, down_y[k]]
        return remote(part, part, cot_ss.at[k], cot_rs.at[k], {"y": up_y[k]})

    @pl.when(s == S - 1)
    def _():
        cot_copy_in.wait()
        for t in range(STEPS):
            for half in range(2):
                for yy in range(Y):
                    first = (half * Y + yy) * LANES
                    cot_st[yy, t, half] = cot_in[t, :, first : first + LANES]
        for t in range(STEPS):
            for half in range(2):
                eb[t, half, y] = cot_st[y, t, half]
        for k in range(Y - 1):
            cot_copy(k).start()

    def ring(way, step, p):
        part = wrt.at[lax.rem(z + Z - step, Z) if way == 0 else lax.rem(z + step, Z), p]
        return remote(
            part, part, ring_ss.at[way, step, p], ring_rs.at[way, step, p],
            {"z": z_up if way == 0 else z_down},
        )

    def ring_arrival(way, step, p):
        part = wrt.at[lax.rem(z + Z - 1 - step, Z) if way == 0 else lax.rem(z + 1 + step, Z), p]
        return remote(
            part, part, ring_ss.at[way, step, p], ring_rs.at[way, step, p],
            {"z": z_up if way == 0 else z_down},
        )

    def ring_has(way, step, p):
        return step < Z // 2 - 1 or p == way

    def ring_turn(step):
        for p in range(2):
            for way in range(2):
                if ring_has(way, step - 1, p):
                    ring_arrival(way, step - 1, p).wait_recv()
                if step < Z // 2 and ring_has(way, step, p):
                    ring(way, step, p).start()

    def turn_block(plane):
        block = wrt[plane].reshape(LANES, D)
        for n in range(2 * Y):
            wts[1, plane, n * LANES : (n + 1) * LANES, :] = block[:, n * LANES : (n + 1) * LANES].T

    for p in range(2):
        @pl.when(is_me(z, owner_x, owner_y[p]))
        def _():
            own_copy.wait()

        @pl.when(jnp.logical_not(is_me(z, owner_x, owner_y[p])))
        def _():
            part = wrt.at[z, p]
            remote(
                part, part, wa_ss.at[0], wa_rs.at[p], {"x": owner_x, "y": owner_y[p]}
            ).wait_recv()

        for way in range(2):
            ring(way, 0, p).start()

    st_own.wait()
    for k in range(S - 1):
        st_arrival(k).wait_recv()
    owners = jnp.broadcast_to(column(owner_ref), (ROWS, LANES))

    def chosen(first):
        value = jnp.zeros((ROWS, LANES), F32)
        for owner in range(S):
            entry = st[owner, :, first : first + LANES].astype(F32)
            value = value + jnp.where(owners == float(owner), entry, 0.0)
        return value.astype(BF16)

    for half in range(2):
        for yy in range(Y):
            first = (half * Y + yy) * LANES
            hb[0, half, yy, y] = chosen(first)
            c_st[yy, half] = chosen(D + first)
    c_in[y] = c_st[y]

    def h0_copy(k):
        part = hb.at[0, :, :, y]
        return remote(part, part, h_ss.at[0, k], h_rs.at[0, k], {"y": up_y[k]})

    def h0_arrival(k):
        part = hb.at[0, :, :, down_y[k]]
        return remote(part, part, h_ss.at[0, k], h_rs.at[0, k], {"y": up_y[k]})

    def c0_copy(k):
        return remote(c_st.at[up_y[k]], c_in.at[y], c_ss.at[k], c_rs.at[k], {"y": up_y[k]})

    def c0_arrival(k):
        part = c_in.at[down_y[k]]
        return remote(part, part, c_ss.at[k], c_rs.at[k], {"y": up_y[k]})

    for k in range(Y - 1):
        h0_copy(k).start()
        c0_copy(k).start()

    turn_block(z)
    ring_turn(1)
    turn_block(z_up)
    turn_block(z_down)
    for k in range(Y - 1):
        info_arrival(k).wait_recv()
        c0_arrival(k).wait_recv()
    marks_all = info[...].reshape(ALL_ROWS, LANES)
    for t in range(STEPS):
        alive_now = (marks_all[:, 0:1] <= float(t)) & (marks_all[:, 1:2] > float(t))
        live[t] = jnp.broadcast_to(jnp.where(alive_now, 1.0, 0.0), (ALL_ROWS, LANES))
    for half in range(2):
        cells[0, half] = c_in[:, half].reshape(ALL_ROWS, LANES).astype(F32)

    ring_turn(2)
    turn_block(lax.rem(z + 2, Z))
    turn_block(lax.rem(z + Z - 2, Z))
    for gate in range(GATES):
        for half in range(2):
            win_copy(gate, half).wait()

    ring_turn(3)
    turn_block(lax.rem(z + 3, Z))
    turn_block(lax.rem(z + Z - 3, Z))

    @pl.when(s == 0)
    def _():
        for k in range(Y - 1):
            obs_arrival(k).wait_recv()

    @pl.when(s > 0)
    def _():
        @pl.loop(0, 2 * GATES)
        def _(block):
            for n in range(2 * Y):
                piece = wts[0, block, n * LANES : (n + 1) * LANES, :]
                wint[block, :, n * LANES : (n + 1) * LANES] = piece.T

    @pl.when(s == S - 1)
    def _():
        for k in range(Y - 1):
            cot_arrival(k).wait_recv()

    for k in range(Y - 1):
        h0_arrival(k).wait_recv()

    def hz_copy(t):
        return remote(hb.at[t], hb_pair.at[t], hz_ss.at[t], hz_rs.at[t], {"z": z_pair})

    def hz_arrival(t):
        return remote(hb_pair.at[t], hb_pair.at[t], hz_ss.at[t], hz_rs.at[t], {"z": z_pair})

    ring_turn(4)
    turn_block(lax.rem(z + Z // 2, Z))
    hz_copy(0).start()

    def whole(ref, *at):
        return jnp.concatenate(
            [
                ref[(*at, half, yy)].reshape(ALL_ROWS, LANES)
                for half in range(2)
                for yy in range(Y)
            ],
            axis=1,
        )

    def h_copy(t, k):
        part = hb.at[t, :, y]
        return remote(part, part, h_ss.at[t, k], h_rs.at[t, k], {"y": up_y[k]})

    def h_arrival(t, k):
        part = hb.at[t, :, down_y[k]]
        return remote(part, part, h_ss.at[t, k], h_rs.at[t, k], {"y": up_y[k]})

    def x_copy(t):
        return remote(hb.at[t + 1], xb.at[t], x_ss.at[t], x_rs.at[t], {"s": up_s[0]})

    def x_arrival(t):
        return remote(xb.at[t], xb.at[t], x_ss.at[t], x_rs.at[t], {"s": up_s[0]})

    def pass_up(t):
        for k in range(Y - 1):
            h_arrival(t + 1, k).wait_recv()

        @pl.when(s < S - 1)
        def _():
            x_copy(t).start()

        @pl.when(t < STEPS - 1)
        def _():
            hz_copy(t + 1).start()

    def product(kind, inputs, gate):
        weights = jnp.concatenate([wts[kind, 2 * gate], wts[kind, 2 * gate + 1]], axis=1)
        return nn_dot(inputs, weights)

    def first_product(kind, t):
        inputs = whole(act, kind, t)
        for gate in range(GATES):
            part = product(kind, inputs, gate)
            for half in range(2):
                first = pl.multiple_of(gate * D + half * Y * LANES + y * LANES, LANES)
                acc[gate, half] = (
                    part[:, half * LANES : (half + 1) * LANES] + bias_ref[:, pl.ds(first, LANES)]
                )

    last_kind = jnp.where(s == 0, 1, 0)

    @pl.loop(0, STEPS)
    def _(t):
        @pl.when(s == 0)
        def _():
            first_product(0, t)

        @pl.when(t > 0)
        def _():
            pass_up(t - 1)

        @pl.when(s > 0)
        def _():
            first_product(1, t)
            x_arrival(t).wait_recv()

        inputs = whole(act, last_kind, t)
        for gate in range(GATES):
            part = product(last_kind, inputs, gate)
            for half in range(2):
                pre = acc[gate, half] + part[:, half * LANES : (half + 1) * LANES]
                gates[t, gate, half] = jnp.tanh(pre) if gate == 2 else sigmoid(pre)
        for half in range(2):
            cell = (
                gates[t, 1, half] * cells[t, half] + gates[t, 0, half] * gates[t, 2, half]
            )
            cells[t + 1, half] = cell
            hidden = (gates[t, 3, half] * jnp.tanh(cell)).astype(BF16)
            hb[t + 1, half, y] = hidden.reshape(Y, ROWS, LANES)
        for k in range(Y - 1):
            h_copy(t + 1, k).start()

    pass_up(STEPS - 1)
    hid_copy = pltpu.make_async_copy(hid_st, hid_out, hid_ls)

    def keep_hidden():
        for t in range(STEPS):
            for half in range(2):
                for yy in range(Y):
                    first = (half * Y + yy) * LANES
                    hid_st[t, :, first : first + LANES] = hb[t + 1, half, yy, y]
        hid_copy.start()
        for t in range(STEPS):
            hz_arrival(t).wait_recv()
            hmat[t * ALL_ROWS : (t + 1) * ALL_ROWS, :] = whole(hb, t)
            hmat_pair[t * ALL_ROWS : (t + 1) * ALL_ROWS, :] = whole(hb_pair, t)

    carry[...] = jnp.zeros_like(carry)

    def gz_copy(t):
        return remote(
            grads_t.at[t, z_other], grads_pair.at[t], gz_ss.at[t], gz_rs.at[t], {"z": z_pair}
        )

    def gz_arrival(t):
        part = grads_pair.at[t]
        return remote(part, part, gz_ss.at[t], gz_rs.at[t], {"z": z_pair})

    def a_copy(t, k):
        return remote(
            a_send.at[t, up_y[k]], a_recv.at[t, y], a_ss.at[t, k], a_rs.at[t, k], {"y": up_y[k]}
        )

    def a_arrival(t, k):
        part = a_recv.at[t, down_y[k]]
        return remote(part, part, a_ss.at[t, k], a_rs.at[t, k], {"y": up_y[k]})

    def g_copy(t, k):
        return remote(
            g_send.at[t, up_y[k]], g_recv.at[t, y], g_ss.at[t, k], g_rs.at[t, k], {"y": up_y[k]}
        )

    def g_arrival(t, k):
        part = g_recv.at[t, down_y[k]]
        return remote(part, part, g_ss.at[t, k], g_rs.at[t, k], {"y": up_y[k]})

    def e_copy(t):
        return remote(e_send.at[t], eb.at[t], e_ss.at[t], e_rs.at[t], {"s": down_s[0]})

    def e_arrival(t):
        return remote(eb.at[t], eb.at[t], e_ss.at[t], e_rs.at[t], {"s": down_s[0]})

    def total(sent, received, t, half):
        value = sent[t, y, half].astype(F32)
        for k in range(Y - 1):
            value = value + received[t, down_y[k], half].astype(F32)
        return value

    @pl.loop(0, STEPS)
    def _(back):
        t = STEPS - 1 - back

        @pl.when(s < S - 1)
        def _():
            e_arrival(t).wait_recv()

        for half in range(2):
            acc[0, half] = eb[t, half].reshape(ALL_ROWS, LANES).astype(F32)

        @pl.when(back > 0)
        def _():
            for k in range(Y - 1):
                a_arrival(t + 1, k).wait_recv()
            for half in range(2):
                acc[0, half] = acc[0, half] + total(a_send, a_recv, t + 1, half)

        for half in range(2):
            in_gate = gates[t, 0, half]
            forget = gates[t, 1, half]
            candidate = gates[t, 2, half]
            out_gate = gates[t, 3, half]
            alive = live[t]
            total_h = acc[0, half]
            squashed = jnp.tanh(cells[t + 1, half])
            total_c = carry[half] + total_h * out_gate * (1.0 - squashed * squashed)
            parts = (
                total_c * candidate * in_gate * (1.0 - in_gate) * alive,
                total_c * cells[t, half] * forget * (1.0 - forget) * alive,
                total_c * in_gate * (1.0 - candidate * candidate) * alive,
                total_h * squashed * out_gate * (1.0 - out_gate) * alive,
            )
            carry[half] = total_c * forget * alive
            for gate in range(GATES):
                grads[2 * gate + half] = parts[gate].astype(BF16)

        gate_grads = jnp.concatenate([grads[block] for block in range(2 * GATES)], axis=1)

        @pl.when(t > 0)
        def _():
            for j in range(4):
                columns = slice(j * 2 * LANES, (j + 1) * 2 * LANES)
                part = nn_dot(
                    gate_grads, wrt[:, :, :, columns].reshape(LOCAL, 2 * LANES)
                ).astype(BF16)
                for n in range(2):
                    block = 2 * j + n
                    a_send[t, block % Y, block // Y] = part[:, n * LANES : (n + 1) * LANES]
            for k in range(Y - 1):
                a_copy(t, k).start()

        @pl.when(s > 0)
        def _():
            for j in range(4):
                columns = slice(j * 2 * LANES, (j + 1) * 2 * LANES)
                part = nn_dot(
                    gate_grads, wint[:, :, columns].reshape(LOCAL, 2 * LANES)
                ).astype(BF16)
                for n in range(2):
                    block = 2 * j + n
                    g_send[t, block % Y, block // Y] = part[:, n * LANES : (n + 1) * LANES]
            for k in range(Y - 1):
                g_copy(t, k).start()

        for gate in range(GATES):
            for half in range(2):
                grads_t[t, half, gate] = grads[2 * gate + half].T
        gz_copy(t).start()

        @pl.when(back == 0)
        def _():
            keep_hidden()

        @pl.when(s > 0)
        def _():
            for k in range(Y - 1):
                g_arrival(t, k).wait_recv()
            for half in range(2):
                e_send[t, half] = total(g_send, g_recv, t, half).astype(BF16).reshape(
                    Y, ROWS, LANES
                )
            e_copy(t).start()

    def dw_copy(k):
        return remote(
            dw_send.at[far[k]], dw_recv.at[quad], dw_ss.at[k], dw_rs.at[k],
            {"z": 2 * far[k] + z_half},
        )

    def dw_arrival(k):
        part = dw_recv.at[near[k]]
        return remote(part, part, dw_ss.at[k], dw_rs.at[k], {"z": 2 * far[k] + z_half})

    def db_copy(k):
        return remote(
            db_send.at[far[k]], db_recv.at[quad], db_ss.at[k], db_rs.at[k],
            {"z": 2 * far[k] + z_half},
        )

    def db_arrival(k):
        part = db_recv.at[near[k]]
        return remote(part, part, db_ss.at[k], db_rs.at[k], {"z": 2 * far[k] + z_half})

    for t in range(1, STEPS):
        gz_arrival(t).wait_recv()

    @pl.loop(0, GATES)
    def _(gate):
        rows = jnp.concatenate([grads_t[t, z_half, gate] for t in range(STEPS)], axis=1)
        rows_pair = jnp.concatenate([grads_pair[t, gate] for t in range(1, STEPS)], axis=1)
        for j in range(4):
            columns = slice(j * 2 * LANES, (j + 1) * 2 * LANES)
            dw_acc[gate, :, columns] = nn_dot(rows, hmat[:, columns]) + nn_dot(
                rows_pair, hmat_pair[ALL_ROWS:, columns]
            )
        db_send[gate] = nt_dot(jnp.ones((8, STEPS * ALL_ROWS), BF16), rows) + nt_dot(
            jnp.ones((8, (STEPS - 1) * ALL_ROWS), BF16), rows_pair
        )

    gz_arrival(0).wait_recv()
    for k in range(QUADS):
        gate = far[k] if k < QUADS - 1 else quad
        rows_pair = grads_pair[0, gate]
        db_send[gate] = db_send[gate] + nt_dot(jnp.ones((8, ALL_ROWS), BF16), rows_pair)
        for j in range(4):
            columns = slice(j * 2 * LANES, (j + 1) * 2 * LANES)
            part = dw_acc[gate, :, columns] + nn_dot(rows_pair, hmat_pair[:ALL_ROWS, columns])
            if k < QUADS - 1:
                dw_send[gate, :, columns] = part.astype(BF16)
            else:
                dw_acc[gate, :, columns] = part
        if k < QUADS - 1:
            db_copy(k).start()
            dw_copy(k).start()

    def dw2_copy(p):
        return remote(
            dw2_send.at[p], dw2_recv.at[x], dw2_ss.at[p], dw2_rs.at[x],
            {"x": owner_x, "y": owner_y[p]},
        )

    def db2_copy(p):
        return remote(
            db2_send, db2_recv.at[x], db2_ss.at[p], db2_rs.at[x],
            {"x": owner_x, "y": owner_y[p]},
        )

    for k in range(QUADS - 1):
        db_arrival(k).wait_recv()
    db2_send[...] = db_send[quad] + db_recv[near[0]] + db_recv[near[1]] + db_recv[near[2]]
    for k in range(QUADS - 1):
        dw_arrival(k).wait_recv()
    for p in range(2):
        rows = slice(p * LANES // 2, (p + 1) * LANES // 2)
        value = dw_acc[quad, rows, :]
        for k in range(QUADS - 1):
            value = value + dw_recv[near[k], rows, :].astype(F32)
        dw2_send[p] = value.astype(BF16)

        @pl.when(is_me(z, owner_x, owner_y[p]))
        def _():
            dw2_recv[x] = dw2_send[p]
            db2_recv[x] = db2_send[...]

        @pl.when(jnp.logical_not(is_me(z, owner_x, owner_y[p])))
        def _():
            db2_copy(p).start()
            dw2_copy(p).start()

    for xx in range(X):
        @pl.when(jnp.logical_not(is_me(z, xx, user_y)))
        def _():
            where = {"x": xx, "y": user_y}
            dw_part = dw2_recv.at[xx]
            db_part = db2_recv.at[xx]
            remote(db_part, db_part, db2_ss.at[0], db2_rs.at[xx], where).wait_recv()
            remote(dw_part, dw_part, dw2_ss.at[0], dw2_rs.at[xx], where).wait_recv()

    dw_out[...] = dw2_recv[0].astype(F32) + dw2_recv[1].astype(F32)
    bias_sum = db2_recv[0, 0:1, :] + db2_recv[1, 0:1, :]
    db_out[...] = jnp.where(own_half == 0, bias_sum[:, : LANES // 2], bias_sum[:, LANES // 2 :])

    for xx in range(X):
        @pl.when(jnp.logical_not(is_me(z, xx, user_y)))
        def _():
            first_hop(xx).wait_send()

    for k in range(S - 1):
        st_copy(k).wait_send()
    for step in range(Z // 2):
        for p in range(2):
            for way in range(2):
                if ring_has(way, step, p):
                    ring(way, step, p).wait_send()
    for k in range(Y - 1):
        info_copy(k).wait_send()
        h0_copy(k).wait_send()
        c0_copy(k).wait_send()

    @pl.when(s == 0)
    def _():
        for k in range(Y - 1):
            obs_copy(k).wait_send()

    @pl.when(s == S - 1)
    def _():
        for k in range(Y - 1):
            cot_copy(k).wait_send()

    @pl.loop(0, STEPS)
    def _(t):
        for k in range(Y - 1):
            h_copy(t + 1, k).wait_send()

        @pl.when(s < S - 1)
        def _():
            x_copy(t).wait_send()

        hz_copy(t).wait_send()
        gz_copy(t).wait_send()

        @pl.when(t > 0)
        def _():
            for k in range(Y - 1):
                a_copy(t, k).wait_send()

        @pl.when(s > 0)
        def _():
            for k in range(Y - 1):
                g_copy(t, k).wait_send()
            e_copy(t).wait_send()

    for k in range(QUADS - 1):
        dw_copy(k).wait_send()
        db_copy(k).wait_send()
    for p in range(2):
        @pl.when(jnp.logical_not(is_me(z, owner_x, owner_y[p])))
        def _():
            dw2_copy(p).wait_send()
            db2_copy(p).wait_send()

    hid_copy.wait()


def on_device(
    obs_features, w_input, w_recurrent, bias, stored_states, state_owner, burn_steps, valid_steps, cotangent
):
    vmem = pl.BlockSpec(memory_space=pltpu.VMEM)
    hbm = pl.BlockSpec(memory_space=pl.ANY)
    dma = pltpu.SemaphoreType.DMA
    piece = (Y, ROWS, LANES)
    hidden, weights, biases = pl.pallas_call(
        kernel,
        out_shape=(
            jax.ShapeDtypeStruct((STEPS, ROWS, D), BF16),
            jax.ShapeDtypeStruct((LANES // 2, D), F32),
            jax.ShapeDtypeStruct((1, LANES // 2), F32),
        ),
        in_specs=[hbm, hbm, hbm, hbm, vmem, hbm, vmem, vmem, vmem],
        out_specs=(hbm, vmem, vmem),
        scratch_shapes=[
            pltpu.VMEM((STEPS, ROWS, D), BF16),
            pltpu.VMEM((STEPS, ROWS, D), BF16),
            pltpu.VMEM((Y, ROWS, LANES), F32),
            pltpu.VMEM((S, ROWS, 2 * D), BF16),
            pltpu.VMEM((2, Z, D, LANES), BF16),
            pltpu.VMEM((Z, 2, LANES // 2, D), BF16),
            pltpu.VMEM((2 * GATES, LANES, D), BF16),
            pltpu.VMEM((2, STEPS + 1, 2, Y, *piece), BF16),
            pltpu.VMEM((STEPS, 2, Y, *piece), BF16),
            pltpu.VMEM((STEPS, 2, *piece), BF16),
            pltpu.VMEM((Y, STEPS, 2, ROWS, LANES), BF16),
            pltpu.VMEM((Y, 2, ROWS, LANES), BF16),
            pltpu.VMEM((Y, 2, ROWS, LANES), BF16),
            pltpu.VMEM((STEPS + 1, 2, ALL_ROWS, LANES), F32),
            pltpu.VMEM((STEPS, GATES, 2, ALL_ROWS, LANES), F32),
            pltpu.VMEM((GATES, 2, ALL_ROWS, LANES), F32),
            pltpu.VMEM((STEPS, ALL_ROWS, LANES), F32),
            pltpu.VMEM((2 * GATES, ALL_ROWS, LANES), BF16),
            pltpu.VMEM((STEPS, 2, GATES, LANES, ALL_ROWS), BF16),
            pltpu.VMEM((STEPS, GATES, LANES, ALL_ROWS), BF16),
            pltpu.VMEM((2, ALL_ROWS, LANES), F32),
            pltpu.VMEM((STEPS, Y, 2, ALL_ROWS, LANES), BF16),
            pltpu.VMEM((STEPS, Y, 2, ALL_ROWS, LANES), BF16),
            pltpu.VMEM((STEPS, Y, 2, ALL_ROWS, LANES), BF16),
            pltpu.VMEM((STEPS, Y, 2, ALL_ROWS, LANES), BF16),
            pltpu.VMEM((STEPS, 2, *piece), BF16),
            pltpu.VMEM((STEPS * ALL_ROWS, D), BF16),
            pltpu.VMEM((STEPS * ALL_ROWS, D), BF16),
            pltpu.VMEM((GATES, LANES, D), F32),
            pltpu.VMEM((GATES, LANES, D), BF16),
            pltpu.VMEM((GATES, LANES, D), BF16),
            pltpu.VMEM((GATES, 8, LANES), F32),
            pltpu.VMEM((GATES, 8, LANES), F32),
            pltpu.VMEM((2, LANES // 2, D), BF16),
            pltpu.VMEM((X, LANES // 2, D), BF16),
            pltpu.VMEM((8, LANES), F32),
            pltpu.VMEM((X, 8, LANES), F32),
            pltpu.VMEM((STEPS, ROWS, D), BF16),
            dma((2,)),
            dma((Y - 1,)), dma((Y - 1,)),
            dma((S - 1,)), dma((S - 1,)), dma,
            dma((X,)), dma((2,)), dma,
            dma((2, Z // 2, 2)), dma((2, Z // 2, 2)),
            dma((2 * GATES,)),
            dma((Y - 1,)), dma((Y - 1,)),
            dma((Y - 1,)), dma((Y - 1,)),
            dma((Y - 1,)), dma((Y - 1,)),
            dma((STEPS + 1, Y - 1)), dma((STEPS + 1, Y - 1)),
            dma((STEPS,)), dma((STEPS,)),
            dma((STEPS,)), dma((STEPS,)),
            dma((STEPS,)), dma((STEPS,)),
            dma((STEPS, Y - 1)), dma((STEPS, Y - 1)),
            dma((STEPS, Y - 1)), dma((STEPS, Y - 1)),
            dma((STEPS,)), dma((STEPS,)),
            dma((3,)), dma((3,)),
            dma((3,)), dma((3,)),
            dma((2,)), dma((X,)),
            dma((2,)), dma((X,)),
            dma,
        ],
        compiler_params=pltpu.CompilerParams(
            collective_id=0, has_side_effects=True, vmem_limit_bytes=56 * 1024 * 1024
        ),
        name="replay_window",
    )(
        obs_features, cotangent, w_input[0], w_recurrent[0].T, bias, stored_states[0],
        state_owner[None], burn_steps[None], valid_steps[None],
    )
    return hidden[None], weights.T[None], biases


def solution(mesh):
    axes = ("s", "z", "x", "y")
    grid = Mesh(mesh.devices.reshape(S, Z, X, Y), axes)
    dp = ("z", "x", "y")
    return jax.shard_map(
        on_device,
        mesh=grid,
        in_specs=(
            P(None, dp, None),
            P("s", None, None),
            P("s", None, dp),
            P("s", None),
            P("s", None, dp, None),
            P(dp),
            P(dp),
            P(dp),
            P(None, dp, None),
        ),
        out_specs=(P("s", None, dp, None), P("s", None, dp), P("s", dp)),
        check_vma=False,
    )
```

```python
import jax
import jax.numpy as jnp
from jax import lax
from jax.experimental import pallas as pl
from jax.experimental.pallas import tpu as pltpu
from jax.sharding import Mesh
from jax.sharding import PartitionSpec as P

S, Z, X, Y = 4, 8, 2, 4
STEPS = 4
ROWS = 32
D = 1024
LANES = 128
ORDER = (0, 2, 1, 3)
GATES = 4
ALL_ROWS = Y * ROWS
LOCAL = GATES * 2 * LANES
MESH = pl.DeviceIdType.MESH
BF16 = jnp.bfloat16
F32 = jnp.float32


def sigmoid(v):
    return 0.5 * jnp.tanh(0.5 * v) + 0.5


def nt_dot(a, b):
    return lax.dot_general(a, b, (((1,), (1,)), ((), ())), preferred_element_type=F32)


def nn_dot(a, b):
    return jnp.dot(a, b, preferred_element_type=F32)


def remote(src, dst, send_sem, recv_sem, where):
    return pltpu.make_async_remote_copy(
        src_ref=src,
        dst_ref=dst,
        send_sem=send_sem,
        recv_sem=recv_sem,
        device_id=where,
        device_id_type=MESH,
    )


def kernel(
    obs_hbm, cot_hbm, win_hbm, wrt_hbm, bias_ref, st_hbm, owner_ref, burn_ref, valid_ref,
    hid_out, dw_out, db_out,
    obs_st, cot_in, info, st, wts, wrt, wint, act, hb_pair, eb, cot_st, c_st, c_in, cells, gates, acc, live,
    grads, grads_t, grads_pair, carry, a_send, a_recv, g_send, g_recv, e_send, hmat, hmat_pair,
    dw_acc, dw_send, dw_recv, db_send, db_recv, dw2_send, dw2_recv, db2_send, db2_recv,
    in_ls, info_ss, info_rs, st_ss, st_rs, st_ls, wa_ss, wa_rs, wa_ls, ring_ss, ring_rs, win_ls,
    obs_ss, obs_rs, cot_ss, cot_rs, c_ss, c_rs, h_ss, h_rs, x_ss, x_rs, hz_ss, hz_rs, gz_ss, gz_rs,
    a_ss, a_rs, g_ss, g_rs, e_ss, e_rs, dw_ss, dw_rs, db_ss, db_rs,
    dw2_ss, dw2_rs, db2_ss, db2_rs, turn_sem,
):
    xb, hb = act.at[0], act.at[1]
    s = lax.axis_index("s")
    z = lax.axis_index("z")
    x = lax.axis_index("x")
    y = lax.axis_index("y")
    up_y = [lax.rem(y + k, Y) for k in range(1, Y)]
    down_y = [lax.rem(y + Y - k, Y) for k in range(1, Y)]
    up_s = [lax.rem(s + k, S) for k in range(1, S)]
    down_s = [lax.rem(s + S - k, S) for k in range(1, S)]
    z_up, z_down = lax.rem(z + 1, Z), lax.rem(z + Z - 1, Z)
    z_half = lax.rem(z, 2)
    z_other = 1 - z_half
    z_pair = z + 1 - 2 * z_half
    quad = z // 2
    QUADS = Z // 2
    far = [lax.rem(quad + k, QUADS) for k in (2, 1, 3)]
    near = [lax.rem(quad + QUADS - k, QUADS) for k in (2, 1, 3)]
    own_half = lax.rem(y, 2)
    user_y = 2 * (y // 2) + x
    owner_x = own_half
    owner_y = [2 * (y // 2) + p for p in range(2)]
    own_block = 2 * own_half + y // 2

    def is_me(zz, xx, yy):
        return (zz == z) & (xx == x) & (yy == y)

    barrier = pltpu.get_barrier_semaphore()

    def greet(where):
        pl.semaphore_signal(barrier, inc=1, device_id=where, device_id_type=MESH)

    for k in range(Y - 1):
        greet({"y": down_y[k]})
    for k in range(S - 1):
        greet({"s": down_s[k]})
    greet({"z": z_up})
    greet({"z": z_down})
    for k in range(QUADS - 1):
        greet({"z": 2 * near[k] + z_half})
    for p in range(2):
        @pl.when(jnp.logical_not(is_me(z, owner_x, owner_y[p])))
        def _():
            greet({"x": owner_x, "y": owner_y[p]})

    for xx in range(X):
        @pl.when(jnp.logical_not(is_me(z, xx, user_y)))
        def _():
            greet({"x": xx, "y": user_y})

    mine = is_me(z, owner_x, owner_y[0]) | is_me(z, owner_x, owner_y[1])
    base = (Y - 1) + (S - 1) + 2 + (QUADS - 1) + X + 2
    obs_copy_in = pltpu.make_async_copy(obs_hbm, obs_st, in_ls.at[0])
    cot_copy_in = pltpu.make_async_copy(cot_hbm, cot_in, in_ls.at[1])

    @pl.when(s == 0)
    def _():
        obs_copy_in.start()

    @pl.when(s == S - 1)
    def _():
        cot_copy_in.start()

    pl.semaphore_wait(barrier, jnp.where(mine, base - 2, base))

    def first_hop(xx):
        return remote(
            wrt_hbm, wrt.at[z, own_half], wa_ss.at[xx], wa_rs.at[own_half],
            {"x": xx, "y": user_y},
        )

    own_copy = pltpu.make_async_copy(wrt_hbm, wrt.at[z, own_half], wa_ls)
    for xx in range(X):
        @pl.when(is_me(z, xx, user_y))
        def _():
            own_copy.start()

        @pl.when(jnp.logical_not(is_me(z, xx, user_y)))
        def _():
            first_hop(xx).start()

    def st_copy(k):
        return remote(st_hbm.at[up_s[k]], st.at[s], st_ss.at[k], st_rs.at[k], {"s": up_s[k]})

    def st_arrival(k):
        return remote(
            st.at[down_s[k]], st.at[down_s[k]], st_ss.at[k], st_rs.at[k], {"s": up_s[k]}
        )

    for k in range(S - 1):
        st_copy(k).start()
    st_own = pltpu.make_async_copy(st_hbm.at[s], st.at[s], st_ls)
    st_own.start()

    def win_copy(gate, half):
        first = pl.multiple_of(gate * D + half * Y * LANES + own_block * LANES, LANES)
        block = gate * 2 + half
        return pltpu.make_async_copy(
            win_hbm.at[:, pl.ds(first, LANES)],
            wts.at[0, block],
            win_ls.at[block],
        )

    for gate in range(GATES):
        for half in range(2):
            win_copy(gate, half).start()

    def column(row_ref):
        row = jnp.broadcast_to(row_ref[...].astype(F32), (ROWS, ROWS))
        down = lax.broadcasted_iota(jnp.int32, (ROWS, ROWS), 0)
        across = lax.broadcasted_iota(jnp.int32, (ROWS, ROWS), 1)
        return jnp.sum(jnp.where(down == across, row, 0.0), axis=1, keepdims=True)

    lane = lax.broadcasted_iota(jnp.int32, (ROWS, LANES), 1)
    info[y] = jnp.where(lane == 0, column(burn_ref), column(valid_ref))

    def info_copy(k):
        return remote(info.at[y], info.at[y], info_ss.at[k], info_rs.at[k], {"y": up_y[k]})

    def info_arrival(k):
        return remote(
            info.at[down_y[k]], info.at[down_y[k]], info_ss.at[k], info_rs.at[k], {"y": up_y[k]}
        )

    for k in range(Y - 1):
        info_copy(k).start()

    def obs_copy(k):
        return remote(
            xb.at[:, :, :, y], xb.at[:, :, :, y], obs_ss.at[k], obs_rs.at[k], {"y": up_y[k]}
        )

    def obs_arrival(k):
        part = xb.at[:, :, :, down_y[k]]
        return remote(part, part, obs_ss.at[k], obs_rs.at[k], {"y": up_y[k]})

    @pl.when(s == 0)
    def _():
        obs_copy_in.wait()
        for t in range(STEPS):
            for half in range(2):
                for yy in range(Y):
                    first = (half * Y + ORDER[yy]) * LANES
                    xb[t, half, yy, y] = obs_st[t, :, first : first + LANES]
        for k in range(Y - 1):
            obs_copy(k).start()

    def cot_copy(k):
        return remote(
            cot_st.at[up_y[k]], eb.at[:, :, y], cot_ss.at[k], cot_rs.at[k], {"y": up_y[k]}
        )

    def cot_arrival(k):
        part = eb.at[:, :, down_y[k]]
        return remote(part, part, cot_ss.at[k], cot_rs.at[k], {"y": up_y[k]})

    @pl.when(s == S - 1)
    def _():
        cot_copy_in.wait()
        for t in range(STEPS):
            for half in range(2):
                for yy in range(Y):
                    first = (half * Y + ORDER[yy]) * LANES
                    cot_st[yy, t, half] = cot_in[t, :, first : first + LANES]
        for t in range(STEPS):
            for half in range(2):
                eb[t, half, y] = cot_st[y, t, half]
        for k in range(Y - 1):
            cot_copy(k).start()

    def ring(way, step, p):
        part = wrt.at[lax.rem(z + Z - step, Z) if way == 0 else lax.rem(z + step, Z), p]
        return remote(
            part, part, ring_ss.at[way, step, p], ring_rs.at[way, step, p],
            {"z": z_up if way == 0 else z_down},
        )

    def ring_arrival(way, step, p):
        part = wrt.at[lax.rem(z + Z - 1 - step, Z) if way == 0 else lax.rem(z + 1 + step, Z), p]
        return remote(
            part, part, ring_ss.at[way, step, p], ring_rs.at[way, step, p],
            {"z": z_up if way == 0 else z_down},
        )

    def ring_has(way, step, p):
        return step < Z // 2 - 1 or p == way

    def ring_turn(step):
        for p in range(2):
            for way in range(2):
                if ring_has(way, step - 1, p):
                    ring_arrival(way, step - 1, p).wait_recv()
                if step < Z // 2 and ring_has(way, step, p):
                    ring(way, step, p).start()

    leads = lax.rem(s, 2) == 0

    def turn_block(plane):
        block = wrt[plane].reshape(LANES, D)
        for n in range(2 * Y):
            wts[1, plane, n * LANES : (n + 1) * LANES, :] = block[:, n * LANES : (n + 1) * LANES].T

    for p in range(2):
        @pl.when(is_me(z, owner_x, owner_y[p]))
        def _():
            own_copy.wait()

        @pl.when(jnp.logical_not(is_me(z, owner_x, owner_y[p])))
        def _():
            part = wrt.at[z, p]
            remote(
                part, part, wa_ss.at[0], wa_rs.at[p], {"x": owner_x, "y": owner_y[p]}
            ).wait_recv()

        @pl.when(leads)
        def _():
            for way in range(2):
                ring(way, 0, p).start()

    st_own.wait()
    for k in range(S - 1):
        st_arrival(k).wait_recv()
    owners = jnp.broadcast_to(column(owner_ref), (ROWS, LANES))

    def chosen(first):
        value = jnp.zeros((ROWS, LANES), F32)
        for owner in range(S):
            entry = st[owner, :, first : first + LANES].astype(F32)
            value = value + jnp.where(owners == float(owner), entry, 0.0)
        return value.astype(BF16)

    for half in range(2):
        for yy in range(Y):
            first = (half * Y + ORDER[yy]) * LANES
            hb[0, half, yy, y] = chosen(first)
            c_st[yy, half] = chosen(D + first)
    c_in[y] = c_st[y]

    def h0_copy(k):
        part = hb.at[0, :, :, y]
        return remote(part, part, h_ss.at[0, k], h_rs.at[0, k], {"y": up_y[k]})

    def h0_arrival(k):
        part = hb.at[0, :, :, down_y[k]]
        return remote(part, part, h_ss.at[0, k], h_rs.at[0, k], {"y": up_y[k]})

    def c0_copy(k):
        return remote(c_st.at[up_y[k]], c_in.at[y], c_ss.at[k], c_rs.at[k], {"y": up_y[k]})

    def c0_arrival(k):
        part = c_in.at[down_y[k]]
        return remote(part, part, c_ss.at[k], c_rs.at[k], {"y": up_y[k]})

    for k in range(Y - 1):
        h0_copy(k).start()
        c0_copy(k).start()

    turn_block(z)

    @pl.when(jnp.logical_not(leads))
    def _():
        pl.semaphore_wait(turn_sem, 1)
        for p in range(2):
            for way in range(2):
                ring(way, 0, p).start()

    ring_turn(1)
    turn_block(z_up)
    turn_block(z_down)
    for k in range(Y - 1):
        info_arrival(k).wait_recv()
        c0_arrival(k).wait_recv()
    marks_all = info[...].reshape(ALL_ROWS, LANES)
    for t in range(STEPS):
        alive_now = (marks_all[:, 0:1] <= float(t)) & (marks_all[:, 1:2] > float(t))
        live[t] = jnp.broadcast_to(jnp.where(alive_now, 1.0, 0.0), (ALL_ROWS, LANES))
    for half in range(2):
        cells[0, half] = c_in[:, half].reshape(ALL_ROWS, LANES).astype(F32)

    ring_turn(2)

    @pl.when(leads)
    def _():
        pl.semaphore_signal(turn_sem, inc=1, device_id={"s": up_s[0]}, device_id_type=MESH)

    turn_block(lax.rem(z + 2, Z))
    turn_block(lax.rem(z + Z - 2, Z))
    for gate in range(GATES):
        for half in range(2):
            win_copy(gate, half).wait()

    ring_turn(3)
    turn_block(lax.rem(z + 3, Z))
    turn_block(lax.rem(z + Z - 3, Z))

    @pl.when(s == 0)
    def _():
        for k in range(Y - 1):
            obs_arrival(k).wait_recv()

    @pl.when(s > 0)
    def _():
        @pl.loop(0, 2 * GATES)
        def _(block):
            for n in range(2 * Y):
                piece = wts[0, block, n * LANES : (n + 1) * LANES, :]
                wint[block, :, n * LANES : (n + 1) * LANES] = piece.T

    @pl.when(s == S - 1)
    def _():
        for k in range(Y - 1):
            cot_arrival(k).wait_recv()

    for k in range(Y - 1):
        h0_arrival(k).wait_recv()

    def hz_copy(t):
        return remote(hb.at[t], hb_pair.at[t], hz_ss.at[t], hz_rs.at[t], {"z": z_pair})

    def hz_arrival(t):
        return remote(hb_pair.at[t], hb_pair.at[t], hz_ss.at[t], hz_rs.at[t], {"z": z_pair})

    ring_turn(4)
    turn_block(lax.rem(z + Z // 2, Z))

    def whole(ref, *at):
        return jnp.concatenate(
            [
                ref[(*at, half, yy)].reshape(ALL_ROWS, LANES)
                for half in range(2)
                for yy in ORDER
            ],
            axis=1,
        )

    def h_copy(t, k):
        part = hb.at[t, :, y]
        return remote(part, part, h_ss.at[t, k], h_rs.at[t, k], {"y": up_y[k]})

    def h_arrival(t, k):
        part = hb.at[t, :, down_y[k]]
        return remote(part, part, h_ss.at[t, k], h_rs.at[t, k], {"y": up_y[k]})

    def x_copy(t):
        return remote(hb.at[t + 1], xb.at[t], x_ss.at[t], x_rs.at[t], {"s": up_s[0]})

    def x_arrival(t):
        return remote(xb.at[t], xb.at[t], x_ss.at[t], x_rs.at[t], {"s": up_s[0]})

    def pass_up(t):
        for k in range(Y - 1):
            h_arrival(t + 1, k).wait_recv()

        @pl.when(s < S - 1)
        def _():
            x_copy(t).start()

        @pl.when(t < STEPS - 1)
        def _():
            hz_copy(t + 1).start()

        @pl.when(t == 0)
        def _():
            hz_copy(0).start()

    def product(kind, inputs, gate):
        weights = jnp.concatenate([wts[kind, 2 * gate], wts[kind, 2 * gate + 1]], axis=1)
        return nn_dot(inputs, weights)

    def first_product(kind, t):
        inputs = whole(act, kind, t)
        for gate in range(GATES):
            part = product(kind, inputs, gate)
            for half in range(2):
                first = pl.multiple_of(gate * D + half * Y * LANES + own_block * LANES, LANES)
                acc[gate, half] = (
                    part[:, half * LANES : (half + 1) * LANES] + bias_ref[:, pl.ds(first, LANES)]
                )

    last_kind = jnp.where(s == 0, 1, 0)

    @pl.loop(0, STEPS)
    def _(t):
        @pl.when(s == 0)
        def _():
            first_product(0, t)

        @pl.when(t > 0)
        def _():
            pass_up(t - 1)

        @pl.when(s > 0)
        def _():
            first_product(1, t)
            x_arrival(t).wait_recv()

        inputs = whole(act, last_kind, t)
        for gate in range(GATES):
            part = product(last_kind, inputs, gate)
            for half in range(2):
                pre = acc[gate, half] + part[:, half * LANES : (half + 1) * LANES]
                gates[t, gate, half] = jnp.tanh(pre) if gate == 2 else sigmoid(pre)
        for half in range(2):
            cell = (
                gates[t, 1, half] * cells[t, half] + gates[t, 0, half] * gates[t, 2, half]
            )
            cells[t + 1, half] = cell
            hidden = (gates[t, 3, half] * jnp.tanh(cell)).astype(BF16)
            hb[t + 1, half, y] = hidden.reshape(Y, ROWS, LANES)
        for k in range(Y - 1):
            h_copy(t + 1, k).start()

    pass_up(STEPS - 1)

    def keep_hidden():
        for t in range(STEPS):
            for half in range(2):
                for yy in range(Y):
                    first = (half * Y + ORDER[yy]) * LANES
                    hid_out[t, :, first : first + LANES] = hb[t + 1, half, yy, y]
        for t in range(STEPS):
            hz_arrival(t).wait_recv()
            hmat[t * ALL_ROWS : (t + 1) * ALL_ROWS, :] = whole(hb, t)
            hmat_pair[t * ALL_ROWS : (t + 1) * ALL_ROWS, :] = whole(hb_pair, t)

    carry[...] = jnp.zeros_like(carry)

    def gz_copy(t):
        return remote(
            grads_t.at[t, z_other], grads_pair.at[t], gz_ss.at[t], gz_rs.at[t], {"z": z_pair}
        )

    def gz_arrival(t):
        part = grads_pair.at[t]
        return remote(part, part, gz_ss.at[t], gz_rs.at[t], {"z": z_pair})

    def a_copy(t, k):
        return remote(
            a_send.at[t, up_y[k]], a_recv.at[t, y], a_ss.at[t, k], a_rs.at[t, k], {"y": up_y[k]}
        )

    def a_arrival(t, k):
        part = a_recv.at[t, down_y[k]]
        return remote(part, part, a_ss.at[t, k], a_rs.at[t, k], {"y": up_y[k]})

    def g_copy(t, k):
        return remote(
            g_send.at[t, up_y[k]], g_recv.at[t, y], g_ss.at[t, k], g_rs.at[t, k], {"y": up_y[k]}
        )

    def g_arrival(t, k):
        part = g_recv.at[t, down_y[k]]
        return remote(part, part, g_ss.at[t, k], g_rs.at[t, k], {"y": up_y[k]})

    def e_copy(t):
        return remote(e_send.at[t], eb.at[t], e_ss.at[t], e_rs.at[t], {"s": down_s[0]})

    def e_arrival(t):
        return remote(eb.at[t], eb.at[t], e_ss.at[t], e_rs.at[t], {"s": down_s[0]})

    def total(sent, received, t, half):
        value = sent[t, y, half].astype(F32)
        for k in range(Y - 1):
            value = value + received[t, down_y[k], half].astype(F32)
        return value

    @pl.loop(0, STEPS)
    def _(back):
        t = STEPS - 1 - back

        @pl.when(s < S - 1)
        def _():
            e_arrival(t).wait_recv()

        for half in range(2):
            acc[0, half] = eb[t, half].reshape(ALL_ROWS, LANES).astype(F32)

        @pl.when(back > 0)
        def _():
            for k in range(Y - 1):
                a_arrival(t + 1, k).wait_recv()
            for half in range(2):
                acc[0, half] = acc[0, half] + total(a_send, a_recv, t + 1, half)

        for half in range(2):
            in_gate = gates[t, 0, half]
            forget = gates[t, 1, half]
            candidate = gates[t, 2, half]
            out_gate = gates[t, 3, half]
            alive = live[t]
            total_h = acc[0, half]
            squashed = jnp.tanh(cells[t + 1, half])
            total_c = carry[half] + total_h * out_gate * (1.0 - squashed * squashed)
            parts = (
                total_c * candidate * in_gate * (1.0 - in_gate) * alive,
                total_c * cells[t, half] * forget * (1.0 - forget) * alive,
                total_c * in_gate * (1.0 - candidate * candidate) * alive,
                total_h * squashed * out_gate * (1.0 - out_gate) * alive,
            )
            carry[half] = total_c * forget * alive
            for gate in range(GATES):
                grads[2 * gate + half] = parts[gate].astype(BF16)

        gate_grads = jnp.concatenate([grads[block] for block in range(2 * GATES)], axis=1)

        @pl.when(t > 0)
        def _():
            for j in range(4):
                columns = slice(j * 2 * LANES, (j + 1) * 2 * LANES)
                part = nn_dot(
                    gate_grads, wrt[:, :, :, columns].reshape(LOCAL, 2 * LANES)
                ).astype(BF16)
                for n in range(2):
                    block = 2 * j + n
                    a_send[t, ORDER[block % Y], block // Y] = part[:, n * LANES : (n + 1) * LANES]
            for k in range(Y - 1):
                a_copy(t, k).start()

        @pl.when(s > 0)
        def _():
            for j in range(4):
                columns = slice(j * 2 * LANES, (j + 1) * 2 * LANES)
                part = nn_dot(
                    gate_grads, wint[:, :, columns].reshape(LOCAL, 2 * LANES)
                ).astype(BF16)
                for n in range(2):
                    block = 2 * j + n
                    g_send[t, ORDER[block % Y], block // Y] = part[:, n * LANES : (n + 1) * LANES]
            for k in range(Y - 1):
                g_copy(t, k).start()

        for gate in range(GATES):
            for half in range(2):
                grads_t[t, half, gate] = grads[2 * gate + half].T
        gz_copy(t).start()

        @pl.when(back == 0)
        def _():
            keep_hidden()

        @pl.when(s > 0)
        def _():
            for k in range(Y - 1):
                g_arrival(t, k).wait_recv()
            for half in range(2):
                e_send[t, half] = total(g_send, g_recv, t, half).astype(BF16).reshape(
                    Y, ROWS, LANES
                )
            e_copy(t).start()

    def dw_copy(k, p):
        return remote(
            dw_send.at[far[k], p], dw_recv.at[quad, p], dw_ss.at[k, p], dw_rs.at[k, p],
            {"z": 2 * far[k] + z_half},
        )

    def dw_arrival(k, p):
        part = dw_recv.at[near[k], p]
        return remote(part, part, dw_ss.at[k, p], dw_rs.at[k, p], {"z": 2 * far[k] + z_half})

    def db_copy(k):
        return remote(
            db_send.at[far[k]], db_recv.at[quad], db_ss.at[k], db_rs.at[k],
            {"z": 2 * far[k] + z_half},
        )

    def db_arrival(k):
        part = db_recv.at[near[k]]
        return remote(part, part, db_ss.at[k], db_rs.at[k], {"z": 2 * far[k] + z_half})

    for t in range(1, STEPS):
        gz_arrival(t).wait_recv()

    @pl.loop(0, GATES)
    def _(gate):
        rows = jnp.concatenate([grads_t[t, z_half, gate] for t in range(STEPS)], axis=1)
        rows_pair = jnp.concatenate([grads_pair[t, gate] for t in range(1, STEPS)], axis=1)
        for j in range(4):
            columns = slice(j * 2 * LANES, (j + 1) * 2 * LANES)
            dw_acc[gate, :, columns] = nn_dot(rows, hmat[:, columns]) + nn_dot(
                rows_pair, hmat_pair[ALL_ROWS:, columns]
            )
        db_send[gate] = nt_dot(jnp.ones((8, STEPS * ALL_ROWS), BF16), rows) + nt_dot(
            jnp.ones((8, (STEPS - 1) * ALL_ROWS), BF16), rows_pair
        )

    gz_arrival(0).wait_recv()
    for k in range(QUADS):
        gate = far[k] if k < QUADS - 1 else quad
        rows_pair = grads_pair[0, gate]
        db_send[gate] = db_send[gate] + nt_dot(jnp.ones((8, ALL_ROWS), BF16), rows_pair)
        for j in range(4):
            columns = slice(j * 2 * LANES, (j + 1) * 2 * LANES)
            part = dw_acc[gate, :, columns] + nn_dot(rows_pair, hmat_pair[:ALL_ROWS, columns])
            if k < QUADS - 1:
                for p in range(2):
                    rows = slice(p * LANES // 2, (p + 1) * LANES // 2)
                    dw_send[gate, p, :, columns] = part[rows].astype(BF16)
            else:
                dw_acc[gate, :, columns] = part
        if k < QUADS - 1:
            db_copy(k).start()
            dw_copy(k, 0).start()
    for k in range(QUADS - 1):
        dw_copy(k, 1).start()

    def dw2_copy(p):
        return remote(
            dw2_send.at[p], dw2_recv.at[x], dw2_ss.at[p], dw2_rs.at[x],
            {"x": owner_x, "y": owner_y[p]},
        )

    def db2_copy(p):
        return remote(
            db2_send, db2_recv.at[x], db2_ss.at[p], db2_rs.at[x],
            {"x": owner_x, "y": owner_y[p]},
        )

    for k in range(QUADS - 1):
        db_arrival(k).wait_recv()
    db2_send[...] = db_send[quad] + db_recv[near[0]] + db_recv[near[1]] + db_recv[near[2]]
    for p in range(2):
        rows = slice(p * LANES // 2, (p + 1) * LANES // 2)
        for k in range(QUADS - 1):
            dw_arrival(k, p).wait_recv()
        value = dw_acc[quad, rows, :]
        for k in range(QUADS - 1):
            value = value + dw_recv[near[k], p].astype(F32)
        dw2_send[p] = value.astype(BF16)

        @pl.when(is_me(z, owner_x, owner_y[p]))
        def _():
            dw2_recv[x] = dw2_send[p]
            db2_recv[x] = db2_send[...]

        @pl.when(jnp.logical_not(is_me(z, owner_x, owner_y[p])))
        def _():
            db2_copy(p).start()
            dw2_copy(p).start()

    for xx in range(X):
        @pl.when(jnp.logical_not(is_me(z, xx, user_y)))
        def _():
            where = {"x": xx, "y": user_y}
            dw_part = dw2_recv.at[xx]
            db_part = db2_recv.at[xx]
            remote(db_part, db_part, db2_ss.at[0], db2_rs.at[xx], where).wait_recv()
            remote(dw_part, dw_part, dw2_ss.at[0], dw2_rs.at[xx], where).wait_recv()

    dw_out[...] = dw2_recv[0].astype(F32) + dw2_recv[1].astype(F32)
    bias_sum = db2_recv[0, 0:1, :] + db2_recv[1, 0:1, :]
    db_out[...] = jnp.where(own_half == 0, bias_sum[:, : LANES // 2], bias_sum[:, LANES // 2 :])

    for xx in range(X):
        @pl.when(jnp.logical_not(is_me(z, xx, user_y)))
        def _():
            first_hop(xx).wait_send()

    for k in range(S - 1):
        st_copy(k).wait_send()
    for step in range(Z // 2):
        for p in range(2):
            for way in range(2):
                if ring_has(way, step, p):
                    ring(way, step, p).wait_send()
    for k in range(Y - 1):
        info_copy(k).wait_send()
        h0_copy(k).wait_send()
        c0_copy(k).wait_send()

    @pl.when(s == 0)
    def _():
        for k in range(Y - 1):
            obs_copy(k).wait_send()

    @pl.when(s == S - 1)
    def _():
        for k in range(Y - 1):
            cot_copy(k).wait_send()

    @pl.loop(0, STEPS)
    def _(t):
        for k in range(Y - 1):
            h_copy(t + 1, k).wait_send()

        @pl.when(s < S - 1)
        def _():
            x_copy(t).wait_send()

        hz_copy(t).wait_send()
        gz_copy(t).wait_send()

        @pl.when(t > 0)
        def _():
            for k in range(Y - 1):
                a_copy(t, k).wait_send()

        @pl.when(s > 0)
        def _():
            for k in range(Y - 1):
                g_copy(t, k).wait_send()
            e_copy(t).wait_send()

    for k in range(QUADS - 1):
        for p in range(2):
            dw_copy(k, p).wait_send()
        db_copy(k).wait_send()
    for p in range(2):
        @pl.when(jnp.logical_not(is_me(z, owner_x, owner_y[p])))
        def _():
            dw2_copy(p).wait_send()
            db2_copy(p).wait_send()


def on_device(
    obs_features, w_input, w_recurrent, bias, stored_states, state_owner, burn_steps, valid_steps, cotangent
):
    vmem = pl.BlockSpec(memory_space=pltpu.VMEM)
    hbm = pl.BlockSpec(memory_space=pl.ANY)
    dma = pltpu.SemaphoreType.DMA
    piece = (Y, ROWS, LANES)
    hidden, weights, biases = pl.pallas_call(
        kernel,
        out_shape=(
            pltpu.VMEM((STEPS, ROWS, D), BF16),
            pltpu.VMEM((LANES // 2, D), F32),
            pltpu.VMEM((1, LANES // 2), F32),
        ),
        in_specs=[hbm, hbm, hbm, hbm, vmem, hbm, vmem, vmem, vmem],
        out_specs=(vmem, vmem, vmem),
        scratch_shapes=[
            pltpu.VMEM((STEPS, ROWS, D), BF16),
            pltpu.VMEM((STEPS, ROWS, D), BF16),
            pltpu.VMEM((Y, ROWS, LANES), F32),
            pltpu.VMEM((S, ROWS, 2 * D), BF16),
            pltpu.VMEM((2, Z, D, LANES), BF16),
            pltpu.VMEM((Z, 2, LANES // 2, D), BF16),
            pltpu.VMEM((2 * GATES, LANES, D), BF16),
            pltpu.VMEM((2, STEPS + 1, 2, Y, *piece), BF16),
            pltpu.VMEM((STEPS, 2, Y, *piece), BF16),
            pltpu.VMEM((STEPS, 2, *piece), BF16),
            pltpu.VMEM((Y, STEPS, 2, ROWS, LANES), BF16),
            pltpu.VMEM((Y, 2, ROWS, LANES), BF16),
            pltpu.VMEM((Y, 2, ROWS, LANES), BF16),
            pltpu.VMEM((STEPS + 1, 2, ALL_ROWS, LANES), F32),
            pltpu.VMEM((STEPS, GATES, 2, ALL_ROWS, LANES), F32),
            pltpu.VMEM((GATES, 2, ALL_ROWS, LANES), F32),
            pltpu.VMEM((STEPS, ALL_ROWS, LANES), F32),
            pltpu.VMEM((2 * GATES, ALL_ROWS, LANES), BF16),
            pltpu.VMEM((STEPS, 2, GATES, LANES, ALL_ROWS), BF16),
            pltpu.VMEM((STEPS, GATES, LANES, ALL_ROWS), BF16),
            pltpu.VMEM((2, ALL_ROWS, LANES), F32),
            pltpu.VMEM((STEPS, Y, 2, ALL_ROWS, LANES), BF16),
            pltpu.VMEM((STEPS, Y, 2, ALL_ROWS, LANES), BF16),
            pltpu.VMEM((STEPS, Y, 2, ALL_ROWS, LANES), BF16),
            pltpu.VMEM((STEPS, Y, 2, ALL_ROWS, LANES), BF16),
            pltpu.VMEM((STEPS, 2, *piece), BF16),
            pltpu.VMEM((STEPS * ALL_ROWS, D), BF16),
            pltpu.VMEM((STEPS * ALL_ROWS, D), BF16),
            pltpu.VMEM((GATES, LANES, D), F32),
            pltpu.VMEM((GATES, 2, LANES // 2, D), BF16),
            pltpu.VMEM((GATES, 2, LANES // 2, D), BF16),
            pltpu.VMEM((GATES, 8, LANES), F32),
            pltpu.VMEM((GATES, 8, LANES), F32),
            pltpu.VMEM((2, LANES // 2, D), BF16),
            pltpu.VMEM((X, LANES // 2, D), BF16),
            pltpu.VMEM((8, LANES), F32),
            pltpu.VMEM((X, 8, LANES), F32),
            dma((2,)),
            dma((Y - 1,)), dma((Y - 1,)),
            dma((S - 1,)), dma((S - 1,)), dma,
            dma((X,)), dma((2,)), dma,
            dma((2, Z // 2, 2)), dma((2, Z // 2, 2)),
            dma((2 * GATES,)),
            dma((Y - 1,)), dma((Y - 1,)),
            dma((Y - 1,)), dma((Y - 1,)),
            dma((Y - 1,)), dma((Y - 1,)),
            dma((STEPS + 1, Y - 1)), dma((STEPS + 1, Y - 1)),
            dma((STEPS,)), dma((STEPS,)),
            dma((STEPS,)), dma((STEPS,)),
            dma((STEPS,)), dma((STEPS,)),
            dma((STEPS, Y - 1)), dma((STEPS, Y - 1)),
            dma((STEPS, Y - 1)), dma((STEPS, Y - 1)),
            dma((STEPS,)), dma((STEPS,)),
            dma((3, 2)), dma((3, 2)),
            dma((3,)), dma((3,)),
            dma((2,)), dma((X,)),
            dma((2,)), dma((X,)),
            pltpu.SemaphoreType.REGULAR,
        ],
        compiler_params=pltpu.CompilerParams(
            collective_id=0, has_side_effects=True, vmem_limit_bytes=56 * 1024 * 1024
        ),
        name="replay_window",
    )(
        obs_features, cotangent, w_input[0], w_recurrent[0].T, bias, stored_states[0],
        state_owner[None], burn_steps[None], valid_steps[None],
    )
    return hidden[None], weights.T[None], biases


def solution(mesh):
    axes = ("s", "z", "x", "y")
    grid = Mesh(mesh.devices.reshape(S, Z, X, Y), axes)
    dp = ("z", "x", "y")
    return jax.shard_map(
        on_device,
        mesh=grid,
        in_specs=(
            P(None, dp, None),
            P("s", None, None),
            P("s", None, dp),
            P("s", None),
            P("s", None, dp, None),
            P(dp),
            P(dp),
            P(dp),
            P(None, dp, None),
        ),
        out_specs=(P("s", None, dp, None), P("s", None, dp), P("s", dp)),
        check_vma=False,
    )
```

```python
import jax
import jax.numpy as jnp
from jax import lax
from jax.experimental import pallas as pl
from jax.experimental.pallas import tpu as pltpu
from jax.sharding import Mesh
from jax.sharding import PartitionSpec as P

S, Z, X, Y = 4, 8, 2, 4
STEPS = 4
ROWS = 32
D = 1024
LANES = 128
ORDER = (0, 2, 1, 3)
GATES = 4
ALL_ROWS = Y * ROWS
PARTS = 2
GROUPS = Y // PARTS
PART_ROWS = ALL_ROWS // PARTS
LOCAL = GATES * 2 * LANES
MESH = pl.DeviceIdType.MESH
BF16 = jnp.bfloat16
F32 = jnp.float32


def sigmoid(v):
    return 0.5 * jnp.tanh(0.5 * v) + 0.5


def nt_dot(a, b):
    return lax.dot_general(a, b, (((1,), (1,)), ((), ())), preferred_element_type=F32)


def nn_dot(a, b):
    return jnp.dot(a, b, preferred_element_type=F32)


def remote(src, dst, send_sem, recv_sem, where):
    return pltpu.make_async_remote_copy(
        src_ref=src,
        dst_ref=dst,
        send_sem=send_sem,
        recv_sem=recv_sem,
        device_id=where,
        device_id_type=MESH,
    )


def kernel(
    obs_hbm, cot_hbm, win_hbm, wrt_hbm, bias_ref, st_hbm, owner_ref, burn_ref, valid_ref,
    hid_out, dw_out, db_out,
    obs_st, cot_in, info, st, wts, wrt, wint, act, hb_pair, eb, cot_st, c_st, c_in, cells, gates, acc, live,
    grads, grads_t, grads_pair, carry, a_send, a_recv, g_send, g_recv, e_send, hmat, hmat_pair,
    dw_acc, dw_send, dw_recv, db_send, db_recv, dw2_send, dw2_recv, db2_send, db2_recv,
    in_ls, info_ss, info_rs, st_ss, st_rs, st_ls, wa_ss, wa_rs, wa_ls, ring_ss, ring_rs, win_ls,
    obs_ss, obs_rs, cot_ss, cot_rs, c_ss, c_rs, h_ss, h_rs, x_ss, x_rs, hz_ss, hz_rs, gz_ss, gz_rs,
    a_ss, a_rs, g_ss, g_rs, e_ss, e_rs, dw_ss, dw_rs, db_ss, db_rs,
    dw2_ss, dw2_rs, db2_ss, db2_rs, turn_sem,
):
    xb, hb = act.at[0], act.at[1]
    s = lax.axis_index("s")
    z = lax.axis_index("z")
    x = lax.axis_index("x")
    y = lax.axis_index("y")
    up_y = [lax.rem(y + k, Y) for k in range(1, Y)]
    down_y = [lax.rem(y + Y - k, Y) for k in range(1, Y)]
    up_s = [lax.rem(s + k, S) for k in range(1, S)]
    down_s = [lax.rem(s + S - k, S) for k in range(1, S)]
    z_up, z_down = lax.rem(z + 1, Z), lax.rem(z + Z - 1, Z)
    z_half = lax.rem(z, 2)
    z_other = 1 - z_half
    z_pair = z + 1 - 2 * z_half
    quad = z // 2
    QUADS = Z // 2
    far = [lax.rem(quad + k, QUADS) for k in (2, 1, 3)]
    near = [lax.rem(quad + QUADS - k, QUADS) for k in (2, 1, 3)]
    own_half = lax.rem(y, 2)
    user_y = 2 * (y // 2) + x
    owner_x = own_half
    owner_y = [2 * (y // 2) + p for p in range(2)]
    own_block = 2 * own_half + y // 2

    def is_me(zz, xx, yy):
        return (zz == z) & (xx == x) & (yy == y)

    barrier = pltpu.get_barrier_semaphore()

    def greet(where):
        pl.semaphore_signal(barrier, inc=1, device_id=where, device_id_type=MESH)

    for k in range(Y - 1):
        greet({"y": down_y[k]})
    for k in range(S - 1):
        greet({"s": down_s[k]})
    greet({"z": z_up})
    greet({"z": z_down})
    for k in range(QUADS - 1):
        greet({"z": 2 * near[k] + z_half})
    for p in range(2):
        @pl.when(jnp.logical_not(is_me(z, owner_x, owner_y[p])))
        def _():
            greet({"x": owner_x, "y": owner_y[p]})

    for xx in range(X):
        @pl.when(jnp.logical_not(is_me(z, xx, user_y)))
        def _():
            greet({"x": xx, "y": user_y})

    mine = is_me(z, owner_x, owner_y[0]) | is_me(z, owner_x, owner_y[1])
    base = (Y - 1) + (S - 1) + 2 + (QUADS - 1) + X + 2
    obs_copy_in = pltpu.make_async_copy(obs_hbm, obs_st, in_ls.at[0])
    cot_copy_in = pltpu.make_async_copy(cot_hbm, cot_in, in_ls.at[1])

    @pl.when(s == 0)
    def _():
        obs_copy_in.start()

    @pl.when(s == S - 1)
    def _():
        cot_copy_in.start()

    pl.semaphore_wait(barrier, jnp.where(mine, base - 2, base))

    def first_hop(xx):
        return remote(
            wrt_hbm, wrt.at[z, own_half], wa_ss.at[xx], wa_rs.at[own_half],
            {"x": xx, "y": user_y},
        )

    own_copy = pltpu.make_async_copy(wrt_hbm, wrt.at[z, own_half], wa_ls)
    for xx in range(X):
        @pl.when(is_me(z, xx, user_y))
        def _():
            own_copy.start()

        @pl.when(jnp.logical_not(is_me(z, xx, user_y)))
        def _():
            first_hop(xx).start()

    def st_copy(k):
        return remote(st_hbm.at[up_s[k]], st.at[s], st_ss.at[k], st_rs.at[k], {"s": up_s[k]})

    def st_arrival(k):
        return remote(
            st.at[down_s[k]], st.at[down_s[k]], st_ss.at[k], st_rs.at[k], {"s": up_s[k]}
        )

    for k in range(S - 1):
        st_copy(k).start()
    st_own = pltpu.make_async_copy(st_hbm.at[s], st.at[s], st_ls)
    st_own.start()

    def win_copy(gate, half):
        first = pl.multiple_of(gate * D + half * Y * LANES + own_block * LANES, LANES)
        block = gate * 2 + half
        return pltpu.make_async_copy(
            win_hbm.at[:, pl.ds(first, LANES)],
            wts.at[0, block],
            win_ls.at[block],
        )

    for gate in range(GATES):
        for half in range(2):
            win_copy(gate, half).start()

    def column(row_ref):
        row = jnp.broadcast_to(row_ref[...].astype(F32), (ROWS, ROWS))
        down = lax.broadcasted_iota(jnp.int32, (ROWS, ROWS), 0)
        across = lax.broadcasted_iota(jnp.int32, (ROWS, ROWS), 1)
        return jnp.sum(jnp.where(down == across, row, 0.0), axis=1, keepdims=True)

    lane = lax.broadcasted_iota(jnp.int32, (ROWS, LANES), 1)
    info[y] = jnp.where(lane == 0, column(burn_ref), column(valid_ref))

    def info_copy(k):
        return remote(info.at[y], info.at[y], info_ss.at[k], info_rs.at[k], {"y": up_y[k]})

    def info_arrival(k):
        return remote(
            info.at[down_y[k]], info.at[down_y[k]], info_ss.at[k], info_rs.at[k], {"y": up_y[k]}
        )

    for k in range(Y - 1):
        info_copy(k).start()

    def obs_copy(k):
        return remote(
            xb.at[:, :, :, y], xb.at[:, :, :, y], obs_ss.at[k], obs_rs.at[k], {"y": up_y[k]}
        )

    def obs_arrival(k):
        part = xb.at[:, :, :, down_y[k]]
        return remote(part, part, obs_ss.at[k], obs_rs.at[k], {"y": up_y[k]})

    @pl.when(s == 0)
    def _():
        obs_copy_in.wait()
        for t in range(STEPS):
            for half in range(2):
                for yy in range(Y):
                    first = (half * Y + ORDER[yy]) * LANES
                    xb[t, half, yy, y] = obs_st[t, :, first : first + LANES]
        for k in range(Y - 1):
            obs_copy(k).start()

    def cot_copy(k):
        return remote(
            cot_st.at[up_y[k]], eb.at[:, :, y], cot_ss.at[k], cot_rs.at[k], {"y": up_y[k]}
        )

    def cot_arrival(k):
        part = eb.at[:, :, down_y[k]]
        return remote(part, part, cot_ss.at[k], cot_rs.at[k], {"y": up_y[k]})

    @pl.when(s == S - 1)
    def _():
        cot_copy_in.wait()
        for t in range(STEPS):
            for half in range(2):
                for yy in range(Y):
                    first = (half * Y + ORDER[yy]) * LANES
                    cot_st[yy, t, half] = cot_in[t, :, first : first + LANES]
        for t in range(STEPS):
            for half in range(2):
                eb[t, half, y] = cot_st[y, t, half]
        for k in range(Y - 1):
            cot_copy(k).start()

    def ring(way, step, p):
        part = wrt.at[lax.rem(z + Z - step, Z) if way == 0 else lax.rem(z + step, Z), p]
        return remote(
            part, part, ring_ss.at[way, step, p], ring_rs.at[way, step, p],
            {"z": z_up if way == 0 else z_down},
        )

    def ring_arrival(way, step, p):
        part = wrt.at[lax.rem(z + Z - 1 - step, Z) if way == 0 else lax.rem(z + 1 + step, Z), p]
        return remote(
            part, part, ring_ss.at[way, step, p], ring_rs.at[way, step, p],
            {"z": z_up if way == 0 else z_down},
        )

    def ring_has(way, step, p):
        return step < Z // 2 - 1 or p == way

    def ring_turn(step):
        for p in range(2):
            for way in range(2):
                if ring_has(way, step - 1, p):
                    ring_arrival(way, step - 1, p).wait_recv()
                if step < Z // 2 and ring_has(way, step, p):
                    ring(way, step, p).start()

    leads = lax.rem(s, 2) == 0

    def turn_block(plane):
        block = wrt[plane].reshape(LANES, D)
        for n in range(2 * Y):
            wts[1, plane, n * LANES : (n + 1) * LANES, :] = block[:, n * LANES : (n + 1) * LANES].T

    for p in range(2):
        @pl.when(is_me(z, owner_x, owner_y[p]))
        def _():
            own_copy.wait()

        @pl.when(jnp.logical_not(is_me(z, owner_x, owner_y[p])))
        def _():
            part = wrt.at[z, p]
            remote(
                part, part, wa_ss.at[0], wa_rs.at[p], {"x": owner_x, "y": owner_y[p]}
            ).wait_recv()

        @pl.when(leads)
        def _():
            for way in range(2):
                ring(way, 0, p).start()

    st_own.wait()
    for k in range(S - 1):
        st_arrival(k).wait_recv()
    owners = jnp.broadcast_to(column(owner_ref), (ROWS, LANES))

    def chosen(first):
        value = jnp.zeros((ROWS, LANES), F32)
        for owner in range(S):
            entry = st[owner, :, first : first + LANES].astype(F32)
            value = value + jnp.where(owners == float(owner), entry, 0.0)
        return value.astype(BF16)

    for half in range(2):
        for yy in range(Y):
            first = (half * Y + ORDER[yy]) * LANES
            hb[0, half, yy, y] = chosen(first)
            c_st[yy, half] = chosen(D + first)
    c_in[y] = c_st[y]

    def h0_copy(k):
        part = hb.at[0, :, :, y]
        return remote(part, part, h_ss.at[0, 0, k], h_rs.at[0, 0, k], {"y": up_y[k]})

    def h0_arrival(k):
        part = hb.at[0, :, :, down_y[k]]
        return remote(part, part, h_ss.at[0, 0, k], h_rs.at[0, 0, k], {"y": up_y[k]})

    def c0_copy(k):
        return remote(c_st.at[up_y[k]], c_in.at[y], c_ss.at[k], c_rs.at[k], {"y": up_y[k]})

    def c0_arrival(k):
        part = c_in.at[down_y[k]]
        return remote(part, part, c_ss.at[k], c_rs.at[k], {"y": up_y[k]})

    for k in range(Y - 1):
        h0_copy(k).start()
        c0_copy(k).start()

    turn_block(z)

    @pl.when(jnp.logical_not(leads))
    def _():
        pl.semaphore_wait(turn_sem, 1)
        for p in range(2):
            for way in range(2):
                ring(way, 0, p).start()

    ring_turn(1)
    turn_block(z_up)
    turn_block(z_down)
    for k in range(Y - 1):
        info_arrival(k).wait_recv()
        c0_arrival(k).wait_recv()
    marks_all = info[...].reshape(ALL_ROWS, LANES)
    for t in range(STEPS):
        alive_now = (marks_all[:, 0:1] <= float(t)) & (marks_all[:, 1:2] > float(t))
        live[t] = jnp.broadcast_to(jnp.where(alive_now, 1.0, 0.0), (ALL_ROWS, LANES)).reshape(
            PARTS, PART_ROWS, LANES
        )
    for half in range(2):
        for part in range(PARTS):
            cells[0, part, half] = (
                c_in[part * GROUPS : (part + 1) * GROUPS, half]
                .reshape(PART_ROWS, LANES)
                .astype(F32)
            )

    ring_turn(2)

    @pl.when(leads)
    def _():
        pl.semaphore_signal(turn_sem, inc=1, device_id={"s": up_s[0]}, device_id_type=MESH)

    turn_block(lax.rem(z + 2, Z))
    turn_block(lax.rem(z + Z - 2, Z))
    for gate in range(GATES):
        for half in range(2):
            win_copy(gate, half).wait()

    ring_turn(3)
    turn_block(lax.rem(z + 3, Z))
    turn_block(lax.rem(z + Z - 3, Z))

    @pl.when(s == 0)
    def _():
        for k in range(Y - 1):
            obs_arrival(k).wait_recv()

    @pl.when(s > 0)
    def _():
        @pl.loop(0, 2 * GATES)
        def _(block):
            for n in range(2 * Y):
                piece = wts[0, block, n * LANES : (n + 1) * LANES, :]
                wint[block, :, n * LANES : (n + 1) * LANES] = piece.T

    @pl.when(s == S - 1)
    def _():
        for k in range(Y - 1):
            cot_arrival(k).wait_recv()

    for k in range(Y - 1):
        h0_arrival(k).wait_recv()

    def hz_copy(t):
        return remote(hb.at[t], hb_pair.at[t], hz_ss.at[t], hz_rs.at[t], {"z": z_pair})

    def hz_arrival(t):
        return remote(hb_pair.at[t], hb_pair.at[t], hz_ss.at[t], hz_rs.at[t], {"z": z_pair})

    ring_turn(4)
    turn_block(lax.rem(z + Z // 2, Z))

    def whole(ref, *at):
        return jnp.concatenate(
            [
                ref[(*at, half, yy)].reshape(ALL_ROWS, LANES)
                for half in range(2)
                for yy in ORDER
            ],
            axis=1,
        )

    def groups(b):
        return pl.ds(b * GROUPS, GROUPS)

    def rows_of(kind, t, b):
        return jnp.concatenate(
            [
                act[kind, t, half, yy, groups(b)].reshape(PART_ROWS, LANES)
                for half in range(2)
                for yy in ORDER
            ],
            axis=1,
        )

    def h_copy(t, b, k):
        part = hb.at[t, :, y, groups(b)]
        return remote(part, part, h_ss.at[t, b, k], h_rs.at[t, b, k], {"y": up_y[k]})

    def h_arrival(t, b, k):
        part = hb.at[t, :, down_y[k], groups(b)]
        return remote(part, part, h_ss.at[t, b, k], h_rs.at[t, b, k], {"y": up_y[k]})

    def x_copy(t, b):
        return remote(
            hb.at[t + 1, :, :, groups(b)], xb.at[t, :, :, groups(b)],
            x_ss.at[t, b], x_rs.at[t, b], {"s": up_s[0]},
        )

    def x_arrival(t, b):
        part = xb.at[t, :, :, groups(b)]
        return remote(part, part, x_ss.at[t, b], x_rs.at[t, b], {"s": up_s[0]})

    def pass_up(t, b):
        for k in range(Y - 1):
            h_arrival(t + 1, b, k).wait_recv()

        @pl.when(s < S - 1)
        def _():
            x_copy(t, b).start()

        @pl.when((t < STEPS - 1) & (b == PARTS - 1))
        def _():
            hz_copy(t + 1).start()

        @pl.when((t == 0) & (b == PARTS - 1))
        def _():
            hz_copy(0).start()

    def product(kind, inputs, gate):
        weights = jnp.concatenate([wts[kind, 2 * gate], wts[kind, 2 * gate + 1]], axis=1)
        return nn_dot(inputs, weights)

    def first_product(kind, t, b):
        inputs = rows_of(kind, t, b)
        for gate in range(GATES):
            part = product(kind, inputs, gate)
            for half in range(2):
                first = pl.multiple_of(
                    gate * D + half * Y * LANES + own_block * LANES, LANES
                )
                acc[gate, half] = (
                    part[:, half * LANES : (half + 1) * LANES] + bias_ref[:, pl.ds(first, LANES)]
                )

    last_kind = jnp.where(s == 0, 1, 0)

    @pl.loop(0, STEPS * PARTS)
    def _(turn):
        t = turn // PARTS
        b = lax.rem(turn, PARTS)

        @pl.when(s == 0)
        def _():
            first_product(0, t, b)

        @pl.when(t > 0)
        def _():
            pass_up(t - 1, b)

        @pl.when(s > 0)
        def _():
            first_product(1, t, b)
            x_arrival(t, b).wait_recv()

        inputs = rows_of(last_kind, t, b)
        for gate in range(GATES):
            part = product(last_kind, inputs, gate)
            for half in range(2):
                pre = acc[gate, half] + part[:, half * LANES : (half + 1) * LANES]
                gates[t, b, gate, half] = jnp.tanh(pre) if gate == 2 else sigmoid(pre)
        for half in range(2):
            cell = (
                gates[t, b, 1, half] * cells[t, b, half]
                + gates[t, b, 0, half] * gates[t, b, 2, half]
            )
            cells[t + 1, b, half] = cell
            hidden = (gates[t, b, 3, half] * jnp.tanh(cell)).astype(BF16)
            hb[t + 1, half, y, groups(b)] = hidden.reshape(GROUPS, ROWS, LANES)
        for k in range(Y - 1):
            h_copy(t + 1, b, k).start()

    for part in range(PARTS):
        pass_up(STEPS - 1, part)

    def keep_hidden():
        for t in range(STEPS):
            for half in range(2):
                for yy in range(Y):
                    first = (half * Y + ORDER[yy]) * LANES
                    hid_out[t, :, first : first + LANES] = hb[t + 1, half, yy, y]
        for t in range(STEPS):
            hz_arrival(t).wait_recv()
            hmat[t * ALL_ROWS : (t + 1) * ALL_ROWS, :] = whole(hb, t)
            hmat_pair[t * ALL_ROWS : (t + 1) * ALL_ROWS, :] = whole(hb_pair, t)

    carry[...] = jnp.zeros_like(carry)

    def gz_copy(t):
        return remote(
            grads_t.at[t, z_other], grads_pair.at[t], gz_ss.at[t], gz_rs.at[t], {"z": z_pair}
        )

    def gz_arrival(t):
        part = grads_pair.at[t]
        return remote(part, part, gz_ss.at[t], gz_rs.at[t], {"z": z_pair})

    def a_copy(t, b, k):
        return remote(
            a_send.at[t, b, up_y[k]], a_recv.at[t, b, y], a_ss.at[t, b, k], a_rs.at[t, b, k],
            {"y": up_y[k]},
        )

    def a_arrival(t, b, k):
        part = a_recv.at[t, b, down_y[k]]
        return remote(part, part, a_ss.at[t, b, k], a_rs.at[t, b, k], {"y": up_y[k]})

    def g_copy(t, b, k):
        return remote(
            g_send.at[t, b, up_y[k]], g_recv.at[t, b, y], g_ss.at[t, b, k], g_rs.at[t, b, k],
            {"y": up_y[k]},
        )

    def g_arrival(t, b, k):
        part = g_recv.at[t, b, down_y[k]]
        return remote(part, part, g_ss.at[t, b, k], g_rs.at[t, b, k], {"y": up_y[k]})

    def e_copy(t, b):
        return remote(
            e_send.at[t, b], eb.at[t, :, groups(b)], e_ss.at[t, b], e_rs.at[t, b],
            {"s": down_s[0]},
        )

    def e_arrival(t, b):
        part = eb.at[t, :, groups(b)]
        return remote(part, part, e_ss.at[t, b], e_rs.at[t, b], {"s": down_s[0]})

    def total(sent, received, t, b, half):
        value = sent[t, b, y, half].astype(F32)
        for k in range(Y - 1):
            value = value + received[t, b, down_y[k], half].astype(F32)
        return value

    def hand_down(t, b):
        for k in range(Y - 1):
            g_arrival(t, b, k).wait_recv()
        for half in range(2):
            e_send[t, b, half] = (
                total(g_send, g_recv, t, b, half).astype(BF16).reshape(GROUPS, ROWS, LANES)
            )
        e_copy(t, b).start()

    def spread(sent, t, b, gate_grads, weights):
        for j in range(4):
            columns = slice(j * 2 * LANES, (j + 1) * 2 * LANES)
            part = nn_dot(gate_grads, weights(columns)).astype(BF16)
            for n in range(2):
                block = 2 * j + n
                sent[t, b, ORDER[block % Y], block // Y] = part[:, n * LANES : (n + 1) * LANES]

    @pl.loop(0, STEPS * PARTS)
    def _(turn):
        back = turn // PARTS
        b = lax.rem(turn, PARTS)
        t = STEPS - 1 - back

        @pl.when(s < S - 1)
        def _():
            e_arrival(t, b).wait_recv()

        for half in range(2):
            acc[0, half] = eb[t, half, groups(b)].reshape(PART_ROWS, LANES).astype(F32)

        @pl.when(back > 0)
        def _():
            for k in range(Y - 1):
                a_arrival(t + 1, b, k).wait_recv()
            for half in range(2):
                acc[0, half] = acc[0, half] + total(a_send, a_recv, t + 1, b, half)

        for half in range(2):
            in_gate = gates[t, b, 0, half]
            forget = gates[t, b, 1, half]
            candidate = gates[t, b, 2, half]
            out_gate = gates[t, b, 3, half]
            alive = live[t, b]
            total_h = acc[0, half]
            squashed = jnp.tanh(cells[t + 1, b, half])
            total_c = carry[b, half] + total_h * out_gate * (1.0 - squashed * squashed)
            parts = (
                total_c * candidate * in_gate * (1.0 - in_gate) * alive,
                total_c * cells[t, b, half] * forget * (1.0 - forget) * alive,
                total_c * in_gate * (1.0 - candidate * candidate) * alive,
                total_h * squashed * out_gate * (1.0 - out_gate) * alive,
            )
            carry[b, half] = total_c * forget * alive
            for gate in range(GATES):
                grads[b, 2 * gate + half] = parts[gate].astype(BF16)

        gate_grads = jnp.concatenate([grads[b, block] for block in range(2 * GATES)], axis=1)

        @pl.when(t > 0)
        def _():
            spread(
                a_send, t, b, gate_grads,
                lambda columns: wrt[:, :, :, columns].reshape(LOCAL, 2 * LANES),
            )
            for k in range(Y - 1):
                a_copy(t, b, k).start()

        @pl.when(s > 0)
        def _():
            spread(
                g_send, t, b, gate_grads,
                lambda columns: wint[:, :, columns].reshape(LOCAL, 2 * LANES),
            )
            for k in range(Y - 1):
                g_copy(t, b, k).start()

        @pl.when(b == PARTS - 1)
        def _():
            for gate in range(GATES):
                for half in range(2):
                    block = jnp.concatenate(
                        [grads[part, 2 * gate + half] for part in range(PARTS)], axis=0
                    )
                    grads_t[t, half, gate] = block.T
            gz_copy(t).start()

            @pl.when(s > 0)
            def _():
                for part in range(PARTS):
                    hand_down(t, part)

            @pl.when(back == 0)
            def _():
                keep_hidden()

    def dw_copy(k, p):
        return remote(
            dw_send.at[far[k], p], dw_recv.at[quad, p], dw_ss.at[k, p], dw_rs.at[k, p],
            {"z": 2 * far[k] + z_half},
        )

    def dw_arrival(k, p):
        part = dw_recv.at[near[k], p]
        return remote(part, part, dw_ss.at[k, p], dw_rs.at[k, p], {"z": 2 * far[k] + z_half})

    def db_copy(k):
        return remote(
            db_send.at[far[k]], db_recv.at[quad], db_ss.at[k], db_rs.at[k],
            {"z": 2 * far[k] + z_half},
        )

    def db_arrival(k):
        part = db_recv.at[near[k]]
        return remote(part, part, db_ss.at[k], db_rs.at[k], {"z": 2 * far[k] + z_half})

    for t in range(1, STEPS):
        gz_arrival(t).wait_recv()

    @pl.loop(0, GATES)
    def _(gate):
        rows = jnp.concatenate([grads_t[t, z_half, gate] for t in range(STEPS)], axis=1)
        rows_pair = jnp.concatenate([grads_pair[t, gate] for t in range(1, STEPS)], axis=1)
        for j in range(4):
            columns = slice(j * 2 * LANES, (j + 1) * 2 * LANES)
            dw_acc[gate, :, columns] = nn_dot(rows, hmat[:, columns]) + nn_dot(
                rows_pair, hmat_pair[ALL_ROWS:, columns]
            )
        db_send[gate] = nt_dot(jnp.ones((8, STEPS * ALL_ROWS), BF16), rows) + nt_dot(
            jnp.ones((8, (STEPS - 1) * ALL_ROWS), BF16), rows_pair
        )

    gz_arrival(0).wait_recv()
    for k in range(QUADS):
        gate = far[k] if k < QUADS - 1 else quad
        rows_pair = grads_pair[0, gate]
        db_send[gate] = db_send[gate] + nt_dot(jnp.ones((8, ALL_ROWS), BF16), rows_pair)
        for j in range(4):
            columns = slice(j * 2 * LANES, (j + 1) * 2 * LANES)
            part = dw_acc[gate, :, columns] + nn_dot(rows_pair, hmat_pair[:ALL_ROWS, columns])
            if k < QUADS - 1:
                for p in range(2):
                    rows = slice(p * LANES // 2, (p + 1) * LANES // 2)
                    dw_send[gate, p, :, columns] = part[rows].astype(BF16)
            else:
                dw_acc[gate, :, columns] = part
        if k < QUADS - 1:
            db_copy(k).start()
            dw_copy(k, 0).start()
    for k in range(QUADS - 1):
        dw_copy(k, 1).start()

    def dw2_copy(p):
        return remote(
            dw2_send.at[p], dw2_recv.at[x], dw2_ss.at[p], dw2_rs.at[x],
            {"x": owner_x, "y": owner_y[p]},
        )

    def db2_copy(p):
        return remote(
            db2_send, db2_recv.at[x], db2_ss.at[p], db2_rs.at[x],
            {"x": owner_x, "y": owner_y[p]},
        )

    for k in range(QUADS - 1):
        db_arrival(k).wait_recv()
    db2_send[...] = db_send[quad] + db_recv[near[0]] + db_recv[near[1]] + db_recv[near[2]]
    for p in range(2):
        rows = slice(p * LANES // 2, (p + 1) * LANES // 2)
        for k in range(QUADS - 1):
            dw_arrival(k, p).wait_recv()
        value = dw_acc[quad, rows, :]
        for k in range(QUADS - 1):
            value = value + dw_recv[near[k], p].astype(F32)
        dw2_send[p] = value.astype(BF16)

        @pl.when(is_me(z, owner_x, owner_y[p]))
        def _():
            dw2_recv[x] = dw2_send[p]
            db2_recv[x] = db2_send[...]

        @pl.when(jnp.logical_not(is_me(z, owner_x, owner_y[p])))
        def _():
            db2_copy(p).start()
            dw2_copy(p).start()

    for xx in range(X):
        @pl.when(jnp.logical_not(is_me(z, xx, user_y)))
        def _():
            where = {"x": xx, "y": user_y}
            dw_part = dw2_recv.at[xx]
            db_part = db2_recv.at[xx]
            remote(db_part, db_part, db2_ss.at[0], db2_rs.at[xx], where).wait_recv()
            remote(dw_part, dw_part, dw2_ss.at[0], dw2_rs.at[xx], where).wait_recv()

    dw_out[...] = dw2_recv[0].astype(F32) + dw2_recv[1].astype(F32)
    bias_sum = db2_recv[0, 0:1, :] + db2_recv[1, 0:1, :]
    db_out[...] = jnp.where(own_half == 0, bias_sum[:, : LANES // 2], bias_sum[:, LANES // 2 :])

    for xx in range(X):
        @pl.when(jnp.logical_not(is_me(z, xx, user_y)))
        def _():
            first_hop(xx).wait_send()

    for k in range(S - 1):
        st_copy(k).wait_send()
    for step in range(Z // 2):
        for p in range(2):
            for way in range(2):
                if ring_has(way, step, p):
                    ring(way, step, p).wait_send()
    for k in range(Y - 1):
        info_copy(k).wait_send()
        h0_copy(k).wait_send()
        c0_copy(k).wait_send()

    @pl.when(s == 0)
    def _():
        for k in range(Y - 1):
            obs_copy(k).wait_send()

    @pl.when(s == S - 1)
    def _():
        for k in range(Y - 1):
            cot_copy(k).wait_send()

    @pl.loop(0, STEPS)
    def _(t):
        hz_copy(t).wait_send()
        gz_copy(t).wait_send()
        for b in range(PARTS):
            for k in range(Y - 1):
                h_copy(t + 1, b, k).wait_send()

            @pl.when(s < S - 1)
            def _():
                x_copy(t, b).wait_send()

            @pl.when(t > 0)
            def _():
                for k in range(Y - 1):
                    a_copy(t, b, k).wait_send()

            @pl.when(s > 0)
            def _():
                for k in range(Y - 1):
                    g_copy(t, b, k).wait_send()
                e_copy(t, b).wait_send()

    for k in range(QUADS - 1):
        for p in range(2):
            dw_copy(k, p).wait_send()
        db_copy(k).wait_send()
    for p in range(2):
        @pl.when(jnp.logical_not(is_me(z, owner_x, owner_y[p])))
        def _():
            dw2_copy(p).wait_send()
            db2_copy(p).wait_send()


def on_device(
    obs_features, w_input, w_recurrent, bias, stored_states, state_owner, burn_steps, valid_steps, cotangent
):
    vmem = pl.BlockSpec(memory_space=pltpu.VMEM)
    hbm = pl.BlockSpec(memory_space=pl.ANY)
    dma = pltpu.SemaphoreType.DMA
    piece = (Y, ROWS, LANES)
    hidden, weights, biases = pl.pallas_call(
        kernel,
        out_shape=(
            pltpu.VMEM((STEPS, ROWS, D), BF16),
            pltpu.VMEM((LANES // 2, D), F32),
            pltpu.VMEM((1, LANES // 2), F32),
        ),
        in_specs=[hbm, hbm, hbm, hbm, vmem, hbm, vmem, vmem, vmem],
        out_specs=(vmem, vmem, vmem),
        scratch_shapes=[
            pltpu.VMEM((STEPS, ROWS, D), BF16),
            pltpu.VMEM((STEPS, ROWS, D), BF16),
            pltpu.VMEM((Y, ROWS, LANES), F32),
            pltpu.VMEM((S, ROWS, 2 * D), BF16),
            pltpu.VMEM((2, Z, D, LANES), BF16),
            pltpu.VMEM((Z, 2, LANES // 2, D), BF16),
            pltpu.VMEM((2 * GATES, LANES, D), BF16),
            pltpu.VMEM((2, STEPS + 1, 2, Y, *piece), BF16),
            pltpu.VMEM((STEPS, 2, Y, *piece), BF16),
            pltpu.VMEM((STEPS, 2, *piece), BF16),
            pltpu.VMEM((Y, STEPS, 2, ROWS, LANES), BF16),
            pltpu.VMEM((Y, 2, ROWS, LANES), BF16),
            pltpu.VMEM((Y, 2, ROWS, LANES), BF16),
            pltpu.VMEM((STEPS + 1, PARTS, 2, PART_ROWS, LANES), F32),
            pltpu.VMEM((STEPS, PARTS, GATES, 2, PART_ROWS, LANES), F32),
            pltpu.VMEM((GATES, 2, PART_ROWS, LANES), F32),
            pltpu.VMEM((STEPS, PARTS, PART_ROWS, LANES), F32),
            pltpu.VMEM((PARTS, 2 * GATES, PART_ROWS, LANES), BF16),
            pltpu.VMEM((STEPS, 2, GATES, LANES, ALL_ROWS), BF16),
            pltpu.VMEM((STEPS, GATES, LANES, ALL_ROWS), BF16),
            pltpu.VMEM((PARTS, 2, PART_ROWS, LANES), F32),
            pltpu.VMEM((STEPS, PARTS, Y, 2, PART_ROWS, LANES), BF16),
            pltpu.VMEM((STEPS, PARTS, Y, 2, PART_ROWS, LANES), BF16),
            pltpu.VMEM((STEPS, PARTS, Y, 2, PART_ROWS, LANES), BF16),
            pltpu.VMEM((STEPS, PARTS, Y, 2, PART_ROWS, LANES), BF16),
            pltpu.VMEM((STEPS, PARTS, 2, GROUPS, ROWS, LANES), BF16),
            pltpu.VMEM((STEPS * ALL_ROWS, D), BF16),
            pltpu.VMEM((STEPS * ALL_ROWS, D), BF16),
            pltpu.VMEM((GATES, LANES, D), F32),
            pltpu.VMEM((GATES, 2, LANES // 2, D), BF16),
            pltpu.VMEM((GATES, 2, LANES // 2, D), BF16),
            pltpu.VMEM((GATES, 8, LANES), F32),
            pltpu.VMEM((GATES, 8, LANES), F32),
            pltpu.VMEM((2, LANES // 2, D), BF16),
            pltpu.VMEM((X, LANES // 2, D), BF16),
            pltpu.VMEM((8, LANES), F32),
            pltpu.VMEM((X, 8, LANES), F32),
            dma((2,)),
            dma((Y - 1,)), dma((Y - 1,)),
            dma((S - 1,)), dma((S - 1,)), dma,
            dma((X,)), dma((2,)), dma,
            dma((2, Z // 2, 2)), dma((2, Z // 2, 2)),
            dma((2 * GATES,)),
            dma((Y - 1,)), dma((Y - 1,)),
            dma((Y - 1,)), dma((Y - 1,)),
            dma((Y - 1,)), dma((Y - 1,)),
            dma((STEPS + 1, PARTS, Y - 1)), dma((STEPS + 1, PARTS, Y - 1)),
            dma((STEPS, PARTS)), dma((STEPS, PARTS)),
            dma((STEPS,)), dma((STEPS,)),
            dma((STEPS,)), dma((STEPS,)),
            dma((STEPS, PARTS, Y - 1)), dma((STEPS, PARTS, Y - 1)),
            dma((STEPS, PARTS, Y - 1)), dma((STEPS, PARTS, Y - 1)),
            dma((STEPS, PARTS)), dma((STEPS, PARTS)),
            dma((3, 2)), dma((3, 2)),
            dma((3,)), dma((3,)),
            dma((2,)), dma((X,)),
            dma((2,)), dma((X,)),
            pltpu.SemaphoreType.REGULAR,
        ],
        compiler_params=pltpu.CompilerParams(
            collective_id=0, has_side_effects=True, vmem_limit_bytes=56 * 1024 * 1024
        ),
        name="replay_window",
    )(
        obs_features, cotangent, w_input[0], w_recurrent[0].T, bias, stored_states[0],
        state_owner[None], burn_steps[None], valid_steps[None],
    )
    return hidden[None], weights.T[None], biases


def solution(mesh):
    axes = ("s", "z", "x", "y")
    grid = Mesh(mesh.devices.reshape(S, Z, X, Y), axes)
    dp = ("z", "x", "y")
    return jax.shard_map(
        on_device,
        mesh=grid,
        in_specs=(
            P(None, dp, None),
            P("s", None, None),
            P("s", None, dp),
            P("s", None),
            P("s", None, dp, None),
            P(dp),
            P(dp),
            P(dp),
            P(None, dp, None),
        ),
        out_specs=(P("s", None, dp, None), P("s", None, dp), P("s", dp)),
        check_vma=False,
    )
```

```python
import jax
import jax.numpy as jnp
from jax import lax
from jax.experimental import pallas as pl
from jax.experimental.pallas import tpu as pltpu
from jax.sharding import Mesh
from jax.sharding import PartitionSpec as P

S, Z, X, Y = 4, 8, 2, 4
STEPS = 4
ROWS = 32
D = 1024
LANES = 128
ORDER = (0, 2, 1, 3)
GATES = 4
ALL_ROWS = Y * ROWS
PARTS = 4
GROUPS = Y // PARTS
PART_ROWS = ALL_ROWS // PARTS
LOCAL = GATES * 2 * LANES
MESH = pl.DeviceIdType.MESH
BF16 = jnp.bfloat16
F32 = jnp.float32


def sigmoid(v):
    return 0.5 * jnp.tanh(0.5 * v) + 0.5


def nt_dot(a, b):
    return lax.dot_general(a, b, (((1,), (1,)), ((), ())), preferred_element_type=F32)


def nn_dot(a, b):
    return jnp.dot(a, b, preferred_element_type=F32)


def remote(src, dst, send_sem, recv_sem, where):
    return pltpu.make_async_remote_copy(
        src_ref=src,
        dst_ref=dst,
        send_sem=send_sem,
        recv_sem=recv_sem,
        device_id=where,
        device_id_type=MESH,
    )


def kernel(
    obs_hbm, cot_hbm, win_hbm, wrt_hbm, bias_ref, st_hbm, owner_ref, burn_ref, valid_ref,
    hid_out, dw_out, db_out,
    obs_st, cot_in, info, st, wts, wrt, wint, act, hb_pair, eb, cot_st, c_st, c_in, cells, gates, acc, live,
    grads, grads_t, grads_pair, carry, a_send, a_recv, g_send, g_recv, e_send, hmat, hmat_pair,
    dw_acc, dw_send, dw_recv, db_send, db_recv, dw2_send, dw2_recv, db2_send, db2_recv,
    in_ls, info_ss, info_rs, st_ss, st_rs, st_ls, wa_ss, wa_rs, wa_ls, ring_ss, ring_rs, win_ls,
    obs_ss, obs_rs, cot_ss, cot_rs, c_ss, c_rs, h_ss, h_rs, x_ss, x_rs, hz_ss, hz_rs, gz_ss, gz_rs,
    a_ss, a_rs, g_ss, g_rs, e_ss, e_rs, dw_ss, dw_rs, db_ss, db_rs,
    dw2_ss, dw2_rs, db2_ss, db2_rs, turn_sem,
):
    xb, hb = act.at[0], act.at[1]
    s = lax.axis_index("s")
    z = lax.axis_index("z")
    x = lax.axis_index("x")
    y = lax.axis_index("y")
    up_y = [lax.rem(y + k, Y) for k in range(1, Y)]
    down_y = [lax.rem(y + Y - k, Y) for k in range(1, Y)]
    up_s = [lax.rem(s + k, S) for k in range(1, S)]
    down_s = [lax.rem(s + S - k, S) for k in range(1, S)]
    z_up, z_down = lax.rem(z + 1, Z), lax.rem(z + Z - 1, Z)
    z_half = lax.rem(z, 2)
    z_other = 1 - z_half
    z_pair = z + 1 - 2 * z_half
    quad = z // 2
    QUADS = Z // 2
    far = [lax.rem(quad + k, QUADS) for k in (2, 1, 3)]
    near = [lax.rem(quad + QUADS - k, QUADS) for k in (2, 1, 3)]
    own_half = lax.rem(y, 2)
    user_y = 2 * (y // 2) + x
    owner_x = own_half
    owner_y = [2 * (y // 2) + p for p in range(2)]
    own_block = 2 * own_half + y // 2

    def is_me(zz, xx, yy):
        return (zz == z) & (xx == x) & (yy == y)

    barrier = pltpu.get_barrier_semaphore()

    def greet(where):
        pl.semaphore_signal(barrier, inc=1, device_id=where, device_id_type=MESH)

    for k in range(Y - 1):
        greet({"y": down_y[k]})
    for k in range(S - 1):
        greet({"s": down_s[k]})
    greet({"z": z_up})
    greet({"z": z_down})
    for k in range(QUADS - 1):
        greet({"z": 2 * near[k] + z_half})
    for p in range(2):
        @pl.when(jnp.logical_not(is_me(z, owner_x, owner_y[p])))
        def _():
            greet({"x": owner_x, "y": owner_y[p]})

    for xx in range(X):
        @pl.when(jnp.logical_not(is_me(z, xx, user_y)))
        def _():
            greet({"x": xx, "y": user_y})

    mine = is_me(z, owner_x, owner_y[0]) | is_me(z, owner_x, owner_y[1])
    base = (Y - 1) + (S - 1) + 2 + (QUADS - 1) + X + 2
    obs_copy_in = pltpu.make_async_copy(obs_hbm, obs_st, in_ls.at[0])
    cot_copy_in = pltpu.make_async_copy(cot_hbm, cot_in, in_ls.at[1])

    @pl.when(s == 0)
    def _():
        obs_copy_in.start()

    @pl.when(s == S - 1)
    def _():
        cot_copy_in.start()

    pl.semaphore_wait(barrier, jnp.where(mine, base - 2, base))

    def first_hop(xx):
        return remote(
            wrt_hbm, wrt.at[z, own_half], wa_ss.at[xx], wa_rs.at[own_half],
            {"x": xx, "y": user_y},
        )

    own_copy = pltpu.make_async_copy(wrt_hbm, wrt.at[z, own_half], wa_ls)
    for xx in range(X):
        @pl.when(is_me(z, xx, user_y))
        def _():
            own_copy.start()

        @pl.when(jnp.logical_not(is_me(z, xx, user_y)))
        def _():
            first_hop(xx).start()

    def st_copy(k):
        return remote(st_hbm.at[up_s[k]], st.at[s], st_ss.at[k], st_rs.at[k], {"s": up_s[k]})

    def st_arrival(k):
        return remote(
            st.at[down_s[k]], st.at[down_s[k]], st_ss.at[k], st_rs.at[k], {"s": up_s[k]}
        )

    for k in range(S - 1):
        st_copy(k).start()
    st_own = pltpu.make_async_copy(st_hbm.at[s], st.at[s], st_ls)
    st_own.start()

    def win_copy(gate, half):
        first = pl.multiple_of(gate * D + half * Y * LANES + own_block * LANES, LANES)
        block = gate * 2 + half
        return pltpu.make_async_copy(
            win_hbm.at[:, pl.ds(first, LANES)],
            wts.at[0, block],
            win_ls.at[block],
        )

    for gate in range(GATES):
        for half in range(2):
            win_copy(gate, half).start()

    def column(row_ref):
        row = jnp.broadcast_to(row_ref[...].astype(F32), (ROWS, ROWS))
        down = lax.broadcasted_iota(jnp.int32, (ROWS, ROWS), 0)
        across = lax.broadcasted_iota(jnp.int32, (ROWS, ROWS), 1)
        return jnp.sum(jnp.where(down == across, row, 0.0), axis=1, keepdims=True)

    lane = lax.broadcasted_iota(jnp.int32, (ROWS, LANES), 1)
    info[y] = jnp.where(lane == 0, column(burn_ref), column(valid_ref))

    def info_copy(k):
        return remote(info.at[y], info.at[y], info_ss.at[k], info_rs.at[k], {"y": up_y[k]})

    def info_arrival(k):
        return remote(
            info.at[down_y[k]], info.at[down_y[k]], info_ss.at[k], info_rs.at[k], {"y": up_y[k]}
        )

    for k in range(Y - 1):
        info_copy(k).start()

    def obs_copy(k):
        return remote(
            xb.at[:, :, :, y], xb.at[:, :, :, y], obs_ss.at[k], obs_rs.at[k], {"y": up_y[k]}
        )

    def obs_arrival(k):
        part = xb.at[:, :, :, down_y[k]]
        return remote(part, part, obs_ss.at[k], obs_rs.at[k], {"y": up_y[k]})

    @pl.when(s == 0)
    def _():
        obs_copy_in.wait()
        for t in range(STEPS):
            for half in range(2):
                for yy in range(Y):
                    first = (half * Y + ORDER[yy]) * LANES
                    xb[t, half, yy, y] = obs_st[t, :, first : first + LANES]
        for k in range(Y - 1):
            obs_copy(k).start()

    def cot_copy(k):
        return remote(
            cot_st.at[up_y[k]], eb.at[:, :, y], cot_ss.at[k], cot_rs.at[k], {"y": up_y[k]}
        )

    def cot_arrival(k):
        part = eb.at[:, :, down_y[k]]
        return remote(part, part, cot_ss.at[k], cot_rs.at[k], {"y": up_y[k]})

    @pl.when(s == S - 1)
    def _():
        cot_copy_in.wait()
        for t in range(STEPS):
            for half in range(2):
                for yy in range(Y):
                    first = (half * Y + ORDER[yy]) * LANES
                    cot_st[yy, t, half] = cot_in[t, :, first : first + LANES]
        for t in range(STEPS):
            for half in range(2):
                eb[t, half, y] = cot_st[y, t, half]
        for k in range(Y - 1):
            cot_copy(k).start()

    def ring(way, step, p):
        part = wrt.at[lax.rem(z + Z - step, Z) if way == 0 else lax.rem(z + step, Z), p]
        return remote(
            part, part, ring_ss.at[way, step, p], ring_rs.at[way, step, p],
            {"z": z_up if way == 0 else z_down},
        )

    def ring_arrival(way, step, p):
        part = wrt.at[lax.rem(z + Z - 1 - step, Z) if way == 0 else lax.rem(z + 1 + step, Z), p]
        return remote(
            part, part, ring_ss.at[way, step, p], ring_rs.at[way, step, p],
            {"z": z_up if way == 0 else z_down},
        )

    def ring_has(way, step, p):
        return step < Z // 2 - 1 or p == way

    def ring_turn(step):
        for p in range(2):
            for way in range(2):
                if ring_has(way, step - 1, p):
                    ring_arrival(way, step - 1, p).wait_recv()
                if step < Z // 2 and ring_has(way, step, p):
                    ring(way, step, p).start()

    leads = lax.rem(s, 2) == 0

    def turn_block(plane):
        block = wrt[plane].reshape(LANES, D)
        for n in range(2 * Y):
            wts[1, plane, n * LANES : (n + 1) * LANES, :] = block[:, n * LANES : (n + 1) * LANES].T

    for p in range(2):
        @pl.when(is_me(z, owner_x, owner_y[p]))
        def _():
            own_copy.wait()

        @pl.when(jnp.logical_not(is_me(z, owner_x, owner_y[p])))
        def _():
            part = wrt.at[z, p]
            remote(
                part, part, wa_ss.at[0], wa_rs.at[p], {"x": owner_x, "y": owner_y[p]}
            ).wait_recv()

        @pl.when(leads)
        def _():
            for way in range(2):
                ring(way, 0, p).start()

    st_own.wait()
    for k in range(S - 1):
        st_arrival(k).wait_recv()
    owners = jnp.broadcast_to(column(owner_ref), (ROWS, LANES))

    def chosen(first):
        value = jnp.zeros((ROWS, LANES), F32)
        for owner in range(S):
            entry = st[owner, :, first : first + LANES].astype(F32)
            value = value + jnp.where(owners == float(owner), entry, 0.0)
        return value.astype(BF16)

    for half in range(2):
        for yy in range(Y):
            first = (half * Y + ORDER[yy]) * LANES
            hb[0, half, yy, y] = chosen(first)
            c_st[yy, half] = chosen(D + first)
    c_in[y] = c_st[y]

    def h0_copy(k):
        part = hb.at[0, :, :, y]
        return remote(part, part, h_ss.at[0, 0, k], h_rs.at[0, 0, k], {"y": up_y[k]})

    def h0_arrival(k):
        part = hb.at[0, :, :, down_y[k]]
        return remote(part, part, h_ss.at[0, 0, k], h_rs.at[0, 0, k], {"y": up_y[k]})

    def c0_copy(k):
        return remote(c_st.at[up_y[k]], c_in.at[y], c_ss.at[k], c_rs.at[k], {"y": up_y[k]})

    def c0_arrival(k):
        part = c_in.at[down_y[k]]
        return remote(part, part, c_ss.at[k], c_rs.at[k], {"y": up_y[k]})

    for k in range(Y - 1):
        h0_copy(k).start()
        c0_copy(k).start()

    turn_block(z)

    @pl.when(jnp.logical_not(leads))
    def _():
        pl.semaphore_wait(turn_sem, 1)
        for p in range(2):
            for way in range(2):
                ring(way, 0, p).start()

    ring_turn(1)
    turn_block(z_up)
    turn_block(z_down)
    for k in range(Y - 1):
        info_arrival(k).wait_recv()
        c0_arrival(k).wait_recv()
    marks_all = info[...].reshape(ALL_ROWS, LANES)
    for t in range(STEPS):
        alive_now = (marks_all[:, 0:1] <= float(t)) & (marks_all[:, 1:2] > float(t))
        live[t] = jnp.broadcast_to(jnp.where(alive_now, 1.0, 0.0), (ALL_ROWS, LANES)).reshape(
            PARTS, PART_ROWS, LANES
        )
    for half in range(2):
        for part in range(PARTS):
            cells[0, part, half] = (
                c_in[part * GROUPS : (part + 1) * GROUPS, half]
                .reshape(PART_ROWS, LANES)
                .astype(F32)
            )

    ring_turn(2)

    @pl.when(leads)
    def _():
        pl.semaphore_signal(turn_sem, inc=1, device_id={"s": up_s[0]}, device_id_type=MESH)

    turn_block(lax.rem(z + 2, Z))
    turn_block(lax.rem(z + Z - 2, Z))
    for gate in range(GATES):
        for half in range(2):
            win_copy(gate, half).wait()

    ring_turn(3)
    turn_block(lax.rem(z + 3, Z))
    turn_block(lax.rem(z + Z - 3, Z))

    @pl.when(s == 0)
    def _():
        for k in range(Y - 1):
            obs_arrival(k).wait_recv()

    @pl.when(s > 0)
    def _():
        @pl.loop(0, 2 * GATES)
        def _(block):
            for n in range(2 * Y):
                piece = wts[0, block, n * LANES : (n + 1) * LANES, :]
                wint[block, :, n * LANES : (n + 1) * LANES] = piece.T

    @pl.when(s == S - 1)
    def _():
        for k in range(Y - 1):
            cot_arrival(k).wait_recv()

    for k in range(Y - 1):
        h0_arrival(k).wait_recv()

    def hz_copy(t):
        return remote(hb.at[t], hb_pair.at[t], hz_ss.at[t], hz_rs.at[t], {"z": z_pair})

    def hz_arrival(t):
        return remote(hb_pair.at[t], hb_pair.at[t], hz_ss.at[t], hz_rs.at[t], {"z": z_pair})

    ring_turn(4)
    turn_block(lax.rem(z + Z // 2, Z))

    def whole(ref, *at):
        return jnp.concatenate(
            [
                ref[(*at, half, yy)].reshape(ALL_ROWS, LANES)
                for half in range(2)
                for yy in ORDER
            ],
            axis=1,
        )

    def groups(b):
        return pl.ds(b * GROUPS, GROUPS)

    def rows_of(kind, t, b):
        return jnp.concatenate(
            [
                act[kind, t, half, yy, groups(b)].reshape(PART_ROWS, LANES)
                for half in range(2)
                for yy in ORDER
            ],
            axis=1,
        )

    def h_copy(t, b, k):
        part = hb.at[t, :, y, groups(b)]
        return remote(part, part, h_ss.at[t, b, k], h_rs.at[t, b, k], {"y": up_y[k]})

    def h_arrival(t, b, k):
        part = hb.at[t, :, down_y[k], groups(b)]
        return remote(part, part, h_ss.at[t, b, k], h_rs.at[t, b, k], {"y": up_y[k]})

    def x_copy(t, b):
        return remote(
            hb.at[t + 1, :, :, groups(b)], xb.at[t, :, :, groups(b)],
            x_ss.at[t, b], x_rs.at[t, b], {"s": up_s[0]},
        )

    def x_arrival(t, b):
        part = xb.at[t, :, :, groups(b)]
        return remote(part, part, x_ss.at[t, b], x_rs.at[t, b], {"s": up_s[0]})

    def pass_up(t, b):
        for k in range(Y - 1):
            h_arrival(t + 1, b, k).wait_recv()

        @pl.when(s < S - 1)
        def _():
            x_copy(t, b).start()

        @pl.when((t < STEPS - 1) & (b == PARTS - 1))
        def _():
            hz_copy(t + 1).start()

        @pl.when((t == 0) & (b == PARTS - 1))
        def _():
            hz_copy(0).start()

    def product(kind, inputs, gate):
        weights = jnp.concatenate([wts[kind, 2 * gate], wts[kind, 2 * gate + 1]], axis=1)
        return nn_dot(inputs, weights)

    def first_product(kind, t, b):
        inputs = rows_of(kind, t, b)
        for gate in range(GATES):
            part = product(kind, inputs, gate)
            for half in range(2):
                first = pl.multiple_of(
                    gate * D + half * Y * LANES + own_block * LANES, LANES
                )
                acc[gate, half] = (
                    part[:, half * LANES : (half + 1) * LANES] + bias_ref[:, pl.ds(first, LANES)]
                )

    last_kind = jnp.where(s == 0, 1, 0)

    @pl.loop(0, STEPS * PARTS)
    def _(turn):
        t = turn // PARTS
        b = lax.rem(turn, PARTS)

        @pl.when(s == 0)
        def _():
            first_product(0, t, b)

        @pl.when(t > 0)
        def _():
            pass_up(t - 1, b)

        @pl.when(s > 0)
        def _():
            first_product(1, t, b)
            x_arrival(t, b).wait_recv()

        inputs = rows_of(last_kind, t, b)
        for gate in range(GATES):
            part = product(last_kind, inputs, gate)
            for half in range(2):
                pre = acc[gate, half] + part[:, half * LANES : (half + 1) * LANES]
                gates[t, b, gate, half] = jnp.tanh(pre) if gate == 2 else sigmoid(pre)
        for half in range(2):
            cell = (
                gates[t, b, 1, half] * cells[t, b, half]
                + gates[t, b, 0, half] * gates[t, b, 2, half]
            )
            cells[t + 1, b, half] = cell
            hidden = (gates[t, b, 3, half] * jnp.tanh(cell)).astype(BF16)
            hb[t + 1, half, y, groups(b)] = hidden.reshape(GROUPS, ROWS, LANES)
        for k in range(Y - 1):
            h_copy(t + 1, b, k).start()

    for part in range(PARTS):
        pass_up(STEPS - 1, part)

    def keep_hidden():
        for t in range(STEPS):
            for half in range(2):
                for yy in range(Y):
                    first = (half * Y + ORDER[yy]) * LANES
                    hid_out[t, :, first : first + LANES] = hb[t + 1, half, yy, y]
        for t in range(STEPS):
            hz_arrival(t).wait_recv()
            hmat[t * ALL_ROWS : (t + 1) * ALL_ROWS, :] = whole(hb, t)
            hmat_pair[t * ALL_ROWS : (t + 1) * ALL_ROWS, :] = whole(hb_pair, t)

    carry[...] = jnp.zeros_like(carry)

    def gz_copy(t):
        return remote(
            grads_t.at[t, z_other], grads_pair.at[t], gz_ss.at[t], gz_rs.at[t], {"z": z_pair}
        )

    def gz_arrival(t):
        part = grads_pair.at[t]
        return remote(part, part, gz_ss.at[t], gz_rs.at[t], {"z": z_pair})

    def a_copy(t, b, k):
        return remote(
            a_send.at[t, b, up_y[k]], a_recv.at[t, b, y], a_ss.at[t, b, k], a_rs.at[t, b, k],
            {"y": up_y[k]},
        )

    def a_arrival(t, b, k):
        part = a_recv.at[t, b, down_y[k]]
        return remote(part, part, a_ss.at[t, b, k], a_rs.at[t, b, k], {"y": up_y[k]})

    def g_copy(t, b, k):
        return remote(
            g_send.at[t, b, up_y[k]], g_recv.at[t, b, y], g_ss.at[t, b, k], g_rs.at[t, b, k],
            {"y": up_y[k]},
        )

    def g_arrival(t, b, k):
        part = g_recv.at[t, b, down_y[k]]
        return remote(part, part, g_ss.at[t, b, k], g_rs.at[t, b, k], {"y": up_y[k]})

    def e_copy(t, b):
        return remote(
            e_send.at[t, b], eb.at[t, :, groups(b)], e_ss.at[t, b], e_rs.at[t, b],
            {"s": down_s[0]},
        )

    def e_arrival(t, b):
        part = eb.at[t, :, groups(b)]
        return remote(part, part, e_ss.at[t, b], e_rs.at[t, b], {"s": down_s[0]})

    def total(sent, received, t, b, half):
        value = sent[t, b, y, half].astype(F32)
        for k in range(Y - 1):
            value = value + received[t, b, down_y[k], half].astype(F32)
        return value

    def hand_down(t, b):
        for k in range(Y - 1):
            g_arrival(t, b, k).wait_recv()
        for half in range(2):
            e_send[t, b, half] = (
                total(g_send, g_recv, t, b, half).astype(BF16).reshape(GROUPS, ROWS, LANES)
            )
        e_copy(t, b).start()

    def spread(sent, t, b, gate_grads, weights):
        for j in range(4):
            columns = slice(j * 2 * LANES, (j + 1) * 2 * LANES)
            part = nn_dot(gate_grads, weights(columns)).astype(BF16)
            for n in range(2):
                block = 2 * j + n
                sent[t, b, ORDER[block % Y], block // Y] = part[:, n * LANES : (n + 1) * LANES]

    @pl.loop(0, STEPS * PARTS)
    def _(turn):
        back = turn // PARTS
        b = lax.rem(turn, PARTS)
        t = STEPS - 1 - back

        @pl.when(s < S - 1)
        def _():
            e_arrival(t, b).wait_recv()

        for half in range(2):
            acc[0, half] = eb[t, half, groups(b)].reshape(PART_ROWS, LANES).astype(F32)

        @pl.when(back > 0)
        def _():
            for k in range(Y - 1):
                a_arrival(t + 1, b, k).wait_recv()
            for half in range(2):
                acc[0, half] = acc[0, half] + total(a_send, a_recv, t + 1, b, half)

        for half in range(2):
            in_gate = gates[t, b, 0, half]
            forget = gates[t, b, 1, half]
            candidate = gates[t, b, 2, half]
            out_gate = gates[t, b, 3, half]
            alive = live[t, b]
            total_h = acc[0, half]
            squashed = jnp.tanh(cells[t + 1, b, half])
            total_c = carry[b, half] + total_h * out_gate * (1.0 - squashed * squashed)
            parts = (
                total_c * candidate * in_gate * (1.0 - in_gate) * alive,
                total_c * cells[t, b, half] * forget * (1.0 - forget) * alive,
                total_c * in_gate * (1.0 - candidate * candidate) * alive,
                total_h * squashed * out_gate * (1.0 - out_gate) * alive,
            )
            carry[b, half] = total_c * forget * alive
            for gate in range(GATES):
                grads[b, 2 * gate + half] = parts[gate].astype(BF16)

        gate_grads = jnp.concatenate([grads[b, block] for block in range(2 * GATES)], axis=1)

        @pl.when(t > 0)
        def _():
            spread(
                a_send, t, b, gate_grads,
                lambda columns: wrt[:, :, :, columns].reshape(LOCAL, 2 * LANES),
            )
            for k in range(Y - 1):
                a_copy(t, b, k).start()

        @pl.when(s > 0)
        def _():
            spread(
                g_send, t, b, gate_grads,
                lambda columns: wint[:, :, columns].reshape(LOCAL, 2 * LANES),
            )
            for k in range(Y - 1):
                g_copy(t, b, k).start()

        @pl.when(b == PARTS - 1)
        def _():
            for gate in range(GATES):
                for half in range(2):
                    block = jnp.concatenate(
                        [grads[part, 2 * gate + half] for part in range(PARTS)], axis=0
                    )
                    grads_t[t, half, gate] = block.T
            gz_copy(t).start()

            @pl.when(s > 0)
            def _():
                for part in range(PARTS):
                    hand_down(t, part)

            @pl.when(back == 0)
            def _():
                keep_hidden()

    def dw_copy(k, p):
        return remote(
            dw_send.at[far[k], p], dw_recv.at[quad, p], dw_ss.at[k, p], dw_rs.at[k, p],
            {"z": 2 * far[k] + z_half},
        )

    def dw_arrival(k, p):
        part = dw_recv.at[near[k], p]
        return remote(part, part, dw_ss.at[k, p], dw_rs.at[k, p], {"z": 2 * far[k] + z_half})

    def db_copy(k):
        return remote(
            db_send.at[far[k]], db_recv.at[quad], db_ss.at[k], db_rs.at[k],
            {"z": 2 * far[k] + z_half},
        )

    def db_arrival(k):
        part = db_recv.at[near[k]]
        return remote(part, part, db_ss.at[k], db_rs.at[k], {"z": 2 * far[k] + z_half})

    for t in range(1, STEPS):
        gz_arrival(t).wait_recv()

    @pl.loop(0, GATES)
    def _(gate):
        rows = jnp.concatenate([grads_t[t, z_half, gate] for t in range(STEPS)], axis=1)
        rows_pair = jnp.concatenate([grads_pair[t, gate] for t in range(1, STEPS)], axis=1)
        for j in range(4):
            columns = slice(j * 2 * LANES, (j + 1) * 2 * LANES)
            dw_acc[gate, :, columns] = nn_dot(rows, hmat[:, columns]) + nn_dot(
                rows_pair, hmat_pair[ALL_ROWS:, columns]
            )
        db_send[gate] = nt_dot(jnp.ones((8, STEPS * ALL_ROWS), BF16), rows) + nt_dot(
            jnp.ones((8, (STEPS - 1) * ALL_ROWS), BF16), rows_pair
        )

    gz_arrival(0).wait_recv()
    for k in range(QUADS):
        gate = far[k] if k < QUADS - 1 else quad
        rows_pair = grads_pair[0, gate]
        db_send[gate] = db_send[gate] + nt_dot(jnp.ones((8, ALL_ROWS), BF16), rows_pair)
        for j in range(4):
            columns = slice(j * 2 * LANES, (j + 1) * 2 * LANES)
            part = dw_acc[gate, :, columns] + nn_dot(rows_pair, hmat_pair[:ALL_ROWS, columns])
            if k < QUADS - 1:
                for p in range(2):
                    rows = slice(p * LANES // 2, (p + 1) * LANES // 2)
                    dw_send[gate, p, :, columns] = part[rows].astype(BF16)
            else:
                dw_acc[gate, :, columns] = part
        if k < QUADS - 1:
            db_copy(k).start()
            dw_copy(k, 0).start()
    for k in range(QUADS - 1):
        dw_copy(k, 1).start()

    def dw2_copy(p):
        return remote(
            dw2_send.at[p], dw2_recv.at[x], dw2_ss.at[p], dw2_rs.at[x],
            {"x": owner_x, "y": owner_y[p]},
        )

    def db2_copy(p):
        return remote(
            db2_send, db2_recv.at[x], db2_ss.at[p], db2_rs.at[x],
            {"x": owner_x, "y": owner_y[p]},
        )

    for k in range(QUADS - 1):
        db_arrival(k).wait_recv()
    db2_send[...] = db_send[quad] + db_recv[near[0]] + db_recv[near[1]] + db_recv[near[2]]
    for p in range(2):
        rows = slice(p * LANES // 2, (p + 1) * LANES // 2)
        for k in range(QUADS - 1):
            dw_arrival(k, p).wait_recv()
        value = dw_acc[quad, rows, :]
        for k in range(QUADS - 1):
            value = value + dw_recv[near[k], p].astype(F32)
        dw2_send[p] = value.astype(BF16)

        @pl.when(is_me(z, owner_x, owner_y[p]))
        def _():
            dw2_recv[x] = dw2_send[p]
            db2_recv[x] = db2_send[...]

        @pl.when(jnp.logical_not(is_me(z, owner_x, owner_y[p])))
        def _():
            db2_copy(p).start()
            dw2_copy(p).start()

    for xx in range(X):
        @pl.when(jnp.logical_not(is_me(z, xx, user_y)))
        def _():
            where = {"x": xx, "y": user_y}
            dw_part = dw2_recv.at[xx]
            db_part = db2_recv.at[xx]
            remote(db_part, db_part, db2_ss.at[0], db2_rs.at[xx], where).wait_recv()
            remote(dw_part, dw_part, dw2_ss.at[0], dw2_rs.at[xx], where).wait_recv()

    dw_out[...] = dw2_recv[0].astype(F32) + dw2_recv[1].astype(F32)
    bias_sum = db2_recv[0, 0:1, :] + db2_recv[1, 0:1, :]
    db_out[...] = jnp.where(own_half == 0, bias_sum[:, : LANES // 2], bias_sum[:, LANES // 2 :])

    for xx in range(X):
        @pl.when(jnp.logical_not(is_me(z, xx, user_y)))
        def _():
            first_hop(xx).wait_send()

    for k in range(S - 1):
        st_copy(k).wait_send()
    for step in range(Z // 2):
        for p in range(2):
            for way in range(2):
                if ring_has(way, step, p):
                    ring(way, step, p).wait_send()
    for k in range(Y - 1):
        info_copy(k).wait_send()
        h0_copy(k).wait_send()
        c0_copy(k).wait_send()

    @pl.when(s == 0)
    def _():
        for k in range(Y - 1):
            obs_copy(k).wait_send()

    @pl.when(s == S - 1)
    def _():
        for k in range(Y - 1):
            cot_copy(k).wait_send()

    @pl.loop(0, STEPS)
    def _(t):
        hz_copy(t).wait_send()
        gz_copy(t).wait_send()
        for b in range(PARTS):
            for k in range(Y - 1):
                h_copy(t + 1, b, k).wait_send()

            @pl.when(s < S - 1)
            def _():
                x_copy(t, b).wait_send()

            @pl.when(t > 0)
            def _():
                for k in range(Y - 1):
                    a_copy(t, b, k).wait_send()

            @pl.when(s > 0)
            def _():
                for k in range(Y - 1):
                    g_copy(t, b, k).wait_send()
                e_copy(t, b).wait_send()

    for k in range(QUADS - 1):
        for p in range(2):
            dw_copy(k, p).wait_send()
        db_copy(k).wait_send()
    for p in range(2):
        @pl.when(jnp.logical_not(is_me(z, owner_x, owner_y[p])))
        def _():
            dw2_copy(p).wait_send()
            db2_copy(p).wait_send()


def on_device(
    obs_features, w_input, w_recurrent, bias, stored_states, state_owner, burn_steps, valid_steps, cotangent
):
    vmem = pl.BlockSpec(memory_space=pltpu.VMEM)
    hbm = pl.BlockSpec(memory_space=pl.ANY)
    dma = pltpu.SemaphoreType.DMA
    piece = (Y, ROWS, LANES)
    hidden, weights, biases = pl.pallas_call(
        kernel,
        out_shape=(
            pltpu.VMEM((STEPS, ROWS, D), BF16),
            pltpu.VMEM((LANES // 2, D), F32),
            pltpu.VMEM((1, LANES // 2), F32),
        ),
        in_specs=[hbm, hbm, hbm, hbm, vmem, hbm, vmem, vmem, vmem],
        out_specs=(vmem, vmem, vmem),
        scratch_shapes=[
            pltpu.VMEM((STEPS, ROWS, D), BF16),
            pltpu.VMEM((STEPS, ROWS, D), BF16),
            pltpu.VMEM((Y, ROWS, LANES), F32),
            pltpu.VMEM((S, ROWS, 2 * D), BF16),
            pltpu.VMEM((2, Z, D, LANES), BF16),
            pltpu.VMEM((Z, 2, LANES // 2, D), BF16),
            pltpu.VMEM((2 * GATES, LANES, D), BF16),
            pltpu.VMEM((2, STEPS + 1, 2, Y, *piece), BF16),
            pltpu.VMEM((STEPS, 2, Y, *piece), BF16),
            pltpu.VMEM((STEPS, 2, *piece), BF16),
            pltpu.VMEM((Y, STEPS, 2, ROWS, LANES), BF16),
            pltpu.VMEM((Y, 2, ROWS, LANES), BF16),
            pltpu.VMEM((Y, 2, ROWS, LANES), BF16),
            pltpu.VMEM((STEPS + 1, PARTS, 2, PART_ROWS, LANES), F32),
            pltpu.VMEM((STEPS, PARTS, GATES, 2, PART_ROWS, LANES), F32),
            pltpu.VMEM((GATES, 2, PART_ROWS, LANES), F32),
            pltpu.VMEM((STEPS, PARTS, PART_ROWS, LANES), F32),
            pltpu.VMEM((PARTS, 2 * GATES, PART_ROWS, LANES), BF16),
            pltpu.VMEM((STEPS, 2, GATES, LANES, ALL_ROWS), BF16),
            pltpu.VMEM((STEPS, GATES, LANES, ALL_ROWS), BF16),
            pltpu.VMEM((PARTS, 2, PART_ROWS, LANES), F32),
            pltpu.VMEM((STEPS, PARTS, Y, 2, PART_ROWS, LANES), BF16),
            pltpu.VMEM((STEPS, PARTS, Y, 2, PART_ROWS, LANES), BF16),
            pltpu.VMEM((STEPS, PARTS, Y, 2, PART_ROWS, LANES), BF16),
            pltpu.VMEM((STEPS, PARTS, Y, 2, PART_ROWS, LANES), BF16),
            pltpu.VMEM((STEPS, PARTS, 2, GROUPS, ROWS, LANES), BF16),
            pltpu.VMEM((STEPS * ALL_ROWS, D), BF16),
            pltpu.VMEM((STEPS * ALL_ROWS, D), BF16),
            pltpu.VMEM((GATES, LANES, D), F32),
            pltpu.VMEM((GATES, 2, LANES // 2, D), BF16),
            pltpu.VMEM((GATES, 2, LANES // 2, D), BF16),
            pltpu.VMEM((GATES, 8, LANES), F32),
            pltpu.VMEM((GATES, 8, LANES), F32),
            pltpu.VMEM((2, LANES // 2, D), BF16),
            pltpu.VMEM((X, LANES // 2, D), BF16),
            pltpu.VMEM((8, LANES), F32),
            pltpu.VMEM((X, 8, LANES), F32),
            dma((2,)),
            dma((Y - 1,)), dma((Y - 1,)),
            dma((S - 1,)), dma((S - 1,)), dma,
            dma((X,)), dma((2,)), dma,
            dma((2, Z // 2, 2)), dma((2, Z // 2, 2)),
            dma((2 * GATES,)),
            dma((Y - 1,)), dma((Y - 1,)),
            dma((Y - 1,)), dma((Y - 1,)),
            dma((Y - 1,)), dma((Y - 1,)),
            dma((STEPS + 1, PARTS, Y - 1)), dma((STEPS + 1, PARTS, Y - 1)),
            dma((STEPS, PARTS)), dma((STEPS, PARTS)),
            dma((STEPS,)), dma((STEPS,)),
            dma((STEPS,)), dma((STEPS,)),
            dma((STEPS, PARTS, Y - 1)), dma((STEPS, PARTS, Y - 1)),
            dma((STEPS, PARTS, Y - 1)), dma((STEPS, PARTS, Y - 1)),
            dma((STEPS, PARTS)), dma((STEPS, PARTS)),
            dma((3, 2)), dma((3, 2)),
            dma((3,)), dma((3,)),
            dma((2,)), dma((X,)),
            dma((2,)), dma((X,)),
            pltpu.SemaphoreType.REGULAR,
        ],
        compiler_params=pltpu.CompilerParams(
            collective_id=0, has_side_effects=True, vmem_limit_bytes=56 * 1024 * 1024
        ),
        name="replay_window",
    )(
        obs_features, cotangent, w_input[0], w_recurrent[0].T, bias, stored_states[0],
        state_owner[None], burn_steps[None], valid_steps[None],
    )
    return hidden[None], weights.T[None], biases


def solution(mesh):
    axes = ("s", "z", "x", "y")
    grid = Mesh(mesh.devices.reshape(S, Z, X, Y), axes)
    dp = ("z", "x", "y")
    return jax.shard_map(
        on_device,
        mesh=grid,
        in_specs=(
            P(None, dp, None),
            P("s", None, None),
            P("s", None, dp),
            P("s", None),
            P("s", None, dp, None),
            P(dp),
            P(dp),
            P(dp),
            P(None, dp, None),
        ),
        out_specs=(P("s", None, dp, None), P("s", None, dp), P("s", dp)),
        check_vma=False,
    )
```

```python
import jax
import jax.numpy as jnp
from jax import lax
from jax.experimental import pallas as pl
from jax.experimental.pallas import tpu as pltpu
from jax.sharding import Mesh
from jax.sharding import PartitionSpec as P

S, Z, X, Y = 4, 8, 2, 4
STEPS = 4
ROWS = 32
D = 1024
LANES = 128
ORDER = (0, 2, 1, 3)
GATES = 4
ALL_ROWS = Y * ROWS
PARTS = 4
GROUPS = Y // PARTS
PART_ROWS = ALL_ROWS // PARTS
LOCAL = GATES * 2 * LANES
MESH = pl.DeviceIdType.MESH
BF16 = jnp.bfloat16
F32 = jnp.float32


def sigmoid(v):
    return 0.5 * jnp.tanh(0.5 * v) + 0.5


def nt_dot(a, b):
    return lax.dot_general(a, b, (((1,), (1,)), ((), ())), preferred_element_type=F32)


def nn_dot(a, b):
    return jnp.dot(a, b, preferred_element_type=F32)


def remote(src, dst, send_sem, recv_sem, where):
    return pltpu.make_async_remote_copy(
        src_ref=src,
        dst_ref=dst,
        send_sem=send_sem,
        recv_sem=recv_sem,
        device_id=where,
        device_id_type=MESH,
    )


def kernel(
    obs_hbm, cot_hbm, win_hbm, wrt_hbm, bias_ref, st_hbm, owner_ref, burn_ref, valid_ref,
    hid_out, dw_out, db_out,
    obs_st, cot_in, info, st, wts, wrt, wint, act, hb_pair, eb, cot_st, c_st, c_in, cells, gates, acc, live,
    grads, grads_t, grads_pair, carry, a_send, a_recv, g_send, g_recv, e_send, hmat, hmat_pair,
    dw_acc, dw_send, dw_relay, dw_joint, dw_recv, db_send, db_recv, dw2_send, dw2_recv, db2_send, db2_recv,
    in_ls, info_ss, info_rs, st_ss, st_rs, st_ls, wa_ss, wa_rs, wa_ls, ring_ss, ring_rs, win_ls,
    obs_ss, obs_rs, cot_ss, cot_rs, c_ss, c_rs, h_ss, h_rs, x_ss, x_rs, hz_ss, hz_rs, gz_ss, gz_rs,
    a_ss, a_rs, g_ss, g_rs, e_ss, e_rs, dw_ss, dw_rs, db_ss, db_rs,
    dw2_ss, dw2_rs, db2_ss, db2_rs, turn_sem,
):
    xb, hb = act.at[0], act.at[1]
    s = lax.axis_index("s")
    z = lax.axis_index("z")
    x = lax.axis_index("x")
    y = lax.axis_index("y")
    up_y = [lax.rem(y + k, Y) for k in range(1, Y)]
    down_y = [lax.rem(y + Y - k, Y) for k in range(1, Y)]
    up_s = [lax.rem(s + k, S) for k in range(1, S)]
    down_s = [lax.rem(s + S - k, S) for k in range(1, S)]
    z_up, z_down = lax.rem(z + 1, Z), lax.rem(z + Z - 1, Z)
    z_half = lax.rem(z, 2)
    z_other = 1 - z_half
    z_pair = z + 1 - 2 * z_half
    quad = z // 2
    QUADS = Z // 2
    far = [lax.rem(quad + k, QUADS) for k in (2, 1, 3)]
    near = [lax.rem(quad + QUADS - k, QUADS) for k in (2, 1, 3)]
    own_half = lax.rem(y, 2)
    user_y = 2 * (y // 2) + x
    owner_x = own_half
    owner_y = [2 * (y // 2) + p for p in range(2)]
    own_block = 2 * own_half + y // 2

    def is_me(zz, xx, yy):
        return (zz == z) & (xx == x) & (yy == y)

    barrier = pltpu.get_barrier_semaphore()

    def greet(where):
        pl.semaphore_signal(barrier, inc=1, device_id=where, device_id_type=MESH)

    for k in range(Y - 1):
        greet({"y": down_y[k]})
    for k in range(S - 1):
        greet({"s": down_s[k]})
    greet({"z": z_up})
    greet({"z": z_down})
    for k in range(QUADS - 1):
        greet({"z": 2 * near[k] + z_half})
    for p in range(2):
        @pl.when(jnp.logical_not(is_me(z, owner_x, owner_y[p])))
        def _():
            greet({"x": owner_x, "y": owner_y[p]})

    for xx in range(X):
        @pl.when(jnp.logical_not(is_me(z, xx, user_y)))
        def _():
            greet({"x": xx, "y": user_y})

    mine = is_me(z, owner_x, owner_y[0]) | is_me(z, owner_x, owner_y[1])
    base = (Y - 1) + (S - 1) + 2 + (QUADS - 1) + X + 2
    obs_copy_in = pltpu.make_async_copy(obs_hbm, obs_st, in_ls.at[0])
    cot_copy_in = pltpu.make_async_copy(cot_hbm, cot_in, in_ls.at[1])

    @pl.when(s == 0)
    def _():
        obs_copy_in.start()

    @pl.when(s == S - 1)
    def _():
        cot_copy_in.start()

    pl.semaphore_wait(barrier, jnp.where(mine, base - 2, base))

    def first_hop(xx):
        return remote(
            wrt_hbm, wrt.at[z, own_half], wa_ss.at[xx], wa_rs.at[own_half],
            {"x": xx, "y": user_y},
        )

    own_copy = pltpu.make_async_copy(wrt_hbm, wrt.at[z, own_half], wa_ls)
    for xx in range(X):
        @pl.when(is_me(z, xx, user_y))
        def _():
            own_copy.start()

        @pl.when(jnp.logical_not(is_me(z, xx, user_y)))
        def _():
            first_hop(xx).start()

    def st_copy(k):
        return remote(st_hbm.at[up_s[k]], st.at[s], st_ss.at[k], st_rs.at[k], {"s": up_s[k]})

    def st_arrival(k):
        return remote(
            st.at[down_s[k]], st.at[down_s[k]], st_ss.at[k], st_rs.at[k], {"s": up_s[k]}
        )

    for k in range(S - 1):
        st_copy(k).start()
    st_own = pltpu.make_async_copy(st_hbm.at[s], st.at[s], st_ls)
    st_own.start()

    def win_copy(gate, half):
        first = pl.multiple_of(gate * D + half * Y * LANES + own_block * LANES, LANES)
        block = gate * 2 + half
        return pltpu.make_async_copy(
            win_hbm.at[:, pl.ds(first, LANES)],
            wts.at[0, block],
            win_ls.at[block],
        )

    for gate in range(GATES):
        for half in range(2):
            win_copy(gate, half).start()

    def column(row_ref):
        row = jnp.broadcast_to(row_ref[...].astype(F32), (ROWS, ROWS))
        down = lax.broadcasted_iota(jnp.int32, (ROWS, ROWS), 0)
        across = lax.broadcasted_iota(jnp.int32, (ROWS, ROWS), 1)
        return jnp.sum(jnp.where(down == across, row, 0.0), axis=1, keepdims=True)

    lane = lax.broadcasted_iota(jnp.int32, (ROWS, LANES), 1)
    info[y] = jnp.where(lane == 0, column(burn_ref), column(valid_ref))

    def info_copy(k):
        return remote(info.at[y], info.at[y], info_ss.at[k], info_rs.at[k], {"y": up_y[k]})

    def info_arrival(k):
        return remote(
            info.at[down_y[k]], info.at[down_y[k]], info_ss.at[k], info_rs.at[k], {"y": up_y[k]}
        )

    for k in range(Y - 1):
        info_copy(k).start()

    def obs_copy(k):
        return remote(
            xb.at[:, :, :, y], xb.at[:, :, :, y], obs_ss.at[k], obs_rs.at[k], {"y": up_y[k]}
        )

    def obs_arrival(k):
        part = xb.at[:, :, :, down_y[k]]
        return remote(part, part, obs_ss.at[k], obs_rs.at[k], {"y": up_y[k]})

    @pl.when(s == 0)
    def _():
        obs_copy_in.wait()
        for t in range(STEPS):
            for half in range(2):
                for yy in range(Y):
                    first = (half * Y + ORDER[yy]) * LANES
                    xb[t, half, yy, y] = obs_st[t, :, first : first + LANES]
        for k in range(Y - 1):
            obs_copy(k).start()

    def cot_copy(k):
        return remote(
            cot_st.at[up_y[k]], eb.at[:, :, y], cot_ss.at[k], cot_rs.at[k], {"y": up_y[k]}
        )

    def cot_arrival(k):
        part = eb.at[:, :, down_y[k]]
        return remote(part, part, cot_ss.at[k], cot_rs.at[k], {"y": up_y[k]})

    @pl.when(s == S - 1)
    def _():
        cot_copy_in.wait()
        for t in range(STEPS):
            for half in range(2):
                for yy in range(Y):
                    first = (half * Y + ORDER[yy]) * LANES
                    cot_st[yy, t, half] = cot_in[t, :, first : first + LANES]
        for t in range(STEPS):
            for half in range(2):
                eb[t, half, y] = cot_st[y, t, half]
        for k in range(Y - 1):
            cot_copy(k).start()

    def ring(way, step, p):
        part = wrt.at[lax.rem(z + Z - step, Z) if way == 0 else lax.rem(z + step, Z), p]
        return remote(
            part, part, ring_ss.at[way, step, p], ring_rs.at[way, step, p],
            {"z": z_up if way == 0 else z_down},
        )

    def ring_arrival(way, step, p):
        part = wrt.at[lax.rem(z + Z - 1 - step, Z) if way == 0 else lax.rem(z + 1 + step, Z), p]
        return remote(
            part, part, ring_ss.at[way, step, p], ring_rs.at[way, step, p],
            {"z": z_up if way == 0 else z_down},
        )

    def ring_has(way, step, p):
        return step < Z // 2 - 1 or p == way

    def ring_turn(step):
        for p in range(2):
            for way in range(2):
                if ring_has(way, step - 1, p):
                    ring_arrival(way, step - 1, p).wait_recv()
                if step < Z // 2 and ring_has(way, step, p):
                    ring(way, step, p).start()

    leads = lax.rem(s, 2) == 0

    def turn_block(plane):
        block = wrt[plane].reshape(LANES, D)
        for n in range(2 * Y):
            wts[1, plane, n * LANES : (n + 1) * LANES, :] = block[:, n * LANES : (n + 1) * LANES].T

    for p in range(2):
        @pl.when(is_me(z, owner_x, owner_y[p]))
        def _():
            own_copy.wait()

        @pl.when(jnp.logical_not(is_me(z, owner_x, owner_y[p])))
        def _():
            part = wrt.at[z, p]
            remote(
                part, part, wa_ss.at[0], wa_rs.at[p], {"x": owner_x, "y": owner_y[p]}
            ).wait_recv()

        @pl.when(leads)
        def _():
            for way in range(2):
                ring(way, 0, p).start()

    st_own.wait()
    for k in range(S - 1):
        st_arrival(k).wait_recv()
    owners = jnp.broadcast_to(column(owner_ref), (ROWS, LANES))

    def chosen(first):
        value = jnp.zeros((ROWS, LANES), F32)
        for owner in range(S):
            entry = st[owner, :, first : first + LANES].astype(F32)
            value = value + jnp.where(owners == float(owner), entry, 0.0)
        return value.astype(BF16)

    for half in range(2):
        for yy in range(Y):
            first = (half * Y + ORDER[yy]) * LANES
            hb[0, half, yy, y] = chosen(first)
            c_st[yy, half] = chosen(D + first)
    c_in[y] = c_st[y]

    def h0_copy(k):
        part = hb.at[0, :, :, y]
        return remote(part, part, h_ss.at[0, 0, k], h_rs.at[0, 0, k], {"y": up_y[k]})

    def h0_arrival(k):
        part = hb.at[0, :, :, down_y[k]]
        return remote(part, part, h_ss.at[0, 0, k], h_rs.at[0, 0, k], {"y": up_y[k]})

    def c0_copy(k):
        return remote(c_st.at[up_y[k]], c_in.at[y], c_ss.at[k], c_rs.at[k], {"y": up_y[k]})

    def c0_arrival(k):
        part = c_in.at[down_y[k]]
        return remote(part, part, c_ss.at[k], c_rs.at[k], {"y": up_y[k]})

    for k in range(Y - 1):
        h0_copy(k).start()
        c0_copy(k).start()

    turn_block(z)

    @pl.when(jnp.logical_not(leads))
    def _():
        pl.semaphore_wait(turn_sem, 1)
        for p in range(2):
            for way in range(2):
                ring(way, 0, p).start()

    ring_turn(1)
    turn_block(z_up)
    turn_block(z_down)
    for k in range(Y - 1):
        info_arrival(k).wait_recv()
        c0_arrival(k).wait_recv()
    marks_all = info[...].reshape(ALL_ROWS, LANES)
    for t in range(STEPS):
        alive_now = (marks_all[:, 0:1] <= float(t)) & (marks_all[:, 1:2] > float(t))
        live[t] = jnp.broadcast_to(jnp.where(alive_now, 1.0, 0.0), (ALL_ROWS, LANES)).reshape(
            PARTS, PART_ROWS, LANES
        )
    for half in range(2):
        for part in range(PARTS):
            cells[0, part, half] = (
                c_in[part * GROUPS : (part + 1) * GROUPS, half]
                .reshape(PART_ROWS, LANES)
                .astype(F32)
            )

    ring_turn(2)

    @pl.when(leads)
    def _():
        pl.semaphore_signal(turn_sem, inc=1, device_id={"s": up_s[0]}, device_id_type=MESH)

    turn_block(lax.rem(z + 2, Z))
    turn_block(lax.rem(z + Z - 2, Z))
    for gate in range(GATES):
        for half in range(2):
            win_copy(gate, half).wait()

    ring_turn(3)
    turn_block(lax.rem(z + 3, Z))
    turn_block(lax.rem(z + Z - 3, Z))

    @pl.when(s == 0)
    def _():
        for k in range(Y - 1):
            obs_arrival(k).wait_recv()

    @pl.when(s > 0)
    def _():
        @pl.loop(0, 2 * GATES)
        def _(block):
            for n in range(2 * Y):
                piece = wts[0, block, n * LANES : (n + 1) * LANES, :]
                wint[block, :, n * LANES : (n + 1) * LANES] = piece.T

    @pl.when(s == S - 1)
    def _():
        for k in range(Y - 1):
            cot_arrival(k).wait_recv()

    for k in range(Y - 1):
        h0_arrival(k).wait_recv()

    def hz_copy(t):
        return remote(hb.at[t], hb_pair.at[t], hz_ss.at[t], hz_rs.at[t], {"z": z_pair})

    def hz_arrival(t):
        return remote(hb_pair.at[t], hb_pair.at[t], hz_ss.at[t], hz_rs.at[t], {"z": z_pair})

    ring_turn(4)
    turn_block(lax.rem(z + Z // 2, Z))

    def whole(ref, *at):
        return jnp.concatenate(
            [
                ref[(*at, half, yy)].reshape(ALL_ROWS, LANES)
                for half in range(2)
                for yy in ORDER
            ],
            axis=1,
        )

    def groups(b):
        return pl.ds(b * GROUPS, GROUPS)

    def rows_of(kind, t, b):
        return jnp.concatenate(
            [
                act[kind, t, half, yy, groups(b)].reshape(PART_ROWS, LANES)
                for half in range(2)
                for yy in ORDER
            ],
            axis=1,
        )

    def h_copy(t, b, k):
        part = hb.at[t, :, y, groups(b)]
        return remote(part, part, h_ss.at[t, b, k], h_rs.at[t, b, k], {"y": up_y[k]})

    def h_arrival(t, b, k):
        part = hb.at[t, :, down_y[k], groups(b)]
        return remote(part, part, h_ss.at[t, b, k], h_rs.at[t, b, k], {"y": up_y[k]})

    def x_copy(t, b):
        return remote(
            hb.at[t + 1, :, :, groups(b)], xb.at[t, :, :, groups(b)],
            x_ss.at[t, b], x_rs.at[t, b], {"s": up_s[0]},
        )

    def x_arrival(t, b):
        part = xb.at[t, :, :, groups(b)]
        return remote(part, part, x_ss.at[t, b], x_rs.at[t, b], {"s": up_s[0]})

    def pass_up(t, b):
        for k in range(Y - 1):
            h_arrival(t + 1, b, k).wait_recv()

        @pl.when(s < S - 1)
        def _():
            x_copy(t, b).start()

        @pl.when((t < STEPS - 1) & (b == PARTS - 1))
        def _():
            hz_copy(t + 1).start()

        @pl.when((t == 0) & (b == PARTS - 1))
        def _():
            hz_copy(0).start()

    def product(kind, inputs, gate):
        weights = jnp.concatenate([wts[kind, 2 * gate], wts[kind, 2 * gate + 1]], axis=1)
        return nn_dot(inputs, weights)

    def first_product(kind, t, b):
        inputs = rows_of(kind, t, b)
        for gate in range(GATES):
            part = product(kind, inputs, gate)
            for half in range(2):
                first = pl.multiple_of(
                    gate * D + half * Y * LANES + own_block * LANES, LANES
                )
                acc[gate, half] = (
                    part[:, half * LANES : (half + 1) * LANES] + bias_ref[:, pl.ds(first, LANES)]
                )

    last_kind = jnp.where(s == 0, 1, 0)

    @pl.loop(0, STEPS * PARTS)
    def _(turn):
        t = turn // PARTS
        b = lax.rem(turn, PARTS)

        @pl.when(s == 0)
        def _():
            first_product(0, t, b)

        @pl.when(t > 0)
        def _():
            pass_up(t - 1, b)

        @pl.when(s > 0)
        def _():
            first_product(1, t, b)
            x_arrival(t, b).wait_recv()

        inputs = rows_of(last_kind, t, b)
        for gate in range(GATES):
            part = product(last_kind, inputs, gate)
            for half in range(2):
                pre = acc[gate, half] + part[:, half * LANES : (half + 1) * LANES]
                gates[t, b, gate, half] = jnp.tanh(pre) if gate == 2 else sigmoid(pre)
        for half in range(2):
            cell = (
                gates[t, b, 1, half] * cells[t, b, half]
                + gates[t, b, 0, half] * gates[t, b, 2, half]
            )
            cells[t + 1, b, half] = cell
            hidden = (gates[t, b, 3, half] * jnp.tanh(cell)).astype(BF16)
            hb[t + 1, half, y, groups(b)] = hidden.reshape(GROUPS, ROWS, LANES)
        for k in range(Y - 1):
            h_copy(t + 1, b, k).start()

    for part in range(PARTS):
        pass_up(STEPS - 1, part)

    def keep_hidden():
        for t in range(STEPS):
            for half in range(2):
                for yy in range(Y):
                    first = (half * Y + ORDER[yy]) * LANES
                    hid_out[t, :, first : first + LANES] = hb[t + 1, half, yy, y]
        for t in range(STEPS):
            hz_arrival(t).wait_recv()
            hmat[t * ALL_ROWS : (t + 1) * ALL_ROWS, :] = whole(hb, t)
            hmat_pair[t * ALL_ROWS : (t + 1) * ALL_ROWS, :] = whole(hb_pair, t)

    carry[...] = jnp.zeros_like(carry)

    def gz_copy(t):
        return remote(
            grads_t.at[t, z_other], grads_pair.at[t], gz_ss.at[t], gz_rs.at[t], {"z": z_pair}
        )

    def gz_arrival(t):
        part = grads_pair.at[t]
        return remote(part, part, gz_ss.at[t], gz_rs.at[t], {"z": z_pair})

    def a_copy(t, b, k):
        return remote(
            a_send.at[t, b, up_y[k]], a_recv.at[t, b, y], a_ss.at[t, b, k], a_rs.at[t, b, k],
            {"y": up_y[k]},
        )

    def a_arrival(t, b, k):
        part = a_recv.at[t, b, down_y[k]]
        return remote(part, part, a_ss.at[t, b, k], a_rs.at[t, b, k], {"y": up_y[k]})

    def g_copy(t, b, k):
        return remote(
            g_send.at[t, b, up_y[k]], g_recv.at[t, b, y], g_ss.at[t, b, k], g_rs.at[t, b, k],
            {"y": up_y[k]},
        )

    def g_arrival(t, b, k):
        part = g_recv.at[t, b, down_y[k]]
        return remote(part, part, g_ss.at[t, b, k], g_rs.at[t, b, k], {"y": up_y[k]})

    def e_copy(t, b):
        return remote(
            e_send.at[t, b], eb.at[t, :, groups(b)], e_ss.at[t, b], e_rs.at[t, b],
            {"s": down_s[0]},
        )

    def e_arrival(t, b):
        part = eb.at[t, :, groups(b)]
        return remote(part, part, e_ss.at[t, b], e_rs.at[t, b], {"s": down_s[0]})

    def total(sent, received, t, b, half):
        value = sent[t, b, y, half].astype(F32)
        for k in range(Y - 1):
            value = value + received[t, b, down_y[k], half].astype(F32)
        return value

    def hand_down(t, b):
        for k in range(Y - 1):
            g_arrival(t, b, k).wait_recv()
        for half in range(2):
            e_send[t, b, half] = (
                total(g_send, g_recv, t, b, half).astype(BF16).reshape(GROUPS, ROWS, LANES)
            )
        e_copy(t, b).start()

    def spread(sent, t, b, gate_grads, weights):
        for j in range(4):
            columns = slice(j * 2 * LANES, (j + 1) * 2 * LANES)
            part = nn_dot(gate_grads, weights(columns)).astype(BF16)
            for n in range(2):
                block = 2 * j + n
                sent[t, b, ORDER[block % Y], block // Y] = part[:, n * LANES : (n + 1) * LANES]

    @pl.loop(0, STEPS * PARTS)
    def _(turn):
        back = turn // PARTS
        b = lax.rem(turn, PARTS)
        t = STEPS - 1 - back

        @pl.when(s < S - 1)
        def _():
            e_arrival(t, b).wait_recv()

        for half in range(2):
            acc[0, half] = eb[t, half, groups(b)].reshape(PART_ROWS, LANES).astype(F32)

        @pl.when(back > 0)
        def _():
            for k in range(Y - 1):
                a_arrival(t + 1, b, k).wait_recv()
            for half in range(2):
                acc[0, half] = acc[0, half] + total(a_send, a_recv, t + 1, b, half)

        for half in range(2):
            in_gate = gates[t, b, 0, half]
            forget = gates[t, b, 1, half]
            candidate = gates[t, b, 2, half]
            out_gate = gates[t, b, 3, half]
            alive = live[t, b]
            total_h = acc[0, half]
            squashed = jnp.tanh(cells[t + 1, b, half])
            total_c = carry[b, half] + total_h * out_gate * (1.0 - squashed * squashed)
            parts = (
                total_c * candidate * in_gate * (1.0 - in_gate) * alive,
                total_c * cells[t, b, half] * forget * (1.0 - forget) * alive,
                total_c * in_gate * (1.0 - candidate * candidate) * alive,
                total_h * squashed * out_gate * (1.0 - out_gate) * alive,
            )
            carry[b, half] = total_c * forget * alive
            for gate in range(GATES):
                grads[b, 2 * gate + half] = parts[gate].astype(BF16)

        gate_grads = jnp.concatenate([grads[b, block] for block in range(2 * GATES)], axis=1)

        @pl.when(t > 0)
        def _():
            spread(
                a_send, t, b, gate_grads,
                lambda columns: wrt[:, :, :, columns].reshape(LOCAL, 2 * LANES),
            )
            for k in range(Y - 1):
                a_copy(t, b, k).start()

        @pl.when(s > 0)
        def _():
            spread(
                g_send, t, b, gate_grads,
                lambda columns: wint[:, :, columns].reshape(LOCAL, 2 * LANES),
            )
            for k in range(Y - 1):
                g_copy(t, b, k).start()

        @pl.when(b == PARTS - 1)
        def _():
            for gate in range(GATES):
                for half in range(2):
                    block = jnp.concatenate(
                        [grads[part, 2 * gate + half] for part in range(PARTS)], axis=0
                    )
                    grads_t[t, half, gate] = block.T
            gz_copy(t).start()

            @pl.when(s > 0)
            def _():
                for part in range(PARTS):
                    hand_down(t, part)

            @pl.when(back == 0)
            def _():
                keep_hidden()

    up_quad, down_quad = far[1], far[2]
    onward = [up_quad, down_quad]

    def relay_copy(p):
        return remote(
            dw_send.at[far[0], p], dw_relay.at[p], dw_ss.at[0, p], dw_rs.at[0, p],
            {"z": 2 * onward[p] + z_half},
        )

    def direct_copy(p):
        return remote(
            dw_send.at[onward[1 - p], p], dw_recv.at[0, p], dw_ss.at[1, p], dw_rs.at[1, p],
            {"z": 2 * onward[1 - p] + z_half},
        )

    def joint_copy(p):
        return remote(
            dw_joint.at[p], dw_recv.at[1, p], dw_ss.at[2, p], dw_rs.at[2, p],
            {"z": 2 * onward[p] + z_half},
        )

    def dw_wait(part, kind, p):
        remote(
            part, part, dw_ss.at[kind, p], dw_rs.at[kind, p], {"z": 2 * onward[p] + z_half}
        ).wait_recv()

    def db_copy(k):
        return remote(
            db_send.at[far[k]], db_recv.at[quad], db_ss.at[k], db_rs.at[k],
            {"z": 2 * far[k] + z_half},
        )

    def db_arrival(k):
        part = db_recv.at[near[k]]
        return remote(part, part, db_ss.at[k], db_rs.at[k], {"z": 2 * far[k] + z_half})

    for t in range(1, STEPS):
        gz_arrival(t).wait_recv()

    @pl.loop(0, GATES)
    def _(gate):
        rows = jnp.concatenate([grads_t[t, z_half, gate] for t in range(STEPS)], axis=1)
        rows_pair = jnp.concatenate([grads_pair[t, gate] for t in range(1, STEPS)], axis=1)
        for j in range(4):
            columns = slice(j * 2 * LANES, (j + 1) * 2 * LANES)
            dw_acc[gate, :, columns] = nn_dot(rows, hmat[:, columns]) + nn_dot(
                rows_pair, hmat_pair[ALL_ROWS:, columns]
            )
        db_send[gate] = nt_dot(jnp.ones((8, STEPS * ALL_ROWS), BF16), rows) + nt_dot(
            jnp.ones((8, (STEPS - 1) * ALL_ROWS), BF16), rows_pair
        )

    gz_arrival(0).wait_recv()
    for k in range(QUADS):
        gate = far[k] if k < QUADS - 1 else quad
        rows_pair = grads_pair[0, gate]
        db_send[gate] = db_send[gate] + nt_dot(jnp.ones((8, ALL_ROWS), BF16), rows_pair)
        for j in range(4):
            columns = slice(j * 2 * LANES, (j + 1) * 2 * LANES)
            part = dw_acc[gate, :, columns] + nn_dot(rows_pair, hmat_pair[:ALL_ROWS, columns])
            if k < QUADS - 1:
                for p in range(2):
                    rows = slice(p * LANES // 2, (p + 1) * LANES // 2)
                    dw_send[gate, p, :, columns] = part[rows].astype(BF16)
            else:
                dw_acc[gate, :, columns] = part
        if k < QUADS - 1:
            db_copy(k).start()
            if k == 0:
                for p in range(2):
                    relay_copy(p).start()
            else:
                direct_copy(2 - k).start()

    def dw2_copy(p):
        return remote(
            dw2_send.at[p], dw2_recv.at[x], dw2_ss.at[p], dw2_rs.at[x],
            {"x": owner_x, "y": owner_y[p]},
        )

    def db2_copy(p):
        return remote(
            db2_send, db2_recv.at[x], db2_ss.at[p], db2_rs.at[x],
            {"x": owner_x, "y": owner_y[p]},
        )

    for p in range(2):
        dw_wait(dw_relay.at[p], 0, p)
        dw_joint[p] = (
            dw_send[onward[p], p].astype(F32) + dw_relay[p].astype(F32)
        ).astype(BF16)
        joint_copy(p).start()
    for k in range(QUADS - 1):
        db_arrival(k).wait_recv()
    db2_send[...] = db_send[quad] + db_recv[near[0]] + db_recv[near[1]] + db_recv[near[2]]
    for p in range(2):
        rows = slice(p * LANES // 2, (p + 1) * LANES // 2)
        for kind in range(2):
            dw_wait(dw_recv.at[kind, p], kind + 1, p)
        value = dw_acc[quad, rows, :]
        for kind in range(2):
            value = value + dw_recv[kind, p].astype(F32)
        dw2_send[p] = value.astype(BF16)

        @pl.when(is_me(z, owner_x, owner_y[p]))
        def _():
            dw2_recv[x] = dw2_send[p]
            db2_recv[x] = db2_send[...]

        @pl.when(jnp.logical_not(is_me(z, owner_x, owner_y[p])))
        def _():
            db2_copy(p).start()
            dw2_copy(p).start()

    for xx in range(X):
        @pl.when(jnp.logical_not(is_me(z, xx, user_y)))
        def _():
            where = {"x": xx, "y": user_y}
            dw_part = dw2_recv.at[xx]
            db_part = db2_recv.at[xx]
            remote(db_part, db_part, db2_ss.at[0], db2_rs.at[xx], where).wait_recv()
            remote(dw_part, dw_part, dw2_ss.at[0], dw2_rs.at[xx], where).wait_recv()

    dw_out[...] = dw2_recv[0].astype(F32) + dw2_recv[1].astype(F32)
    bias_sum = db2_recv[0, 0:1, :] + db2_recv[1, 0:1, :]
    db_out[...] = jnp.where(own_half == 0, bias_sum[:, : LANES // 2], bias_sum[:, LANES // 2 :])

    for xx in range(X):
        @pl.when(jnp.logical_not(is_me(z, xx, user_y)))
        def _():
            first_hop(xx).wait_send()

    for k in range(S - 1):
        st_copy(k).wait_send()
    for step in range(Z // 2):
        for p in range(2):
            for way in range(2):
                if ring_has(way, step, p):
                    ring(way, step, p).wait_send()
    for k in range(Y - 1):
        info_copy(k).wait_send()
        h0_copy(k).wait_send()
        c0_copy(k).wait_send()

    @pl.when(s == 0)
    def _():
        for k in range(Y - 1):
            obs_copy(k).wait_send()

    @pl.when(s == S - 1)
    def _():
        for k in range(Y - 1):
            cot_copy(k).wait_send()

    @pl.loop(0, STEPS)
    def _(t):
        hz_copy(t).wait_send()
        gz_copy(t).wait_send()
        for b in range(PARTS):
            for k in range(Y - 1):
                h_copy(t + 1, b, k).wait_send()

            @pl.when(s < S - 1)
            def _():
                x_copy(t, b).wait_send()

            @pl.when(t > 0)
            def _():
                for k in range(Y - 1):
                    a_copy(t, b, k).wait_send()

            @pl.when(s > 0)
            def _():
                for k in range(Y - 1):
                    g_copy(t, b, k).wait_send()
                e_copy(t, b).wait_send()

    for k in range(QUADS - 1):
        db_copy(k).wait_send()
    for p in range(2):
        relay_copy(p).wait_send()
        direct_copy(p).wait_send()
        joint_copy(p).wait_send()
    for p in range(2):
        @pl.when(jnp.logical_not(is_me(z, owner_x, owner_y[p])))
        def _():
            dw2_copy(p).wait_send()
            db2_copy(p).wait_send()


def on_device(
    obs_features, w_input, w_recurrent, bias, stored_states, state_owner, burn_steps, valid_steps, cotangent
):
    vmem = pl.BlockSpec(memory_space=pltpu.VMEM)
    hbm = pl.BlockSpec(memory_space=pl.ANY)
    dma = pltpu.SemaphoreType.DMA
    piece = (Y, ROWS, LANES)
    hidden, weights, biases = pl.pallas_call(
        kernel,
        out_shape=(
            pltpu.VMEM((STEPS, ROWS, D), BF16),
            pltpu.VMEM((LANES // 2, D), F32),
            pltpu.VMEM((1, LANES // 2), F32),
        ),
        in_specs=[hbm, hbm, hbm, hbm, vmem, hbm, vmem, vmem, vmem],
        out_specs=(vmem, vmem, vmem),
        scratch_shapes=[
            pltpu.VMEM((STEPS, ROWS, D), BF16),
            pltpu.VMEM((STEPS, ROWS, D), BF16),
            pltpu.VMEM((Y, ROWS, LANES), F32),
            pltpu.VMEM((S, ROWS, 2 * D), BF16),
            pltpu.VMEM((2, Z, D, LANES), BF16),
            pltpu.VMEM((Z, 2, LANES // 2, D), BF16),
            pltpu.VMEM((2 * GATES, LANES, D), BF16),
            pltpu.VMEM((2, STEPS + 1, 2, Y, *piece), BF16),
            pltpu.VMEM((STEPS, 2, Y, *piece), BF16),
            pltpu.VMEM((STEPS, 2, *piece), BF16),
            pltpu.VMEM((Y, STEPS, 2, ROWS, LANES), BF16),
            pltpu.VMEM((Y, 2, ROWS, LANES), BF16),
            pltpu.VMEM((Y, 2, ROWS, LANES), BF16),
            pltpu.VMEM((STEPS + 1, PARTS, 2, PART_ROWS, LANES), F32),
            pltpu.VMEM((STEPS, PARTS, GATES, 2, PART_ROWS, LANES), F32),
            pltpu.VMEM((GATES, 2, PART_ROWS, LANES), F32),
            pltpu.VMEM((STEPS, PARTS, PART_ROWS, LANES), F32),
            pltpu.VMEM((PARTS, 2 * GATES, PART_ROWS, LANES), BF16),
            pltpu.VMEM((STEPS, 2, GATES, LANES, ALL_ROWS), BF16),
            pltpu.VMEM((STEPS, GATES, LANES, ALL_ROWS), BF16),
            pltpu.VMEM((PARTS, 2, PART_ROWS, LANES), F32),
            pltpu.VMEM((STEPS, PARTS, Y, 2, PART_ROWS, LANES), BF16),
            pltpu.VMEM((STEPS, PARTS, Y, 2, PART_ROWS, LANES), BF16),
            pltpu.VMEM((STEPS, PARTS, Y, 2, PART_ROWS, LANES), BF16),
            pltpu.VMEM((STEPS, PARTS, Y, 2, PART_ROWS, LANES), BF16),
            pltpu.VMEM((STEPS, PARTS, 2, GROUPS, ROWS, LANES), BF16),
            pltpu.VMEM((STEPS * ALL_ROWS, D), BF16),
            pltpu.VMEM((STEPS * ALL_ROWS, D), BF16),
            pltpu.VMEM((GATES, LANES, D), F32),
            pltpu.VMEM((GATES, 2, LANES // 2, D), BF16),
            pltpu.VMEM((2, LANES // 2, D), BF16),
            pltpu.VMEM((2, LANES // 2, D), BF16),
            pltpu.VMEM((2, 2, LANES // 2, D), BF16),
            pltpu.VMEM((GATES, 8, LANES), F32),
            pltpu.VMEM((GATES, 8, LANES), F32),
            pltpu.VMEM((2, LANES // 2, D), BF16),
            pltpu.VMEM((X, LANES // 2, D), BF16),
            pltpu.VMEM((8, LANES), F32),
            pltpu.VMEM((X, 8, LANES), F32),
            dma((2,)),
            dma((Y - 1,)), dma((Y - 1,)),
            dma((S - 1,)), dma((S - 1,)), dma,
            dma((X,)), dma((2,)), dma,
            dma((2, Z // 2, 2)), dma((2, Z // 2, 2)),
            dma((2 * GATES,)),
            dma((Y - 1,)), dma((Y - 1,)),
            dma((Y - 1,)), dma((Y - 1,)),
            dma((Y - 1,)), dma((Y - 1,)),
            dma((STEPS + 1, PARTS, Y - 1)), dma((STEPS + 1, PARTS, Y - 1)),
            dma((STEPS, PARTS)), dma((STEPS, PARTS)),
            dma((STEPS,)), dma((STEPS,)),
            dma((STEPS,)), dma((STEPS,)),
            dma((STEPS, PARTS, Y - 1)), dma((STEPS, PARTS, Y - 1)),
            dma((STEPS, PARTS, Y - 1)), dma((STEPS, PARTS, Y - 1)),
            dma((STEPS, PARTS)), dma((STEPS, PARTS)),
            dma((3, 2)), dma((3, 2)),
            dma((3,)), dma((3,)),
            dma((2,)), dma((X,)),
            dma((2,)), dma((X,)),
            pltpu.SemaphoreType.REGULAR,
        ],
        compiler_params=pltpu.CompilerParams(
            collective_id=0, has_side_effects=True, vmem_limit_bytes=56 * 1024 * 1024
        ),
        name="replay_window",
    )(
        obs_features, cotangent, w_input[0], w_recurrent[0].T, bias, stored_states[0],
        state_owner[None], burn_steps[None], valid_steps[None],
    )
    return hidden[None], weights.T[None], biases


def solution(mesh):
    axes = ("s", "z", "x", "y")
    grid = Mesh(mesh.devices.reshape(S, Z, X, Y), axes)
    dp = ("z", "x", "y")
    return jax.shard_map(
        on_device,
        mesh=grid,
        in_specs=(
            P(None, dp, None),
            P("s", None, None),
            P("s", None, dp),
            P("s", None),
            P("s", None, dp, None),
            P(dp),
            P(dp),
            P(dp),
            P(None, dp, None),
        ),
        out_specs=(P("s", None, dp, None), P("s", None, dp), P("s", dp)),
        check_vma=False,
    )
```
